256 devices in a mesh: layer: 8 (over y, x_lo), tile: 32 (over z, x_hi, core).
Axes of the slice: x: 4 (x_hi: 2, x_lo: 2; x = x_hi * 2 + x_lo), y: 4, z: 8, core: 2. Of those that a mesh axis runs over, the one named last changes fastest.
Arguments:
- blocks: bfloat16 [8, 32, 320, 128, 128], P('layer', 'tile'), may hold values from 0.00049 to 0.0041
- slot_rows: int32 [8, 32, 320], P('layer', 'tile'), may hold values from 0 to 63, as said below
- slot_cols: int32 [8, 32, 320], P('layer', 'tile'), may hold values from 0 to 127
- rotation: int32 [8, 32, 320], P('layer', 'tile'), may hold values from 0 to 1
- live_block_count: int32 [8, 32], P('layer', 'tile'), may hold values from 64 to 320, as said below
- density: bfloat16 [8, 32, 8192], P('layer', 'tile'), may hold values from 0.29882812 to 3
- start: bfloat16 [8, 32, 64, 8192], P('layer', 'tile'), may hold values from -6 to 6
Outputs:
- vectors: bfloat16 [8, 32, 64, 8192], P('layer', 'tile')
The draws below stay inside these ranges and needn't reach their ends.
Inputs may be any that keep to these rules, and one draw needn't show every extreme that they name: `slot_rows`: slots 0 to 63 of every device are live and hold the diagonal blocks (row s, source s, no rotation). Only the first live_block_count slots of a device are live; some device has all 320 slots live and some device only 64.
All inputs are finite; a program needn't handle non-finite values.
Results may differ from the reference program's by a relative error of at most 0.005.
Values may be sent and summed in bfloat16 or wider, within the bound.
No kernel may reach another device: no remote copies, remote signals or barrier semaphores. Data moves between devices by JAX's collectives and lax.ppermute only.
A program may use at most 128 MiB of HBM per device.

```python
import math
import jax
import jax.numpy as jnp
from jax import lax

BLOCK = 128
VEC = 64
ITERS = 2
BLK_DEV = 64
EDGE = 16
SLOTS = 320
CELLS_DEV = 8192
LAYERS = 8
TILES = 32
TOTAL_CELLS = 2097152


def slot_tables(key):
    keys = jax.random.split(jax.random.fold_in(key, 7), 6)
    table_shape = (LAYERS, TILES, SLOTS)
    position = jnp.arange(SLOTS).astype(jnp.int32)
    diagonal = (position < BLK_DEV)[None, None, :]
    own_index = (position % BLK_DEV)[None, None, :]
    row_draw = jax.random.randint(keys[0], table_shape, 0, BLK_DEV).astype(jnp.int32)
    col_draw = jax.random.randint(keys[1], table_shape, 0, BLK_DEV + 4 * EDGE).astype(jnp.int32)
    turn_draw = jax.random.randint(keys[2], table_shape, 0, 2).astype(jnp.int32)
    slot_row = jnp.where(diagonal, own_index, row_draw).astype(jnp.int32)
    slot_col = jnp.where(diagonal, own_index, col_draw).astype(jnp.int32)
    turned = jnp.where(diagonal, 0, turn_draw).astype(jnp.int32)
    first_extra = jax.random.randint(keys[3], (LAYERS, TILES), 0, 4 * BLK_DEV + 1).astype(jnp.int32)
    second_extra = jax.random.randint(keys[4], (LAYERS, TILES), 0, 4 * BLK_DEV + 1).astype(jnp.int32)
    counts = (BLK_DEV + jnp.minimum(first_extra, second_extra)).reshape(-1)
    device_total = LAYERS * TILES
    chosen = jax.random.randint(keys[5], (), 0, device_total).astype(jnp.int32)
    counts = counts.at[chosen].set(SLOTS)
    counts = counts.at[(chosen + 1) % device_total].set(BLK_DEV)
    return (slot_row, slot_col, turned, counts.reshape(LAYERS, TILES).astype(jnp.int32))


def draw_slot_rows(key, part):
    return slot_tables(key)[0]


def draw_slot_cols(key, part):
    return slot_tables(key)[1]


def draw_rotation(key, part):
    return slot_tables(key)[2]


def draw_live_block_count(key, part):
    return slot_tables(key)[3]


def draw_blocks(key, part):
    keys = jax.random.split(jax.random.fold_in(key, 11), 2)
    band_width = max(BLOCK / 16.0, 2.0)
    floor_level = 0.2
    shift_range = BLOCK // 8
    offset = jax.random.randint(keys[0], (LAYERS, TILES, SLOTS, 1, 1), -shift_range, shift_range + 1).astype(jnp.float32)
    destination = jnp.arange(BLOCK).astype(jnp.float32)[:, None]
    source = jnp.arange(BLOCK).astype(jnp.float32)[None, :]
    jitter_factor = jax.random.uniform(keys[1], (LAYERS, TILES, SLOTS, BLOCK, BLOCK), jnp.float32, floor_level, 1.0)
    band_shape = jnp.exp(-jnp.square((destination - source - offset) / band_width))
    values = 0.0005 + 0.0035 * band_shape * jitter_factor
    return values.astype(jnp.bfloat16)


def levels(stream_key, shape, cuts, least, top_value):
    level, own = 1.0, jax.random.fold_in(stream_key, 6)
    for axis_at, shards_of in cuts:
        heights = jnp.exp(jax.random.uniform(jax.random.fold_in(own, axis_at), (shards_of,), jnp.float32, least / len(cuts), top_value / len(cuts)))
        level = level * jnp.repeat(heights, shape[axis_at] // shards_of).reshape([-1 if axis == axis_at else 1 for axis in range(len(shape))])
    return level


def bell_draw(stream_key, dims, deviation, limit, cuts=(), kind=jnp.bfloat16):
    drawn = deviation * jax.random.normal(stream_key, dims, jnp.float32)
    if cuts:
        drawn = drawn * levels(stream_key, dims, cuts, -0.22, 0.18)
    return jnp.clip(drawn, -limit, limit).astype(kind)


def setup_inputs(seed: int = 0) -> dict:
    key_of = jax.random.split(jax.random.key(seed), 8)
    return {
        "blocks": draw_blocks(jax.random.fold_in(key_of[7], 71), 0),
        "slot_rows": draw_slot_rows(jax.random.fold_in(key_of[7], 71), 0),
        "slot_cols": draw_slot_cols(jax.random.fold_in(key_of[7], 71), 0),
        "rotation": draw_rotation(jax.random.fold_in(key_of[7], 71), 0),
        "live_block_count": draw_live_block_count(jax.random.fold_in(key_of[7], 71), 0),
        "density": jnp.clip(jnp.exp(math.log(3.0) - 2.306499 * jax.random.uniform(key_of[5], (LAYERS, TILES, CELLS_DEV), jnp.float32) ** levels(key_of[5], (LAYERS, TILES, CELLS_DEV), ((0, 8), (1, 32)), -0.2, 0.2)), 0.29882812, 3.0).astype(jnp.bfloat16),
        "start": bell_draw(key_of[6], (LAYERS, TILES, VEC, CELLS_DEV), 1.0, 6.0, ((0, 8), (1, 32))),
    }


def extend(blocked):
    zero_rim = jnp.zeros_like(blocked[:1, :, :, :EDGE])
    left_rim = jnp.roll(blocked[:, :, :, BLK_DEV - EDGE:], 1, axis=1)
    right_rim = jnp.roll(blocked[:, :, :, :EDGE], -1, axis=1)
    upper_rim = jnp.concatenate([zero_rim, blocked[:-1, :, :, BLK_DEV - EDGE:]], axis=0)
    lower_rim = jnp.concatenate([blocked[1:, :, :, :EDGE], zero_rim], axis=0)
    return jnp.concatenate([blocked, left_rim, right_rim, upper_rim, lower_rim], axis=3)

def slot_live_flags(entry_count):
    return (jnp.arange(SLOTS).astype(jnp.int32) < entry_count).astype(jnp.float32)[:, None, None]

def forward_one(packed):
    transfer_matrix, slot_row, slot_col, turned, entry_count, extended = packed
    source_vectors = jnp.take(extended, slot_col, axis=1)
    source_vectors = jnp.where((turned == 1)[None, :, None], source_vectors[:, :, ::-1], source_vectors)
    slot_weights = jnp.einsum('rdv,trv->rtd', transfer_matrix.astype(jnp.float32), source_vectors.astype(jnp.float32), precision=lax.Precision.HIGHEST) * slot_live_flags(entry_count)
    summed = jax.ops.segment_sum(slot_weights, slot_row, num_segments=BLK_DEV)
    return jnp.transpose(summed, (1, 0, 2))

def adjoint_one(packed):
    transfer_matrix, slot_row, slot_col, turned, entry_count, image_rows = packed
    selected_entries = jnp.take(image_rows, slot_row, axis=1)
    slot_weights = jnp.einsum('laq,rla->lrq', transfer_matrix.astype(jnp.float32), selected_entries.astype(jnp.float32), precision=lax.Precision.HIGHEST) * slot_live_flags(entry_count)
    slot_weights = jnp.where((turned == 1)[:, None, None], slot_weights[:, :, ::-1], slot_weights)
    spread = jax.ops.segment_sum(slot_weights, slot_col, num_segments=BLK_DEV + 4 * EDGE)
    return jnp.transpose(spread, (1, 0, 2))

def fold_back(spread):
    total_part = spread[:, :, :, :BLK_DEV]
    left_part = spread[:, :, :, BLK_DEV:BLK_DEV + EDGE]
    right_part = spread[:, :, :, BLK_DEV + EDGE:BLK_DEV + 2 * EDGE]
    upper_part = spread[:, :, :, BLK_DEV + 2 * EDGE:BLK_DEV + 3 * EDGE]
    lower_part = spread[:, :, :, BLK_DEV + 3 * EDGE:]
    zero_rim = jnp.zeros_like(upper_part[:1])
    total_part = total_part.at[:, :, :, BLK_DEV - EDGE:].add(jnp.roll(left_part, -1, axis=1))
    total_part = total_part.at[:, :, :, :EDGE].add(jnp.roll(right_part, 1, axis=1))
    total_part = total_part.at[:, :, :, BLK_DEV - EDGE:].add(jnp.concatenate([upper_part[1:], zero_rim], axis=0))
    total_part = total_part.at[:, :, :, :EDGE].add(jnp.concatenate([zero_rim, lower_part[:-1]], axis=0))
    return total_part

def reference(blocks, slot_rows, slot_cols, rotation, live_block_count, density, start):
    device_count = LAYERS * TILES

    def flatten(array):
        return array.reshape((device_count,) + array.shape[2:])
    fixed = (flatten(blocks), flatten(slot_rows), flatten(slot_cols), flatten(rotation), flatten(live_block_count))

    def forward(blocked):
        extended = flatten(extend(blocked))
        result = lax.map(forward_one, fixed + (extended,))
        return result.reshape((LAYERS, TILES, blocked.shape[2], BLK_DEV, BLOCK))
    image_density = forward(density.reshape(LAYERS, TILES, 1, BLK_DEV, BLOCK))[:, :, 0]
    weight_full = density.astype(jnp.float32)[:, :, None, :]
    iterate = start.astype(jnp.float32)
    for turn_index in range(ITERS):
        scaled = (weight_full * iterate).astype(jnp.bfloat16).reshape(LAYERS, TILES, VEC, BLK_DEV, BLOCK)
        forward_rows = forward(scaled)
        image_rows = (forward_rows / image_density[:, :, None]).astype(jnp.bfloat16)
        spread = lax.map(adjoint_one, fixed + (flatten(image_rows),))
        spread = spread.reshape(LAYERS, TILES, VEC, BLK_DEV + 4 * EDGE, BLOCK)
        pulled = fold_back(spread).reshape(LAYERS, TILES, VEC, CELLS_DEV)
        global_sums = lax.optimization_barrier(jnp.sum(weight_full * pulled * pulled, axis=(0, 1, 3)))
        iterate = pulled * lax.rsqrt(global_sums / TOTAL_CELLS + 1e-06)[None, None, :, None]
    return iterate.astype(jnp.bfloat16)
```

```python
import functools

import jax
import jax.numpy as jnp
from jax import lax
from jax.experimental import pallas as pl
from jax.experimental.pallas import tpu as pltpu
from jax.sharding import PartitionSpec as P

UNROLL = 4
CHUNKS = 10
VM = pltpu.VMEM
VMEM_SPEC = pl.BlockSpec(memory_space=pltpu.VMEM)
SMEM_SPEC = pl.BlockSpec(memory_space=pltpu.SMEM)
ANY_SPEC = pl.BlockSpec(memory_space=pl.ANY)


def pair_tables(slot_row, slot_col, live, num_blocks, places):
    slots = slot_row.shape[0]
    index = jnp.arange(slots, dtype=jnp.int32)
    half = (slot_col >= num_blocks).astype(jnp.int32)
    source = slot_col - half * num_blocks
    tables, counts = [], []
    keys = jnp.arange(num_blocks, dtype=jnp.int32)
    place = jnp.arange(places, dtype=jnp.int32)
    for dest, operand in ((slot_row, source), (source, slot_row)):
        packed = index + operand * 512 + dest * 65536
        for side in (0, 1):
            used = live & (half == side)
            hit = (dest[:, None] == dest[None, :]) & used[:, None] & (index[:, None] < index[None, :])
            rank = jnp.sum(hit.astype(jnp.int32), axis=0)
            member = (dest[:, None] == keys[None, :]) & used[:, None]
            pairs = (jnp.sum(member.astype(jnp.int32), axis=0) + 1) // 2
            before = jnp.sum(jnp.where(keys[:, None] < keys[None, :], pairs[:, None], 0), axis=0)
            position = 2 * jnp.sum(jnp.where(dest[:, None] == keys[None, :], before[None, :], 0), axis=1)
            position = jnp.where(used, position + rank, -1)
            found = position[:, None] == place[None, :]
            empty = num_blocks * 512
            tables.append(jnp.sum(jnp.where(found, packed[:, None] - empty, 0), axis=0) + empty)
            counts.append((jnp.sum(pairs) + UNROLL - 1) // UNROLL)
    return tables, jnp.stack(counts)


def pair_loop(tab, trips, source, matrix, acc, transposed):
    def body(step, carry):
        done = []
        for u in range(UNROLL):
            place = (step * UNROLL + u) * 2
            one, two = tab[place], tab[place + 1]
            lhs = jnp.concatenate([source[(one >> 9) & 127], source[(two >> 9) & 127]], axis=1)
            first, second = matrix[one & 511], matrix[two & 511]
            if transposed:
                rhs = jnp.concatenate([first, second], axis=0)
                dims = (((1,), (0,)), ((), ()))
            else:
                rhs = jnp.concatenate([first, second], axis=1)
                dims = (((1,), (1,)), ((), ()))
            done.append((one >> 16, lax.dot_general(lhs, rhs, dims, preferred_element_type=jnp.float32)))
        for dest, value in done:
            acc[dest] += value
        return carry

    lax.fori_loop(0, trips, body, 0)


def clear(ref):
    def body(b, carry):
        ref[b] = jnp.zeros(ref.shape[1:], ref.dtype)
        return carry

    lax.fori_loop(0, ref.shape[0], body, 0)


def first_kernel(rot, meta, tab, blocks, start, density, matrix, rows, source, sems):
    slots = blocks.shape[0]
    step_slots = slots // CHUNKS
    for c in range(CHUNKS):
        part = pl.ds(c * step_slots, step_slots)
        pltpu.make_async_copy(blocks.at[part], matrix.at[part], sems.at[c]).start()
    num_blocks, vectors = rows.shape[0], start.shape[0]
    size = blocks.shape[-1]
    clear(rows)

    def fill(b, carry):
        cells = pl.ds(pl.multiple_of(b * size, size), size)
        weight = density[:, cells]
        scaled = (start[:, cells].astype(jnp.float32) * weight.astype(jnp.float32)).astype(jnp.bfloat16)
        pad = jnp.where(
            lax.broadcasted_iota(jnp.int32, (16, size), 0) == 0,
            jnp.broadcast_to(weight, (16, size)).astype(jnp.float32),
            0.0,
        ).astype(jnp.bfloat16)
        source[b, :vectors] = scaled
        source[b, vectors:] = pad
        return carry

    lax.fori_loop(0, num_blocks, fill, 0)
    source[num_blocks] = jnp.zeros(source.shape[1:], source.dtype)
    lanes = lax.broadcasted_iota(jnp.int32, (size, size), 0)
    other = lax.broadcasted_iota(jnp.int32, (size, size), 1)
    live = meta[4]
    for c in range(CHUNKS):
        part = pl.ds(c * step_slots, step_slots)
        pltpu.make_async_copy(blocks.at[part], matrix.at[part], sems.at[c]).wait()

    def turn(step, carry):
        done = []
        for u in range(UNROLL):
            slot = step * UNROLL + u
            flip = rot[slot]
            target = jnp.where(flip == 1, size - 1 - other, other)
            select = (lanes == target).astype(jnp.float32).astype(jnp.bfloat16)
            done.append(
                (slot, jnp.dot(matrix[slot], select, preferred_element_type=jnp.float32).astype(jnp.bfloat16))
            )
        for slot, value in done:
            matrix[slot] = value
        return carry

    lax.fori_loop(0, (live + UNROLL - 1) // UNROLL, turn, 0)
    pair_loop(tab, meta[0], source, matrix, rows, False)


def own_kernel(meta, tab, matrix, head, middle, tail, rows, source):
    clear(rows)
    edge = head.shape[0]
    num_blocks = rows.shape[0]
    source[:edge] = head[...]
    source[edge : num_blocks - edge] = middle[...]
    source[num_blocks - edge : num_blocks] = tail[...]
    source[num_blocks] = jnp.zeros(source.shape[1:], source.dtype)
    pair_loop(tab, meta[0], source, matrix, rows, False)


def rim_kernel(first, meta, tab, tab_back, matrix, rows, rims, *rest):
    if first:
        image, image_density, back, source, total = rest
    else:
        inverse_in, image, back, source, total = rest
    num_blocks, size = rows.shape[0], rows.shape[2]
    vectors = image.shape[1]
    edge = num_blocks // 4
    for side in range(4):
        def fill(b, carry, side=side):
            source[side * edge + b, :vectors] = rims[side][pl.ds(pl.multiple_of(b * vectors, vectors), vectors)]
            return carry

        lax.fori_loop(0, edge, fill, 0)
        if first:
            weights = rims[side][edge * vectors :].astype(jnp.float32)
            top = lax.broadcasted_iota(jnp.int32, (16, size), 0) == 0
            for b in range(edge):
                pad = jnp.where(top, jnp.broadcast_to(weights[b : b + 1], (16, size)), 0.0)
                source[side * edge + b, vectors:] = pad.astype(jnp.bfloat16)
    source[num_blocks] = jnp.zeros(source.shape[1:], source.dtype)
    clear(total)
    pair_loop(tab, meta[1], source, matrix, rows, False)

    def divide(b, carry):
        if first:
            inverse = 1.0 / rows[b, vectors : vectors + 8]
            image_density[b] = inverse
        else:
            inverse = inverse_in[b]
        image[b] = (rows[b, :vectors] * inverse[:1]).astype(jnp.bfloat16)
        return carry

    lax.fori_loop(0, num_blocks, divide, 0)
    image[num_blocks] = jnp.zeros(image.shape[1:], image.dtype)
    pair_loop(tab_back, meta[3], image, matrix, total, True)

    def send(b, carry):
        back[b] = total[b].astype(jnp.bfloat16)
        return carry

    lax.fori_loop(0, num_blocks, send, 0)


def adjoint_kernel(last, meta, tab, matrix, image, density, *rest):
    if last:
        total, norm = rest
    else:
        total, norm, middle = rest
    clear(total)
    num_blocks = total.shape[0]
    edge = num_blocks // 4
    pair_loop(tab, meta[2], image, matrix, total, True)
    norm[...] = jnp.zeros_like(norm)

    def finish(b, carry):
        value = total[b]
        weighted = value * density[b]
        norm[...] += weighted * value
        if not last:
            middle[b - edge] = weighted.astype(jnp.bfloat16)
        return carry

    lax.fori_loop(edge, num_blocks - edge, finish, 0)


def final_kernel(scale, total, head, tail, out):
    edge = head.shape[0]
    num_blocks, vectors, size = total.shape
    factor = jnp.broadcast_to(scale[...], (vectors, size))

    def write(ref, shift):
        def body(b, carry):
            cells = pl.ds(pl.multiple_of((b + shift) * size, size), size)
            out[:, cells] = (ref[b] * factor).astype(jnp.bfloat16)
            return carry

        return body

    lax.fori_loop(0, edge, write(head, 0), 0)
    lax.fori_loop(edge, num_blocks - edge, write(total, 0), 0)
    lax.fori_loop(0, edge, write(tail, num_blocks - edge), 0)


def shift(x, axis, step, periodic):
    count = lax.axis_size(axis)
    route = [(i, (i + step) % count) for i in range(count) if periodic or 0 <= i + step < count]
    return lax.ppermute(x, axis, route)


def outward(head, tail):
    return (
        shift(tail, "tile", 1, True),
        shift(head, "tile", -1, True),
        shift(tail, "layer", 1, False),
        shift(head, "layer", -1, False),
    )


def group_sum(x):
    tiles, layers = lax.axis_size("tile"), lax.axis_size("layer")
    for axis, count in (("tile", tiles), ("layer", layers)):
        stride = 1
        while stride < count:
            width = 4 if count // stride >= 4 else count // stride
            parts = [
                lax.ppermute(x, axis, [(i, i ^ (stride * k)) for i in range(count)]) for k in range(1, width)
            ]
            x = x + sum(parts)
            stride *= width
    return x


def call(kernel, name, outs, in_specs, scratch, flops, nbytes):
    return pl.pallas_call(
        kernel,
        name=name,
        out_shape=outs,
        in_specs=in_specs,
        out_specs=[VMEM_SPEC] * len(outs),
        scratch_shapes=scratch,
        compiler_params=pltpu.CompilerParams(vmem_limit_bytes=30 * 1024 * 1024),
        cost_estimate=pl.CostEstimate(flops=flops, bytes_accessed=nbytes, transcendentals=0),
    )


def local(blocks, slot_rows, slot_cols, rotation, live_block_count, density, start):
    bf16, f32 = jnp.bfloat16, jnp.float32
    blocks, start = blocks[0, 0], start[0, 0]
    slots, size = blocks.shape[0], blocks.shape[2]
    vectors, cells = start.shape
    num_blocks = cells // size
    edge = num_blocks // 4
    rot = rotation[0, 0]
    weights = density[0, 0]
    weight_blocks = weights.reshape(num_blocks, size)
    wide = weight_blocks.astype(f32)[:, None, :]
    total_cells = cells * lax.axis_size("layer") * lax.axis_size("tile")

    def first_rim(lo):
        piece = lax.slice_in_dim(start, lo * size, (lo + edge) * size, axis=1)
        piece = piece.reshape(vectors, edge, size).transpose(1, 0, 2).astype(f32)
        scaled = (piece * wide[lo : lo + edge]).astype(bf16).reshape(edge * vectors, size)
        return jnp.concatenate([scaled, weight_blocks[lo : lo + edge]], axis=0)

    rims = outward(first_rim(0), first_rim(num_blocks - edge))

    live = jnp.arange(slots, dtype=jnp.int32) < live_block_count[0, 0]
    places = 2 * ((slots + num_blocks) // 2)
    tables, counts = pair_tables(slot_rows[0, 0], slot_cols[0, 0], live, num_blocks, places)
    meta = jnp.concatenate([counts, live_block_count[0], jnp.zeros((3,), jnp.int32)])

    tall = vectors + 16
    matrix, rows = call(
        first_kernel,
        "own_first",
        [VM((slots, size, size), bf16), VM((num_blocks, tall, size), f32)],
        [SMEM_SPEC, SMEM_SPEC, SMEM_SPEC, ANY_SPEC, VMEM_SPEC, VMEM_SPEC],
        [VM((num_blocks + 1, tall, size), bf16), pltpu.SemaphoreType.DMA((CHUNKS,))],
        2 * slots * size * size * 2 * size,
        2 * blocks.size * 2,
    )(rot, meta, tables[0], blocks, start, weights[None])

    block_f32 = VM((num_blocks, vectors, size), f32)
    image_type = VM((num_blocks + 1, vectors, size), bf16)
    back_type = VM((num_blocks, vectors, size), bf16)
    inverse = None
    norms = []
    for turn in range(2):
        first, last = turn == 0, turn == 1
        if not first:
            (rows,) = call(
                own_kernel,
                "own_next",
                [block_f32],
                [SMEM_SPEC, SMEM_SPEC] + [VMEM_SPEC] * 4,
                [VM((num_blocks + 1, vectors, size), bf16)],
                slots * size * size * vectors,
                blocks.size,
            )(meta, tables[0], matrix, head, middle, tail)
            rims = outward(head.reshape(edge * vectors, size), tail.reshape(edge * vectors, size))
        height = tall if first else vectors
        extra = [] if first else [inverse]
        outs = [image_type] + ([VM((num_blocks, 8, size), f32)] if first else []) + [back_type]

        def rim_body(meta_ref, tab, tab_back, matrix_ref, rows_in, r0, r1, r2, r3, *rest, first=first):
            if first:
                image, dens, back, source, total, acc = rest
                more = (image, dens, back, source, total)
            else:
                inv, image, back, source, total, acc = rest
                more = (inv, image, back, source, total)

            def copy(b, carry):
                acc[b] = rows_in[b]
                return carry

            lax.fori_loop(0, acc.shape[0], copy, 0)
            rim_kernel(first, meta_ref, tab, tab_back, matrix_ref, acc, (r0, r1, r2, r3), *more)

        result = call(
            rim_body,
            "rim_first" if first else "rim_next",
            outs,
            [SMEM_SPEC] * 3 + [VMEM_SPEC] * (6 + len(extra)),
            [VM((num_blocks + 1, height, size), bf16), block_f32, VM((num_blocks, height, size), f32)],
            2 * slots * size * size * vectors,
            blocks.size,
        )(meta, tables[1], tables[3], matrix, rows, *rims, *extra)
        if first:
            image, inverse, back = result
        else:
            image, back = result
        sides = [back[i * edge : (i + 1) * edge] for i in range(4)]
        from_right = shift(sides[0], "tile", -1, True)
        from_left = shift(sides[1], "tile", 1, True)
        from_below = shift(sides[2], "layer", -1, False)
        from_above = shift(sides[3], "layer", 1, False)
        norm_type = VM((vectors, size), f32)
        result = call(
            functools.partial(adjoint_kernel, last),
            "adjoint_last" if last else "adjoint_first",
            [block_f32, norm_type] + ([] if last else [VM((num_blocks - 2 * edge, vectors, size), bf16)]),
            [SMEM_SPEC] * 2 + [VMEM_SPEC] * 3,
            [],
            slots * size * size * vectors,
            blocks.size,
        )(meta, tables[2], matrix, image, wide)
        total, norm = result[0], result[1]
        pulled_head = total[:edge] + (from_left.astype(f32) + from_above.astype(f32))
        pulled_tail = total[num_blocks - edge :] + (from_right.astype(f32) + from_below.astype(f32))
        weighted_head = pulled_head * wide[:edge]
        weighted_tail = pulled_tail * wide[num_blocks - edge :]
        norms.append(
            jnp.sum(norm, axis=1)
            + jnp.sum(weighted_head * pulled_head, axis=(0, 2))
            + jnp.sum(weighted_tail * pulled_tail, axis=(0, 2))
        )
        if not last:
            middle = result[2]
            head, tail = weighted_head.astype(bf16), weighted_tail.astype(bf16)
    sums = group_sum(jnp.concatenate(norms))
    factor = lax.rsqrt(sums[:vectors] / total_cells + 1e-06)
    scale = factor * lax.rsqrt(factor * factor * sums[vectors:] / total_cells + 1e-06)
    out = call(
        final_kernel,
        "write_out",
        [jax.ShapeDtypeStruct((vectors, cells), bf16)],
        [VMEM_SPEC] * 4,
        [],
        0,
        cells * vectors * 6,
    )(scale[:, None], total, pulled_head, pulled_tail)[0]
    return out[None, None]


def solution(mesh):
    in_specs = (
        P("layer", "tile", None, None, None),
        P("layer", "tile", None),
        P("layer", "tile", None),
        P("layer", "tile", None),
        P("layer", "tile"),
        P("layer", "tile", None),
        P("layer", "tile", None, None),
    )
    out_specs = P("layer", "tile", None, None)
    return jax.shard_map(local, mesh=mesh, in_specs=in_specs, out_specs=out_specs, check_vma=False)
```

```python
import functools

import jax
import jax.numpy as jnp
from jax import lax
from jax.experimental import pallas as pl
from jax.experimental.pallas import tpu as pltpu
from jax.sharding import PartitionSpec as P

UNROLL = 16
TURN = 8
CHUNKS = 8
VM = pltpu.VMEM
VMEM_SPEC = pl.BlockSpec(memory_space=pltpu.VMEM)
SMEM_SPEC = pl.BlockSpec(memory_space=pltpu.SMEM)
HBM_SPEC = pl.BlockSpec(memory_space=pltpu.HBM)
FORWARD_OWN, FORWARD_RIM, ADJOINT_OWN, ADJOINT_RIM = range(4)


def pair_tables(slot_row, slot_col, turned, live_count, num_blocks, places):
    slots = slot_row.shape[0]
    index = jnp.arange(slots, dtype=jnp.int32)
    live = index < live_count
    half = (slot_col >= num_blocks).astype(jnp.int32)
    source = slot_col - half * num_blocks
    keys = jnp.arange(num_blocks, dtype=jnp.int32)
    place = jnp.arange(places, dtype=jnp.int32)
    dest = jnp.stack([slot_row, slot_row, source, source])
    operand = jnp.stack([source, source, slot_row, slot_row])
    side = jnp.arange(4, dtype=jnp.int32)[:, None] & 1
    used = live[None] & (half[None] == side)
    earlier = index[:, None] < index[None, :]
    hit = (dest[:, :, None] == dest[:, None, :]) & used[:, :, None] & earlier[None]
    rank = jnp.sum(hit.astype(jnp.int32), axis=1)
    member = (dest[:, :, None] == keys) & used[:, :, None]
    pairs = (jnp.sum(member.astype(jnp.int32), axis=1) + 1) >> 1
    before = jnp.sum(jnp.where(keys[:, None] < keys[None, :], pairs[:, :, None], 0), axis=1)
    position = 2 * jnp.sum(jnp.where(dest[:, :, None] == keys, before[:, None, :], 0), axis=2) + rank
    position = jnp.where(used, position, -1)
    empty = num_blocks * 512
    packed = index[None] + operand * 512 + dest * 65536 - empty
    tables = jnp.sum(jnp.where(position[:, :, None] == place, packed[:, :, None], 0), axis=1) + empty
    trips = (jnp.sum(pairs, axis=1) + UNROLL - 1) // UNROLL
    flip = live & (turned == 1)
    flip_rank = jnp.sum((flip[:, None] & earlier).astype(jnp.int32), axis=0)
    flip_rank = jnp.where(flip, flip_rank, -1)
    flips = jnp.sum(jnp.where(flip_rank[:, None] == index[None, :], index[:, None] - slots, 0), axis=0) + slots
    flip_trips = (jnp.sum(flip.astype(jnp.int32)) + TURN - 1) // TURN
    meta = jnp.concatenate([trips, jnp.full((4,), flip_trips, jnp.int32)])
    return tables.reshape(-1), flips, meta


def pair_loop(which, meta, tab, source, matrix, acc):
    start = which * (tab.shape[0] // 4)
    transposed = which >= ADJOINT_OWN

    def body(step, carry):
        done = []
        for u in range(UNROLL):
            place = start + (step * UNROLL + u) * 2
            one, two = tab[place], tab[place + 1]
            lhs = jnp.concatenate([source[(one >> 9) & 127], source[(two >> 9) & 127]], axis=1)
            first, second = matrix[one & 511], matrix[two & 511]
            rhs = jnp.concatenate([first, second], axis=0 if transposed else 1)
            dims = (((1,), (0 if transposed else 1,)), ((), ()))
            done.append((one >> 16, lax.dot_general(lhs, rhs, dims, preferred_element_type=jnp.float32)))
        for dest, value in done:
            acc[dest] += value
        return carry

    lax.fori_loop(0, meta[which], body, 0)


def clear(ref):
    def body(b, carry):
        ref[b] = jnp.zeros(ref.shape[1:], ref.dtype)
        return carry

    lax.fori_loop(0, ref.shape[0], body, 0)


def edge_kernel(start, density, head, tail, held, sems):
    size = head.shape[1]
    vectors = start.shape[0]
    edge = head.shape[0] // (vectors + 1)
    width = edge * size
    outs = (head, tail)
    origin = (0, start.shape[1] - width)
    copies = [
        pltpu.make_async_copy(start.at[:, pl.ds(origin[i], width)], held.at[i], sems.at[i]) for i in range(2)
    ]
    for copy in copies:
        copy.start()
    for i in range(2):
        copies[i].wait()
        weights = []
        for b in range(edge):
            cells = pl.ds(origin[i] + b * size, size)
            weight = density[:, cells].astype(jnp.float32)
            weights.append(weight)
            value = held[i, :, b * size : (b + 1) * size].astype(jnp.float32) * weight
            outs[i][b * vectors : (b + 1) * vectors] = value.astype(jnp.bfloat16)
        outs[i][edge * vectors :] = jnp.concatenate(weights, axis=0).astype(jnp.bfloat16)


def first_kernel(meta, tab, flips, blocks, start, density, matrix, rows, source, held, sems):
    slots = blocks.shape[0]
    part = slots // CHUNKS
    copies = [pltpu.make_async_copy(start, held, sems.at[CHUNKS])]
    for c in range(CHUNKS):
        here = pl.ds(c * part, part)
        copies.append(pltpu.make_async_copy(blocks.at[here], matrix.at[here], sems.at[c]))
    for copy in copies:
        copy.start()
    num_blocks, vectors = rows.shape[0], start.shape[0]
    size = blocks.shape[-1]
    clear(rows)
    matrix[slots] = jnp.zeros((size, size), matrix.dtype)
    source[num_blocks] = jnp.zeros(source.shape[1:], source.dtype)
    copies[0].wait()
    top = lax.broadcasted_iota(jnp.int32, (16, size), 0) == 0

    def fill(b, carry):
        cells = pl.ds(pl.multiple_of(b * size, size), size)
        weight = density[:, cells].astype(jnp.float32)
        source[b, :vectors] = (held[:, cells].astype(jnp.float32) * weight).astype(jnp.bfloat16)
        source[b, vectors:] = jnp.where(top, jnp.broadcast_to(weight, (16, size)), 0.0).astype(jnp.bfloat16)
        return carry

    lax.fori_loop(0, num_blocks, fill, 0, unroll=4)
    across = lax.broadcasted_iota(jnp.int32, (size, size), 0)
    along = lax.broadcasted_iota(jnp.int32, (size, size), 1)
    mirror = (across + along == size - 1).astype(jnp.float32).astype(jnp.bfloat16)
    for copy in copies[1:]:
        copy.wait()

    def turn(step, carry):
        done = []
        for u in range(TURN):
            slot = flips[step * TURN + u]
            value = jnp.dot(matrix[slot], mirror, preferred_element_type=jnp.float32)
            done.append((slot, value.astype(jnp.bfloat16)))
        for slot, value in done:
            matrix[slot] = value
        return carry

    lax.fori_loop(0, meta[4], turn, 0)
    pair_loop(FORWARD_OWN, meta, tab, source, matrix, rows)


def own_kernel(meta, tab, matrix, head, middle, tail, rows, source):
    clear(rows)
    num_blocks = rows.shape[0]
    edge = num_blocks // 4
    vectors = rows.shape[1]
    for b in range(edge):
        source[b] = head[b * vectors : (b + 1) * vectors]
        source[num_blocks - edge + b] = tail[b * vectors : (b + 1) * vectors]
    source[edge : num_blocks - edge] = middle[...]
    source[num_blocks] = jnp.zeros(source.shape[1:], source.dtype)
    pair_loop(FORWARD_OWN, meta, tab, source, matrix, rows)


def rim_kernel(first, meta, tab, matrix, rows_in, left, right, upper, lower, *rest):
    del rows_in
    if first:
        rows, image, inverse = rest[:3]
        rest = rest[3:]
    else:
        inverse, rows, image = rest[:3]
        rest = rest[3:]
    backs, (source, total) = rest[:4], rest[4:]
    num_blocks, size = rows.shape[0], rows.shape[2]
    vectors = image.shape[1]
    edge = num_blocks // 4
    for side, rim in enumerate((left, right, upper, lower)):
        for b in range(edge):
            source[side * edge + b, :vectors] = rim[b * vectors : (b + 1) * vectors]
        if first:
            weights = rim[edge * vectors :].astype(jnp.float32)
            top = lax.broadcasted_iota(jnp.int32, (16, size), 0) == 0
            for b in range(edge):
                pad = jnp.where(top, jnp.broadcast_to(weights[b : b + 1], (16, size)), 0.0)
                source[side * edge + b, vectors:] = pad.astype(jnp.bfloat16)
    source[num_blocks] = jnp.zeros(source.shape[1:], source.dtype)
    clear(total)
    pair_loop(FORWARD_RIM, meta, tab, source, matrix, rows)

    def divide(b, carry):
        if first:
            factor = 1.0 / rows[b, vectors : vectors + 8]
            inverse[b] = factor
        else:
            factor = inverse[b]
        image[b] = (rows[b, :vectors] * factor[:1]).astype(jnp.bfloat16)
        return carry

    lax.fori_loop(0, num_blocks, divide, 0, unroll=4)
    image[num_blocks] = jnp.zeros(image.shape[1:], image.dtype)
    pair_loop(ADJOINT_RIM, meta, tab, image, matrix, total)
    for side in range(4):
        for b in range(edge):
            backs[side][b * vectors : (b + 1) * vectors] = total[side * edge + b].astype(jnp.bfloat16)


def adjoint_kernel(meta, tab, matrix, image, total):
    clear(total)
    pair_loop(ADJOINT_OWN, meta, tab, image, matrix, total)


def collect(total, density, lows, highs, store):
    num_blocks, vectors, size = total.shape
    edge = num_blocks // 4

    def add(b, norm, parts):
        value = total[b]
        if parts:
            here = b if parts is lows else b - (num_blocks - edge)
            rows = pl.ds(pl.multiple_of(here * vectors, vectors), vectors)
            value = value + (parts[0][rows].astype(jnp.float32) + parts[1][rows].astype(jnp.float32))
        cells = pl.ds(pl.multiple_of(b * size, size), size)
        weighted = value * density[:, cells].astype(jnp.float32)
        store(b, value, weighted)
        return norm + weighted * value

    norm = jnp.zeros((vectors, size), jnp.float32)
    norm = lax.fori_loop(0, edge, lambda b, n: add(b, n, lows), norm)
    norm = lax.fori_loop(edge, num_blocks - edge, lambda b, n: add(b, n, None), norm)
    norm = lax.fori_loop(num_blocks - edge, num_blocks, lambda b, n: add(b, n, highs), norm)
    ones = jnp.ones((8, size), jnp.float32)
    return lax.dot_general(
        ones, norm, (((1,), (1,)), ((), ())), precision=lax.Precision.HIGHEST, preferred_element_type=jnp.float32
    )


def join_kernel(total, density, low0, low1, high0, high1, head, middle, tail, norm):
    num_blocks, vectors, size = total.shape
    edge = num_blocks // 4
    high_from = num_blocks - edge

    def store(b, value, weighted):
        del value
        scaled = weighted.astype(jnp.bfloat16)

        def rows(first):
            return pl.ds(pl.multiple_of((b - first) * vectors, vectors), vectors)

        @pl.when(b < edge)
        def _():
            head[rows(0)] = scaled

        @pl.when((b >= edge) & (b < high_from))
        def _():
            middle[b - edge] = scaled

        @pl.when(b >= high_from)
        def _():
            tail[rows(high_from)] = scaled

    norm[...] = collect(total, density, (low0, low1), (high0, high1), store)


def sum_kernel(total_in, density, low0, low1, high0, high1, norm, total, message):
    del total_in

    def store(b, value, weighted):
        del weighted
        total[b] = value

    last = collect(total, density, (low0, low1), (high0, high1), store)
    both = jnp.concatenate([norm[...], last], axis=1)[:1]
    message[...] = jnp.broadcast_to(both, message.shape)


def final_kernel(total_cells, sums, total, out):
    num_blocks, vectors, size = total.shape
    both = jnp.sum(sums[...], axis=0, keepdims=True) * (1.0 / total_cells)
    diagonal = lax.broadcasted_iota(jnp.int32, (vectors, size), 0)
    lane = lax.broadcasted_iota(jnp.int32, (vectors, size), 1)
    both = jnp.broadcast_to(both, (vectors, size))
    first = jnp.sum(jnp.where(lane == diagonal, both, 0.0), axis=1, keepdims=True)
    second = jnp.sum(jnp.where(lane == diagonal + vectors, both, 0.0), axis=1, keepdims=True)
    factor = lax.rsqrt(first + 1e-06)
    scale = jnp.broadcast_to(factor * lax.rsqrt(factor * factor * second + 1e-06), (vectors, size))

    def body(b, carry):
        cells = pl.ds(pl.multiple_of(b * size, size), size)
        out[:, cells] = (total[b] * scale).astype(jnp.bfloat16)
        return carry

    lax.fori_loop(0, num_blocks, body, 0, unroll=4)


def shift(x, axis, step, periodic):
    count = lax.axis_size(axis)
    route = [(i, (i + step) % count) for i in range(count) if periodic or 0 <= i + step < count]
    return lax.ppermute(x, axis, route)


def outward(head, tail):
    return (
        shift(tail, "tile", 1, True),
        shift(head, "tile", -1, True),
        shift(tail, "layer", 1, False),
        shift(head, "layer", -1, False),
    )


def call(kernel, name, outs, in_specs, scratch, flops, nbytes, aliases={}):
    return pl.pallas_call(
        kernel,
        name=name,
        out_shape=outs,
        in_specs=in_specs,
        out_specs=[VMEM_SPEC] * len(outs),
        scratch_shapes=scratch,
        input_output_aliases=aliases,
        compiler_params=pltpu.CompilerParams(vmem_limit_bytes=16 * 1024 * 1024),
        cost_estimate=pl.CostEstimate(flops=flops, bytes_accessed=nbytes, transcendentals=0),
    )


def local(blocks, slot_rows, slot_cols, rotation, live_block_count, density, start):
    bf16, f32 = jnp.bfloat16, jnp.float32
    blocks, start = blocks[0, 0], start[0, 0]
    slots, size = blocks.shape[0], blocks.shape[2]
    vectors, cells = start.shape
    num_blocks = cells // size
    edge = num_blocks // 4
    weights = density[0]
    devices = lax.axis_size("layer") * lax.axis_size("tile")
    total_cells = cells * devices
    work = slots * size * size * vectors
    tall = vectors + 16
    rim_type = VM((edge * vectors, size), bf16)
    first_rim_type = VM((edge * (vectors + 1), size), bf16)
    block_f32 = VM((num_blocks, vectors, size), f32)
    tall_f32 = VM((num_blocks, tall, size), f32)
    image_type = VM((num_blocks + 1, vectors, size), bf16)
    middle_type = VM((num_blocks - 2 * edge, vectors, size), bf16)
    norm_type = VM((8, vectors), f32)

    head, tail = call(
        edge_kernel,
        "edges",
        [first_rim_type, first_rim_type],
        [HBM_SPEC, VMEM_SPEC],
        [VM((2, vectors, edge * size), bf16), pltpu.SemaphoreType.DMA((2,))],
        0,
        start.size,
    )(start, weights)
    rims = outward(head, tail)

    places = 2 * ((slots + num_blocks) // 2)
    tab, flips, meta = pair_tables(
        slot_rows[0, 0], slot_cols[0, 0], rotation[0, 0], live_block_count[0, 0], num_blocks, places
    )
    matrix, rows = call(
        first_kernel,
        "own_first",
        [VM((slots + 1, size, size), bf16), tall_f32],
        [SMEM_SPEC] * 3 + [HBM_SPEC, HBM_SPEC, VMEM_SPEC],
        [
            VM((num_blocks + 1, tall, size), bf16),
            VM((vectors, cells), bf16),
            pltpu.SemaphoreType.DMA((CHUNKS + 1,)),
        ],
        2 * work,
        2 * blocks.size * 2,
    )(meta, tab, flips, blocks, start, weights)

    inverse = norm = None
    for turn in range(2):
        first = turn == 0
        if not first:
            (rows,) = call(
                own_kernel,
                "own_next",
                [block_f32],
                [SMEM_SPEC] * 2 + [VMEM_SPEC] * 4,
                [VM((num_blocks + 1, vectors, size), bf16)],
                work,
                blocks.size,
            )(meta, tab, matrix, head, middle, tail)
            rims = outward(head, tail)
        extra = [] if first else [inverse]
        result = call(
            functools.partial(rim_kernel, first),
            "rim_first" if first else "rim_next",
            [tall_f32 if first else block_f32, image_type]
            + ([VM((num_blocks, 8, size), f32)] if first else [])
            + [rim_type] * 4,
            [SMEM_SPEC] * 2 + [VMEM_SPEC] * (6 + len(extra)),
            [VM((num_blocks + 1, tall if first else vectors, size), bf16), block_f32],
            2 * work,
            blocks.size,
            {3: 0},
        )(meta, tab, matrix, rows, *rims, *extra)
        image = result[1]
        if first:
            inverse = result[2]
        left, right, upper, lower = result[-4:]
        lows = (shift(right, "tile", 1, True), shift(lower, "layer", 1, False))
        highs = (shift(left, "tile", -1, True), shift(upper, "layer", -1, False))
        (total,) = call(
            adjoint_kernel,
            "adjoint_first" if first else "adjoint_last",
            [block_f32],
            [SMEM_SPEC] * 2 + [VMEM_SPEC] * 2,
            [],
            work,
            blocks.size,
        )(meta, tab, matrix, image)
        if first:
            head, middle, tail, norm = call(
                join_kernel,
                "join",
                [rim_type, middle_type, rim_type, norm_type],
                [VMEM_SPEC] * 6,
                [],
                0,
                num_blocks * vectors * size * 8,
            )(total, weights, *lows, *highs)
    total, message = call(
        sum_kernel,
        "join_last",
        [block_f32, VM((devices, 2 * vectors), f32)],
        [VMEM_SPEC] * 7,
        [],
        0,
        num_blocks * vectors * size * 8,
        {0: 0},
    )(total, weights, *lows, *highs, norm)
    sums = lax.all_to_all(message, ("layer", "tile"), 0, 0, tiled=True)
    out = call(
        functools.partial(final_kernel, total_cells),
        "write_out",
        [jax.ShapeDtypeStruct((vectors, cells), bf16)],
        [VMEM_SPEC] * 2,
        [],
        0,
        cells * vectors * 6,
    )(sums, total)[0]
    return out[None, None]


def solution(mesh):
    in_specs = (
        P("layer", "tile", None, None, None),
        P("layer", "tile", None),
        P("layer", "tile", None),
        P("layer", "tile", None),
        P("layer", "tile"),
        P("layer", "tile", None),
        P("layer", "tile", None, None),
    )
    out_specs = P("layer", "tile", None, None)
    return jax.shard_map(local, mesh=mesh, in_specs=in_specs, out_specs=out_specs, check_vma=False)
```

```python
import functools

import jax
import jax.numpy as jnp
from jax import lax
from jax.experimental import pallas as pl
from jax.experimental.pallas import tpu as pltpu
from jax.sharding import PartitionSpec as P

UNROLL = 16
TURN = 8
CHUNKS = 8
VM = pltpu.VMEM
VMEM_SPEC = pl.BlockSpec(memory_space=pltpu.VMEM)
SMEM_SPEC = pl.BlockSpec(memory_space=pltpu.SMEM)
HBM_SPEC = pl.BlockSpec(memory_space=pltpu.HBM)
FORWARD_OWN, FORWARD_RIM, ADJOINT_OWN, ADJOINT_RIM = range(4)


def fill_tables(live_count, row, col, turned, num_blocks, tab):
    f32, bf16 = jnp.float32, jnp.bfloat16
    slots = row.shape[1]
    places = tab.shape[1]
    index = lax.broadcasted_iota(jnp.int32, (1, slots), 1)
    live = index < live_count
    rim = col >= num_blocks
    source = col - jnp.where(rim, num_blocks, 0)
    key = lax.broadcasted_iota(jnp.int32, (num_blocks, slots), 0)
    place = lax.broadcasted_iota(jnp.int32, (places, slots), 0)
    earlier = (
        lax.broadcasted_iota(jnp.int32, (slots, slots), 0) < lax.broadcasted_iota(jnp.int32, (slots, slots), 1)
    ).astype(f32).astype(bf16)
    below = (
        lax.broadcasted_iota(jnp.int32, (num_blocks, num_blocks), 1)
        < lax.broadcasted_iota(jnp.int32, (num_blocks, num_blocks), 0)
    ).astype(f32).astype(bf16)
    lane = lax.broadcasted_iota(jnp.int32, (1, places), 1)
    meta = jnp.zeros((1, places), jnp.int32)

    def invert(position, parts):
        found = (place == position).astype(f32).astype(bf16)
        parts = parts + [jnp.zeros((1, slots), jnp.int32)] * (8 - len(parts))
        values = jnp.concatenate([p.astype(f32) for p in parts], axis=0).astype(bf16)
        moved = lax.dot_general(values, found, (((1,), (1,)), ((), ())), preferred_element_type=f32)
        return moved.astype(jnp.int32)

    for which in range(4):
        dest, operand = (row, source) if which < ADJOINT_OWN else (source, row)
        used = live & (rim if which % 2 else ~rim)
        wanted = jnp.where(used, dest, -1)
        member = (key == wanted).astype(f32)
        before = jnp.dot(member.astype(bf16), earlier, preferred_element_type=f32)
        pairs = (jnp.sum(member, axis=1, keepdims=True).astype(jnp.int32) + 1) >> 1
        wide = jnp.broadcast_to(pairs.astype(f32), (num_blocks, 128)).astype(bf16)
        offset = jnp.dot(below, wide, preferred_element_type=f32)[:, :1]
        position = jnp.sum(member * (before + 2.0 * offset), axis=0, keepdims=True).astype(jnp.int32)
        position = jnp.where(used, position, -1)
        moved = invert(position, [index & 255, index >> 8, operand - num_blocks, dest])
        packed = moved[0:1] + (moved[1:2] << 8) + ((moved[2:3] + num_blocks) << 9) + (moved[3:4] << 16)
        tab[which : which + 1] = packed
        count = jnp.sum(pairs.astype(f32), axis=0, keepdims=True).astype(jnp.int32)
        meta = meta + jnp.where(lane == which, (count + (UNROLL - 1)) // UNROLL, 0)
    flip = live & (turned == 1)
    ones = jnp.broadcast_to(flip.astype(f32), (8, slots))
    rank = jnp.dot(ones.astype(bf16), earlier, preferred_element_type=f32)[:1].astype(jnp.int32)
    rank = jnp.where(flip, rank, -1)
    moved = invert(rank, [index & 255, index >> 8, flip.astype(jnp.int32)])
    tab[4:5] = jnp.where(moved[2:3] == 1, moved[0:1] + (moved[1:2] << 8), slots)
    count = jnp.sum(ones[:1], axis=1, keepdims=True).astype(jnp.int32)
    meta = meta + jnp.where(lane == 4, (count + (TURN - 1)) // TURN, 0)
    tab[5:6] = meta
    tab[6:8] = jnp.zeros((2, places), jnp.int32)


def pair_loop(which, tab, source, matrix, acc):
    transposed = which >= ADJOINT_OWN

    def body(step, carry):
        done = []
        for u in range(UNROLL):
            place = (step * UNROLL + u) * 2
            one, two = tab[which, place], tab[which, place + 1]
            lhs = jnp.concatenate([source[(one >> 9) & 127], source[(two >> 9) & 127]], axis=1)
            first, second = matrix[one & 511], matrix[two & 511]
            rhs = jnp.concatenate([first, second], axis=0 if transposed else 1)
            dims = (((1,), (0 if transposed else 1,)), ((), ()))
            done.append((one >> 16, lax.dot_general(lhs, rhs, dims, preferred_element_type=jnp.float32)))
        for dest, value in done:
            acc[dest] += value
        return carry

    lax.fori_loop(0, tab[5, which], body, 0)


def clear(ref):
    def body(b, carry):
        ref[b] = jnp.zeros(ref.shape[1:], ref.dtype)
        return carry

    lax.fori_loop(0, ref.shape[0], body, 0)


def edge_kernel(start, density, head, tail, weights, held, raw, sems):
    size = head.shape[1]
    vectors = start.shape[0]
    edge = head.shape[0] // (vectors + 1)
    width = edge * size
    outs = (head, tail)
    origin = (0, start.shape[1] - width)
    copies = [
        pltpu.make_async_copy(start.at[:, pl.ds(origin[i], width)], held.at[i], sems.at[i]) for i in range(2)
    ]
    copies.append(pltpu.make_async_copy(density, raw, sems.at[2]))
    for copy in copies:
        copy.start()
    copies[2].wait()
    for b in range(weights.shape[0]):
        weights[b : b + 1] = raw[:, b * size : (b + 1) * size].astype(jnp.float32)
    for i in range(2):
        copies[i].wait()
        first = origin[i] // size
        for b in range(edge):
            value = held[i, :, b * size : (b + 1) * size].astype(jnp.float32) * weights[first + b : first + b + 1]
            outs[i][b * vectors : (b + 1) * vectors] = value.astype(jnp.bfloat16)
        outs[i][edge * vectors :] = weights[first : first + edge].astype(jnp.bfloat16)


def first_kernel(count, blocks, start, row, col, turned, weights, matrix, rows, tab, source, held, lists, smem, sems):
    slots = blocks.shape[0]
    part = slots // CHUNKS
    small = [pltpu.make_async_copy(ref, lists.at[i], sems.at[CHUNKS + 1 + i]) for i, ref in enumerate((row, col, turned))]
    copies = small + [pltpu.make_async_copy(start, held, sems.at[CHUNKS])]
    for c in range(CHUNKS):
        here = pl.ds(c * part, part)
        copies.append(pltpu.make_async_copy(blocks.at[here], matrix.at[here], sems.at[c]))
    for copy in copies:
        copy.start()
    num_blocks, vectors = rows.shape[0], start.shape[0]
    size = blocks.shape[-1]
    clear(rows)
    matrix[slots] = jnp.zeros((size, size), matrix.dtype)
    source[num_blocks] = jnp.zeros(source.shape[1:], source.dtype)
    for copy in small:
        copy.wait()
    fill_tables(count[0], lists[0], lists[1], lists[2], num_blocks, tab)
    table_copy = pltpu.make_async_copy(tab, smem, sems.at[CHUNKS + 4])
    table_copy.start()
    copies[3].wait()
    top = lax.broadcasted_iota(jnp.int32, (16, size), 0) == 0

    def fill(b, carry):
        cells = pl.ds(pl.multiple_of(b * size, size), size)
        weight = weights[pl.ds(b, 1)]
        source[b, :vectors] = (held[:, cells].astype(jnp.float32) * weight).astype(jnp.bfloat16)
        source[b, vectors:] = jnp.where(top, jnp.broadcast_to(weight, (16, size)), 0.0).astype(jnp.bfloat16)
        return carry

    lax.fori_loop(0, num_blocks, fill, 0, unroll=4)
    across = lax.broadcasted_iota(jnp.int32, (size, size), 0)
    along = lax.broadcasted_iota(jnp.int32, (size, size), 1)
    mirror = (across + along == size - 1).astype(jnp.float32).astype(jnp.bfloat16)
    table_copy.wait()
    for copy in copies[4:]:
        copy.wait()

    def turn(step, carry):
        done = []
        for u in range(TURN):
            slot = smem[4, step * TURN + u]
            value = jnp.dot(matrix[slot], mirror, preferred_element_type=jnp.float32)
            done.append((slot, value.astype(jnp.bfloat16)))
        for slot, value in done:
            matrix[slot] = value
        return carry

    lax.fori_loop(0, smem[5, 4], turn, 0)
    pair_loop(FORWARD_OWN, smem, source, matrix, rows)


def own_kernel(tab, matrix, head, middle, tail, rows, source):
    clear(rows)
    num_blocks = rows.shape[0]
    edge = num_blocks // 4
    vectors = rows.shape[1]
    for b in range(edge):
        source[b] = head[b * vectors : (b + 1) * vectors]
        source[num_blocks - edge + b] = tail[b * vectors : (b + 1) * vectors]
    source[edge : num_blocks - edge] = middle[...]
    source[num_blocks] = jnp.zeros(source.shape[1:], source.dtype)
    pair_loop(FORWARD_OWN, tab, source, matrix, rows)


def rim_kernel(first, tab, matrix, rows_in, left, right, upper, lower, *rest):
    del rows_in
    if first:
        rows, image, inverse = rest[:3]
        rest = rest[3:]
    else:
        inverse, rows, image = rest[:3]
        rest = rest[3:]
    backs, (source, total) = rest[:4], rest[4:]
    num_blocks, size = rows.shape[0], rows.shape[2]
    vectors = image.shape[1]
    edge = num_blocks // 4
    for side, rim in enumerate((left, right, upper, lower)):
        for b in range(edge):
            source[side * edge + b, :vectors] = rim[b * vectors : (b + 1) * vectors]
        if first:
            weights = rim[edge * vectors :].astype(jnp.float32)
            top = lax.broadcasted_iota(jnp.int32, (16, size), 0) == 0
            for b in range(edge):
                pad = jnp.where(top, jnp.broadcast_to(weights[b : b + 1], (16, size)), 0.0)
                source[side * edge + b, vectors:] = pad.astype(jnp.bfloat16)
    source[num_blocks] = jnp.zeros(source.shape[1:], source.dtype)
    clear(total)
    pair_loop(FORWARD_RIM, tab, source, matrix, rows)

    def divide(b, carry):
        if first:
            factor = 1.0 / rows[b, vectors : vectors + 8]
            inverse[b] = factor
        else:
            factor = inverse[b]
        image[b] = (rows[b, :vectors] * factor[:1]).astype(jnp.bfloat16)
        return carry

    lax.fori_loop(0, num_blocks, divide, 0, unroll=4)
    image[num_blocks] = jnp.zeros(image.shape[1:], image.dtype)
    pair_loop(ADJOINT_RIM, tab, image, matrix, total)
    for side in range(4):
        for b in range(edge):
            backs[side][b * vectors : (b + 1) * vectors] = total[side * edge + b].astype(jnp.bfloat16)


def adjoint_kernel(tab, matrix, image, total):
    clear(total)
    pair_loop(ADJOINT_OWN, tab, image, matrix, total)


def collect(total, density, lows, highs, store):
    num_blocks, vectors, size = total.shape
    edge = num_blocks // 4

    def add(b, norm, parts):
        value = total[b]
        if parts:
            here = b if parts is lows else b - (num_blocks - edge)
            rows = pl.ds(pl.multiple_of(here * vectors, vectors), vectors)
            value = value + (parts[0][rows].astype(jnp.float32) + parts[1][rows].astype(jnp.float32))
        weighted = value * density[pl.ds(b, 1)]
        store(b, value, weighted)
        return norm + weighted * value

    norm = jnp.zeros((vectors, size), jnp.float32)
    norm = lax.fori_loop(0, edge, lambda b, n: add(b, n, lows), norm)
    norm = lax.fori_loop(edge, num_blocks - edge, lambda b, n: add(b, n, None), norm)
    norm = lax.fori_loop(num_blocks - edge, num_blocks, lambda b, n: add(b, n, highs), norm)
    ones = jnp.ones((8, size), jnp.float32)
    return lax.dot_general(
        ones, norm, (((1,), (1,)), ((), ())), precision=lax.Precision.HIGHEST, preferred_element_type=jnp.float32
    )


def join_kernel(total, density, low0, low1, high0, high1, head, middle, tail, norm):
    num_blocks, vectors, size = total.shape
    edge = num_blocks // 4
    high_from = num_blocks - edge

    def store(b, value, weighted):
        del value
        scaled = weighted.astype(jnp.bfloat16)

        def rows(first):
            return pl.ds(pl.multiple_of((b - first) * vectors, vectors), vectors)

        @pl.when(b < edge)
        def _():
            head[rows(0)] = scaled

        @pl.when((b >= edge) & (b < high_from))
        def _():
            middle[b - edge] = scaled

        @pl.when(b >= high_from)
        def _():
            tail[rows(high_from)] = scaled

    norm[...] = collect(total, density, (low0, low1), (high0, high1), store)


def sum_kernel(total_in, density, low0, low1, high0, high1, norm, total, message):
    del total_in

    def store(b, value, weighted):
        del weighted
        total[b] = value

    last = collect(total, density, (low0, low1), (high0, high1), store)
    both = jnp.concatenate([norm[...], last], axis=1)[:1]
    message[...] = jnp.broadcast_to(both, message.shape)


def final_kernel(total_cells, sums, total, out):
    num_blocks, vectors, size = total.shape
    both = jnp.sum(sums[...], axis=0, keepdims=True) * (1.0 / total_cells)
    diagonal = lax.broadcasted_iota(jnp.int32, (vectors, size), 0)
    lane = lax.broadcasted_iota(jnp.int32, (vectors, size), 1)
    both = jnp.broadcast_to(both, (vectors, size))
    first = jnp.sum(jnp.where(lane == diagonal, both, 0.0), axis=1, keepdims=True)
    second = jnp.sum(jnp.where(lane == diagonal + vectors, both, 0.0), axis=1, keepdims=True)
    factor = lax.rsqrt(first + 1e-06)
    scale = jnp.broadcast_to(factor * lax.rsqrt(factor * factor * second + 1e-06), (vectors, size))

    def body(b, carry):
        cells = pl.ds(pl.multiple_of(b * size, size), size)
        out[:, cells] = (total[b] * scale).astype(jnp.bfloat16)
        return carry

    lax.fori_loop(0, num_blocks, body, 0, unroll=4)


def shift(x, axis, step, periodic):
    count = lax.axis_size(axis)
    route = [(i, (i + step) % count) for i in range(count) if periodic or 0 <= i + step < count]
    return lax.ppermute(x, axis, route)


def outward(head, tail):
    return (
        shift(tail, "tile", 1, True),
        shift(head, "tile", -1, True),
        shift(tail, "layer", 1, False),
        shift(head, "layer", -1, False),
    )


def call(kernel, name, outs, in_specs, scratch, flops, nbytes, aliases={}):
    return pl.pallas_call(
        kernel,
        name=name,
        out_shape=outs,
        in_specs=in_specs,
        out_specs=[VMEM_SPEC] * len(outs),
        scratch_shapes=scratch,
        input_output_aliases=aliases,
        compiler_params=pltpu.CompilerParams(vmem_limit_bytes=16 * 1024 * 1024),
        cost_estimate=pl.CostEstimate(flops=flops, bytes_accessed=nbytes, transcendentals=0),
    )


def local(blocks, slot_rows, slot_cols, rotation, live_block_count, density, start):
    bf16, f32 = jnp.bfloat16, jnp.float32
    blocks, start = blocks[0, 0], start[0, 0]
    slots, size = blocks.shape[0], blocks.shape[2]
    vectors, cells = start.shape
    num_blocks = cells // size
    edge = num_blocks // 4
    devices = lax.axis_size("layer") * lax.axis_size("tile")
    total_cells = cells * devices
    work = slots * size * size * vectors
    tall = vectors + 16
    rim_type = VM((edge * vectors, size), bf16)
    first_rim_type = VM((edge * (vectors + 1), size), bf16)
    block_f32 = VM((num_blocks, vectors, size), f32)
    tall_f32 = VM((num_blocks, tall, size), f32)
    image_type = VM((num_blocks + 1, vectors, size), bf16)
    middle_type = VM((num_blocks - 2 * edge, vectors, size), bf16)
    norm_type = VM((8, vectors), f32)

    def outside(x):
        return pltpu.with_memory_space_constraint(x, pltpu.HBM)

    start = outside(start)
    head, tail, weights = call(
        edge_kernel,
        "edges",
        [first_rim_type, first_rim_type, VM((num_blocks, size), f32)],
        [HBM_SPEC, HBM_SPEC],
        [
            VM((2, vectors, edge * size), bf16),
            VM((1, cells), bf16),
            pltpu.SemaphoreType.DMA((3,)),
        ],
        0,
        start.size,
    )(start, outside(density[0]))
    rims = outward(head, tail)

    places = 2 * ((slots + num_blocks) // 2)
    matrix, rows, tab = call(
        first_kernel,
        "own_first",
        [VM((slots + 1, size, size), bf16), tall_f32, VM((8, places), jnp.int32)],
        [SMEM_SPEC] + [HBM_SPEC] * 5 + [VMEM_SPEC],
        [
            VM((num_blocks + 1, tall, size), bf16),
            VM((vectors, cells), bf16),
            VM((3, 1, slots), jnp.int32),
            pltpu.SMEM((8, places), jnp.int32),
            pltpu.SemaphoreType.DMA((CHUNKS + 5,)),
        ],
        2 * work,
        2 * blocks.size * 2,
    )(
        live_block_count[0],
        outside(blocks),
        start,
        outside(slot_rows[0]),
        outside(slot_cols[0]),
        outside(rotation[0]),
        weights,
    )

    inverse = norm = None
    for turn in range(2):
        first = turn == 0
        if not first:
            (rows,) = call(
                own_kernel,
                "own_next",
                [block_f32],
                [SMEM_SPEC] + [VMEM_SPEC] * 4,
                [VM((num_blocks + 1, vectors, size), bf16)],
                work,
                blocks.size,
            )(tab, matrix, head, middle, tail)
            rims = outward(head, tail)
        extra = [] if first else [inverse]
        result = call(
            functools.partial(rim_kernel, first),
            "rim_first" if first else "rim_next",
            [tall_f32 if first else block_f32, image_type]
            + ([VM((num_blocks, 8, size), f32)] if first else [])
            + [rim_type] * 4,
            [SMEM_SPEC] + [VMEM_SPEC] * (6 + len(extra)),
            [VM((num_blocks + 1, tall if first else vectors, size), bf16), block_f32],
            2 * work,
            blocks.size,
            {2: 0},
        )(tab, matrix, rows, *rims, *extra)
        image = result[1]
        if first:
            inverse = result[2]
        left, right, upper, lower = result[-4:]
        lows = (shift(right, "tile", 1, True), shift(lower, "layer", 1, False))
        highs = (shift(left, "tile", -1, True), shift(upper, "layer", -1, False))
        (total,) = call(
            adjoint_kernel,
            "adjoint_first" if first else "adjoint_last",
            [block_f32],
            [SMEM_SPEC] + [VMEM_SPEC] * 2,
            [],
            work,
            blocks.size,
        )(tab, matrix, image)
        if first:
            head, middle, tail, norm = call(
                join_kernel,
                "join",
                [rim_type, middle_type, rim_type, norm_type],
                [VMEM_SPEC] * 6,
                [],
                0,
                num_blocks * vectors * size * 8,
            )(total, weights, *lows, *highs)
    total, message = call(
        sum_kernel,
        "join_last",
        [block_f32, VM((devices, 2 * vectors), f32)],
        [VMEM_SPEC] * 7,
        [],
        0,
        num_blocks * vectors * size * 8,
        {0: 0},
    )(total, weights, *lows, *highs, norm)
    sums = lax.all_to_all(message, ("layer", "tile"), 0, 0, tiled=True)
    out = call(
        functools.partial(final_kernel, total_cells),
        "write_out",
        [jax.ShapeDtypeStruct((vectors, cells), bf16)],
        [VMEM_SPEC] * 2,
        [],
        0,
        cells * vectors * 6,
    )(sums, total)[0]
    return out[None, None]


def solution(mesh):
    in_specs = (
        P("layer", "tile", None, None, None),
        P("layer", "tile", None),
        P("layer", "tile", None),
        P("layer", "tile", None),
        P("layer", "tile"),
        P("layer", "tile", None),
        P("layer", "tile", None, None),
    )
    out_specs = P("layer", "tile", None, None)
    return jax.shard_map(local, mesh=mesh, in_specs=in_specs, out_specs=out_specs, check_vma=False)
```

```python
import functools

import jax
import jax.numpy as jnp
from jax import lax
from jax.experimental import pallas as pl
from jax.experimental.pallas import tpu as pltpu
from jax.sharding import PartitionSpec as P

UNROLL = 16
TURN = 8
CHUNKS = 8
VM = pltpu.VMEM
VMEM_SPEC = pl.BlockSpec(memory_space=pltpu.VMEM)
SMEM_SPEC = pl.BlockSpec(memory_space=pltpu.SMEM)
HBM_SPEC = pl.BlockSpec(memory_space=pltpu.HBM)
FORWARD_OWN, FORWARD_HEADS, FORWARD_TAILS, ADJOINT_OWN, ADJOINT_HEADS, ADJOINT_TAILS, FLIPS, TRIPS = range(8)


def fill_tables(live_count, row, col, turned, num_blocks, tab):
    f32, bf16 = jnp.float32, jnp.bfloat16
    slots = row.shape[1]
    places = tab.shape[1]
    index = lax.broadcasted_iota(jnp.int32, (1, slots), 1)
    live = index < live_count
    edge = num_blocks // 4
    outer = col - num_blocks
    side = outer // edge
    own = outer < 0
    heads = (outer >= 0) & ((side & 1) == 1)
    tails = (outer >= 0) & ((side & 1) == 0)
    source = jnp.where(own, col, (side >> 1) * edge + outer - side * edge)
    key = lax.broadcasted_iota(jnp.int32, (num_blocks, slots), 0)
    place = lax.broadcasted_iota(jnp.int32, (places, slots), 0)
    earlier = (
        lax.broadcasted_iota(jnp.int32, (slots, slots), 0) < lax.broadcasted_iota(jnp.int32, (slots, slots), 1)
    ).astype(f32).astype(bf16)
    below = (
        lax.broadcasted_iota(jnp.int32, (num_blocks, num_blocks), 1)
        < lax.broadcasted_iota(jnp.int32, (num_blocks, num_blocks), 0)
    ).astype(f32).astype(bf16)
    lane = lax.broadcasted_iota(jnp.int32, (1, places), 1)
    meta = jnp.zeros((1, places), jnp.int32)

    def invert(position, parts):
        found = (place == position).astype(f32).astype(bf16)
        parts = parts + [jnp.zeros((1, slots), jnp.int32)] * (8 - len(parts))
        values = jnp.concatenate([p.astype(f32) for p in parts], axis=0).astype(bf16)
        moved = lax.dot_general(values, found, (((1,), (1,)), ((), ())), preferred_element_type=f32)
        return moved.astype(jnp.int32)

    parts = ((own, num_blocks), (heads, 2 * edge), (tails, 2 * edge))
    for which in range(6):
        chosen, empty = parts[which % 3]
        dest, operand = row, source
        if which >= ADJOINT_OWN:
            dest, operand, empty = source, row, num_blocks
        used = live & chosen
        wanted = jnp.where(used, dest, -1)
        member = (key == wanted).astype(f32)
        before = jnp.dot(member.astype(bf16), earlier, preferred_element_type=f32)
        pairs = (jnp.sum(member, axis=1, keepdims=True).astype(jnp.int32) + 1) >> 1
        wide = jnp.broadcast_to(pairs.astype(f32), (num_blocks, 128)).astype(bf16)
        offset = jnp.dot(below, wide, preferred_element_type=f32)[:, :1]
        position = jnp.sum(member * (before + 2.0 * offset), axis=0, keepdims=True).astype(jnp.int32)
        position = jnp.where(used, position, -1)
        moved = invert(position, [index & 255, index >> 8, operand - empty, dest])
        packed = moved[0:1] + (moved[1:2] << 8) + ((moved[2:3] + empty) << 9) + (moved[3:4] << 16)
        tab[which : which + 1] = packed
        count = jnp.sum(pairs.astype(f32), axis=0, keepdims=True).astype(jnp.int32)
        meta = meta + jnp.where(lane == which, (count + (UNROLL - 1)) // UNROLL, 0)
    flip = live & (turned == 1)
    ones = jnp.broadcast_to(flip.astype(f32), (8, slots))
    rank = jnp.dot(ones.astype(bf16), earlier, preferred_element_type=f32)[:1].astype(jnp.int32)
    rank = jnp.where(flip, rank, -1)
    moved = invert(rank, [index & 255, index >> 8, flip.astype(jnp.int32)])
    tab[FLIPS : FLIPS + 1] = jnp.where(moved[2:3] == 1, moved[0:1] + (moved[1:2] << 8), slots)
    count = jnp.sum(ones[:1], axis=1, keepdims=True).astype(jnp.int32)
    meta = meta + jnp.where(lane == FLIPS, (count + (TURN - 1)) // TURN, 0)
    tab[TRIPS : TRIPS + 1] = meta


def pair_loop(which, tab, source, matrix, acc):
    transposed = which >= ADJOINT_OWN

    def body(step, carry):
        done = []
        for u in range(UNROLL):
            place = (step * UNROLL + u) * 2
            one, two = tab[which, place], tab[which, place + 1]
            lhs = jnp.concatenate([source[(one >> 9) & 127], source[(two >> 9) & 127]], axis=1)
            first, second = matrix[one & 511], matrix[two & 511]
            rhs = jnp.concatenate([first, second], axis=0 if transposed else 1)
            dims = (((1,), (0 if transposed else 1,)), ((), ()))
            done.append((one >> 16, lax.dot_general(lhs, rhs, dims, preferred_element_type=jnp.float32)))
        for dest, value in done:
            acc[dest] += value
        return carry

    lax.fori_loop(0, tab[TRIPS, which], body, 0)


def clear(ref):
    def body(b, carry):
        ref[b] = jnp.zeros(ref.shape[1:], ref.dtype)
        return carry

    lax.fori_loop(0, ref.shape[0], body, 0)


def edge_kernel(start, density, head, tail, weights, held, raw, sems):
    size = head.shape[1]
    vectors = start.shape[0]
    edge = head.shape[0] // (vectors + 1)
    width = edge * size
    outs = (head, tail)
    origin = (0, start.shape[1] - width)
    copies = [
        pltpu.make_async_copy(start.at[:, pl.ds(origin[i], width)], held.at[i], sems.at[i]) for i in range(2)
    ]
    copies.append(pltpu.make_async_copy(density, raw, sems.at[2]))
    for copy in copies:
        copy.start()
    copies[2].wait()
    for b in range(weights.shape[0]):
        weights[b : b + 1] = raw[:, b * size : (b + 1) * size].astype(jnp.float32)
    for i in range(2):
        copies[i].wait()
        first = origin[i] // size
        for b in range(edge):
            value = held[i, :, b * size : (b + 1) * size].astype(jnp.float32) * weights[first + b : first + b + 1]
            outs[i][b * vectors : (b + 1) * vectors] = value.astype(jnp.bfloat16)
        outs[i][edge * vectors :] = weights[first : first + edge].astype(jnp.bfloat16)


def first_kernel(count, blocks, start, row, col, turned, weights, matrix, rows, tab, source, held, lists, smem, sems):
    slots = blocks.shape[0]
    part = slots // CHUNKS
    small = [pltpu.make_async_copy(ref, lists.at[i], sems.at[CHUNKS + 1 + i]) for i, ref in enumerate((row, col, turned))]
    copies = small + [pltpu.make_async_copy(start, held, sems.at[CHUNKS])]
    for c in range(CHUNKS):
        here = pl.ds(c * part, part)
        copies.append(pltpu.make_async_copy(blocks.at[here], matrix.at[here], sems.at[c]))
    for copy in copies:
        copy.start()
    num_blocks, vectors = rows.shape[0], start.shape[0]
    size = blocks.shape[-1]
    clear(rows)
    matrix[slots] = jnp.zeros((size, size), matrix.dtype)
    source[num_blocks] = jnp.zeros(source.shape[1:], source.dtype)
    for copy in small:
        copy.wait()
    fill_tables(count[0], lists[0], lists[1], lists[2], num_blocks, tab)
    table_copy = pltpu.make_async_copy(tab, smem, sems.at[CHUNKS + 4])
    table_copy.start()
    copies[3].wait()
    top = lax.broadcasted_iota(jnp.int32, (16, size), 0) == 0

    def fill(b, carry):
        cells = pl.ds(pl.multiple_of(b * size, size), size)
        weight = weights[pl.ds(b, 1)]
        source[b, :vectors] = (held[:, cells].astype(jnp.float32) * weight).astype(jnp.bfloat16)
        source[b, vectors:] = jnp.where(top, jnp.broadcast_to(weight, (16, size)), 0.0).astype(jnp.bfloat16)
        return carry

    lax.fori_loop(0, num_blocks, fill, 0, unroll=4)
    across = lax.broadcasted_iota(jnp.int32, (size, size), 0)
    along = lax.broadcasted_iota(jnp.int32, (size, size), 1)
    mirror = (across + along == size - 1).astype(jnp.float32).astype(jnp.bfloat16)
    table_copy.wait()
    for copy in copies[4:]:
        copy.wait()

    def turn(step, carry):
        done = []
        for u in range(TURN):
            slot = smem[FLIPS, step * TURN + u]
            value = jnp.dot(matrix[slot], mirror, preferred_element_type=jnp.float32)
            done.append((slot, value.astype(jnp.bfloat16)))
        for slot, value in done:
            matrix[slot] = value
        return carry

    lax.fori_loop(0, smem[TRIPS, FLIPS], turn, 0)
    pair_loop(FORWARD_OWN, smem, source, matrix, rows)


def own_kernel(tab, matrix, head, middle, tail, rows, source):
    clear(rows)
    num_blocks = rows.shape[0]
    edge = num_blocks // 4
    vectors = rows.shape[1]
    for b in range(edge):
        source[b] = head[b * vectors : (b + 1) * vectors]
        source[num_blocks - edge + b] = tail[b * vectors : (b + 1) * vectors]
    source[edge : num_blocks - edge] = middle[...]
    source[num_blocks] = jnp.zeros(source.shape[1:], source.dtype)
    pair_loop(FORWARD_OWN, tab, source, matrix, rows)


def load_rims(first, rims, source):
    edge = source.shape[0] // 2
    vectors = rims[0].shape[0] // edge - (1 if first else 0)
    size = source.shape[2]
    for side, rim in enumerate(rims):
        for b in range(edge):
            source[side * edge + b, :vectors] = rim[b * vectors : (b + 1) * vectors]
        if first:
            weights = rim[edge * vectors :].astype(jnp.float32)
            top = lax.broadcasted_iota(jnp.int32, (16, size), 0) == 0
            for b in range(edge):
                pad = jnp.where(top, jnp.broadcast_to(weights[b : b + 1], (16, size)), 0.0)
                source[side * edge + b, vectors:] = pad.astype(jnp.bfloat16)
    source[2 * edge] = jnp.zeros(source.shape[1:], source.dtype)


def heads_kernel(first, tab, matrix, rows_in, right, lower, rows, source):
    del rows_in
    load_rims(first, (right, lower), source)
    pair_loop(FORWARD_HEADS, tab, source, matrix, rows)


def send_back(total, backs):
    vectors = total.shape[1]
    edge = total.shape[0] // 2
    for side in range(2):
        for b in range(edge):
            backs[side][b * vectors : (b + 1) * vectors] = total[side * edge + b].astype(jnp.bfloat16)


def middle_kernel(first, tab, matrix, rows_in, left, upper, *rest):
    del rows_in
    if first:
        rows, image, inverse = rest[:3]
    else:
        inverse, rows, image = rest[:3]
    right_back, lower_back, source, total = rest[3:]
    num_blocks = rows.shape[0]
    vectors = image.shape[1]
    load_rims(first, (left, upper), source)
    clear(total)
    pair_loop(FORWARD_TAILS, tab, source, matrix, rows)

    def divide(b, carry):
        if first:
            factor = 1.0 / rows[b, vectors : vectors + 8]
            inverse[b] = factor
        else:
            factor = inverse[b]
        image[b] = (rows[b, :vectors] * factor[:1]).astype(jnp.bfloat16)
        return carry

    lax.fori_loop(0, num_blocks, divide, 0, unroll=4)
    image[num_blocks] = jnp.zeros(image.shape[1:], image.dtype)
    pair_loop(ADJOINT_HEADS, tab, image, matrix, total)
    send_back(total, (right_back, lower_back))


def tails_kernel(tab, matrix, image, left_back, upper_back, total):
    clear(total)
    pair_loop(ADJOINT_TAILS, tab, image, matrix, total)
    send_back(total, (left_back, upper_back))


def adjoint_kernel(tab, matrix, image, weights, total, norm, *rest):
    clear(total)
    pair_loop(ADJOINT_OWN, tab, image, matrix, total)
    num_blocks = total.shape[0]
    edge = num_blocks // 4

    def inside(b, sums):
        value = total[b]
        weighted = value * weights[pl.ds(b, 1)]
        if rest:
            rest[0][b - edge] = weighted.astype(jnp.bfloat16)
        return sums + weighted * value

    zero = jnp.zeros(norm.shape, jnp.float32)
    norm[...] = lax.fori_loop(edge, num_blocks - edge, inside, zero)


def add_edge(total, weights, from_block, one, two, sums, store):
    vectors = total.shape[1]

    def add(b, carry):
        rows = pl.ds(pl.multiple_of(b * vectors, vectors), vectors)
        value = total[from_block + b] + (one[rows].astype(jnp.float32) + two[rows].astype(jnp.float32))
        weighted = value * weights[pl.ds(from_block + b, 1)]
        store(b, rows, value, weighted)
        return carry + weighted * value

    return lax.fori_loop(0, total.shape[0] // 4, add, sums, unroll=2)


def join_kernel(tail, total, weights, one, two, norm_in, out, norm):
    def store(b, rows, value, weighted):
        out[rows] = weighted.astype(jnp.bfloat16)

    from_block = total.shape[0] // 4 * 3 if tail else 0
    norm[...] = add_edge(total, weights, from_block, one, two, norm_in[...], store)


def sum_kernel(total_in, weights, low0, low1, high0, high1, norm_in, norm_first, total, message):
    del total_in
    sums = norm_in[...]
    size = total.shape[2]
    for from_block, one, two in ((0, low0, low1), (total.shape[0] // 4 * 3, high0, high1)):

        def store(b, rows, value, weighted, from_block=from_block):
            total[from_block + b] = value

        sums = add_edge(total, weights, from_block, one, two, sums, store)
    ones = jnp.ones((8, size), jnp.float32)
    both = [
        lax.dot_general(
            ones, part, (((1,), (1,)), ((), ())), precision=lax.Precision.HIGHEST, preferred_element_type=jnp.float32
        )
        for part in (norm_first[...], sums)
    ]
    message[...] = jnp.broadcast_to(jnp.concatenate(both, axis=1)[:1], message.shape)


def final_kernel(total_cells, sums, total, out):
    num_blocks, vectors, size = total.shape
    both = jnp.sum(sums[...], axis=0, keepdims=True) * (1.0 / total_cells)
    diagonal = lax.broadcasted_iota(jnp.int32, (vectors, size), 0)
    lane = lax.broadcasted_iota(jnp.int32, (vectors, size), 1)
    both = jnp.broadcast_to(both, (vectors, size))
    first = jnp.sum(jnp.where(lane == diagonal, both, 0.0), axis=1, keepdims=True)
    second = jnp.sum(jnp.where(lane == diagonal + vectors, both, 0.0), axis=1, keepdims=True)
    factor = lax.rsqrt(first + 1e-06)
    scale = jnp.broadcast_to(factor * lax.rsqrt(factor * factor * second + 1e-06), (vectors, size))

    def body(b, carry):
        cells = pl.ds(pl.multiple_of(b * size, size), size)
        out[:, cells] = (total[b] * scale).astype(jnp.bfloat16)
        return carry

    lax.fori_loop(0, num_blocks, body, 0, unroll=4)


def shift(x, axis, step, periodic):
    count = lax.axis_size(axis)
    route = [(i, (i + step) % count) for i in range(count) if periodic or 0 <= i + step < count]
    return lax.ppermute(x, axis, route)


def heads_out(head):
    return shift(head, "tile", -1, True), shift(head, "layer", -1, False)


def tails_out(tail):
    return shift(tail, "tile", 1, True), shift(tail, "layer", 1, False)


def call(kernel, name, outs, in_specs, scratch, flops, nbytes, aliases={}):
    return pl.pallas_call(
        kernel,
        name=name,
        out_shape=outs,
        in_specs=in_specs,
        out_specs=[VMEM_SPEC] * len(outs),
        scratch_shapes=scratch,
        input_output_aliases=aliases,
        compiler_params=pltpu.CompilerParams(vmem_limit_bytes=16 * 1024 * 1024),
        cost_estimate=pl.CostEstimate(flops=flops, bytes_accessed=nbytes, transcendentals=0),
    )


def local(blocks, slot_rows, slot_cols, rotation, live_block_count, density, start):
    bf16, f32 = jnp.bfloat16, jnp.float32
    blocks, start = blocks[0, 0], start[0, 0]
    slots, size = blocks.shape[0], blocks.shape[2]
    vectors, cells = start.shape
    num_blocks = cells // size
    edge = num_blocks // 4
    devices = lax.axis_size("layer") * lax.axis_size("tile")
    total_cells = cells * devices
    work = slots * size * size * vectors
    tall = vectors + 16
    rim_type = VM((edge * vectors, size), bf16)
    first_rim_type = VM((edge * (vectors + 1), size), bf16)
    block_f32 = VM((num_blocks, vectors, size), f32)
    tall_f32 = VM((num_blocks, tall, size), f32)
    image_type = VM((num_blocks + 1, vectors, size), bf16)
    middle_type = VM((num_blocks - 2 * edge, vectors, size), bf16)
    norm_type = VM((vectors, size), f32)

    def outside(x):
        return pltpu.with_memory_space_constraint(x, pltpu.HBM)

    start = outside(start)
    head, tail, weights = call(
        edge_kernel,
        "edges",
        [first_rim_type, first_rim_type, VM((num_blocks, size), f32)],
        [HBM_SPEC, HBM_SPEC],
        [
            VM((2, vectors, edge * size), bf16),
            VM((1, cells), bf16),
            pltpu.SemaphoreType.DMA((3,)),
        ],
        0,
        start.size,
    )(start, outside(density[0]))
    heads, tails = heads_out(head), tails_out(tail)

    places = 2 * ((slots + num_blocks) // 2)
    matrix, rows, tab = call(
        first_kernel,
        "own_first",
        [VM((slots + 1, size, size), bf16), tall_f32, VM((8, places), jnp.int32)],
        [SMEM_SPEC] + [HBM_SPEC] * 5 + [VMEM_SPEC],
        [
            VM((num_blocks + 1, tall, size), bf16),
            VM((vectors, cells), bf16),
            VM((3, 1, slots), jnp.int32),
            pltpu.SMEM((8, places), jnp.int32),
            pltpu.SemaphoreType.DMA((CHUNKS + 5,)),
        ],
        2 * work,
        2 * blocks.size * 2,
    )(
        live_block_count[0],
        outside(blocks),
        start,
        outside(slot_rows[0]),
        outside(slot_cols[0]),
        outside(rotation[0]),
        weights,
    )

    inverse = None
    for turn in range(2):
        first = turn == 0
        rows_type = tall_f32 if first else block_f32
        source_type = VM((2 * edge + 1, tall if first else vectors, size), bf16)
        half_f32 = VM((2 * edge, vectors, size), f32)
        suffix = "_first" if first else "_next"
        if not first:
            (rows,) = call(
                own_kernel,
                "own_next",
                [block_f32],
                [SMEM_SPEC] + [VMEM_SPEC] * 4,
                [VM((num_blocks + 1, vectors, size), bf16)],
                work,
                blocks.size,
            )(tab, matrix, head, middle, tail)
        (rows,) = call(
            functools.partial(heads_kernel, first),
            "heads" + suffix,
            [rows_type],
            [SMEM_SPEC] + [VMEM_SPEC] * 4,
            [source_type],
            work // 2,
            blocks.size // 2,
            {2: 0},
        )(tab, matrix, rows, *heads)
        extra = [] if first else [inverse]
        result = call(
            functools.partial(middle_kernel, first),
            "middle" + suffix,
            [rows_type, image_type] + ([VM((num_blocks, 8, size), f32)] if first else []) + [rim_type] * 2,
            [SMEM_SPEC] + [VMEM_SPEC] * (4 + len(extra)),
            [source_type, half_f32],
            work,
            blocks.size,
            {2: 0},
        )(tab, matrix, rows, *tails, *extra)
        image = result[1]
        if first:
            inverse = result[2]
        right, lower = result[-2:]
        lows = (shift(right, "tile", 1, True), shift(lower, "layer", 1, False))
        left, upper = call(
            tails_kernel,
            "tails" + suffix,
            [rim_type] * 2,
            [SMEM_SPEC] + [VMEM_SPEC] * 2,
            [half_f32],
            work // 2,
            blocks.size // 2,
        )(tab, matrix, image)
        highs = (shift(left, "tile", -1, True), shift(upper, "layer", -1, False))
        result = call(
            adjoint_kernel,
            "adjoint" + suffix,
            [block_f32, norm_type] + ([middle_type] if first else []),
            [SMEM_SPEC] + [VMEM_SPEC] * 3,
            [],
            work,
            blocks.size,
        )(tab, matrix, image, weights)
        total, norm = result[:2]
        if first:
            middle = result[2]
            head, norm = call(
                functools.partial(join_kernel, False),
                "join_head",
                [rim_type, norm_type],
                [VMEM_SPEC] * 5,
                [],
                0,
                edge * vectors * size * 8,
            )(total, weights, *lows, norm)
            heads = heads_out(head)
            tail, norm_first = call(
                functools.partial(join_kernel, True),
                "join_tail",
                [rim_type, norm_type],
                [VMEM_SPEC] * 5,
                [],
                0,
                edge * vectors * size * 8,
            )(total, weights, *highs, norm)
            tails = tails_out(tail)
    total, message = call(
        sum_kernel,
        "join_last",
        [block_f32, VM((devices, 2 * vectors), f32)],
        [VMEM_SPEC] * 8,
        [],
        0,
        2 * edge * vectors * size * 8,
        {0: 0},
    )(total, weights, *lows, *highs, norm, norm_first)
    sums = lax.all_to_all(message, ("layer", "tile"), 0, 0, tiled=True)
    out = call(
        functools.partial(final_kernel, total_cells),
        "write_out",
        [jax.ShapeDtypeStruct((vectors, cells), bf16)],
        [VMEM_SPEC] * 2,
        [],
        0,
        cells * vectors * 6,
    )(sums, total)[0]
    return out[None, None]


def solution(mesh):
    in_specs = (
        P("layer", "tile", None, None, None),
        P("layer", "tile", None),
        P("layer", "tile", None),
        P("layer", "tile", None),
        P("layer", "tile"),
        P("layer", "tile", None),
        P("layer", "tile", None, None),
    )
    out_specs = P("layer", "tile", None, None)
    return jax.shard_map(local, mesh=mesh, in_specs=in_specs, out_specs=out_specs, check_vma=False)
```

```python
import functools

import jax
import jax.numpy as jnp
from jax import lax
from jax.experimental import pallas as pl
from jax.experimental.pallas import tpu as pltpu
from jax.sharding import PartitionSpec as P

UNROLL = 16
TURN = 8
CHUNKS = 8
VM = pltpu.VMEM
VMEM_SPEC = pl.BlockSpec(memory_space=pltpu.VMEM)
SMEM_SPEC = pl.BlockSpec(memory_space=pltpu.SMEM)
HBM_SPEC = pl.BlockSpec(memory_space=pltpu.HBM)
FORWARD_OWN, FORWARD_HEADS, FORWARD_TAILS, ADJOINT_OWN, ADJOINT_HEADS, ADJOINT_TAILS, FLIPS, TRIPS = range(8)


def fill_tables(live_count, above, beneath, row, col, turned, num_blocks, tab):
    f32, bf16 = jnp.float32, jnp.bfloat16
    slots = row.shape[1]
    places = tab.shape[1]
    index = lax.broadcasted_iota(jnp.int32, (1, slots), 1)
    live = index < live_count
    edge = num_blocks // 4
    outer = col - num_blocks
    side = outer // edge
    live = live & ((side != 2) | (above == 1)) & ((side != 3) | (beneath == 1))
    own = outer < 0
    heads = (outer >= 0) & ((side & 1) == 1)
    tails = (outer >= 0) & ((side & 1) == 0)
    source = jnp.where(own, col, (side >> 1) * edge + outer - side * edge)
    key = lax.broadcasted_iota(jnp.int32, (num_blocks, slots), 0)
    place = lax.broadcasted_iota(jnp.int32, (places, slots), 0)
    earlier = (
        lax.broadcasted_iota(jnp.int32, (slots, slots), 0) < lax.broadcasted_iota(jnp.int32, (slots, slots), 1)
    ).astype(f32).astype(bf16)
    below = (
        lax.broadcasted_iota(jnp.int32, (num_blocks, num_blocks), 1)
        < lax.broadcasted_iota(jnp.int32, (num_blocks, num_blocks), 0)
    ).astype(f32).astype(bf16)
    lane = lax.broadcasted_iota(jnp.int32, (1, places), 1)
    meta = jnp.zeros((1, places), jnp.int32)

    def invert(position, parts):
        found = (place == position).astype(f32).astype(bf16)
        parts = parts + [jnp.zeros((1, slots), jnp.int32)] * (8 - len(parts))
        values = jnp.concatenate([p.astype(f32) for p in parts], axis=0).astype(bf16)
        moved = lax.dot_general(values, found, (((1,), (1,)), ((), ())), preferred_element_type=f32)
        return moved.astype(jnp.int32)

    parts = ((own, num_blocks), (heads, 2 * edge), (tails, 2 * edge))
    for which in range(6):
        chosen, empty = parts[which % 3]
        dest, operand = row, source
        if which >= ADJOINT_OWN:
            dest, operand, empty = source, row, num_blocks
        used = live & chosen
        wanted = jnp.where(used, dest, -1)
        member = (key == wanted).astype(f32)
        before = jnp.dot(member.astype(bf16), earlier, preferred_element_type=f32)
        pairs = (jnp.sum(member, axis=1, keepdims=True).astype(jnp.int32) + 1) >> 1
        wide = jnp.broadcast_to(pairs.astype(f32), (num_blocks, 128)).astype(bf16)
        offset = jnp.dot(below, wide, preferred_element_type=f32)[:, :1]
        position = jnp.sum(member * (before + 2.0 * offset), axis=0, keepdims=True).astype(jnp.int32)
        position = jnp.where(used, position, -1)
        moved = invert(position, [index & 255, index >> 8, operand - empty, dest])
        packed = moved[0:1] + (moved[1:2] << 8) + ((moved[2:3] + empty) << 9) + (moved[3:4] << 16)
        tab[which : which + 1] = packed
        count = jnp.sum(pairs.astype(f32), axis=0, keepdims=True).astype(jnp.int32)
        meta = meta + jnp.where(lane == which, (count + (UNROLL - 1)) // UNROLL, 0)
    flip = live & (turned == 1)
    ones = jnp.broadcast_to(flip.astype(f32), (8, slots))
    rank = jnp.dot(ones.astype(bf16), earlier, preferred_element_type=f32)[:1].astype(jnp.int32)
    rank = jnp.where(flip, rank, -1)
    moved = invert(rank, [index & 255, index >> 8, flip.astype(jnp.int32)])
    tab[FLIPS : FLIPS + 1] = jnp.where(moved[2:3] == 1, moved[0:1] + (moved[1:2] << 8), slots)
    count = jnp.sum(ones[:1], axis=1, keepdims=True).astype(jnp.int32)
    meta = meta + jnp.where(lane == FLIPS, (count + (TURN - 1)) // TURN, 0)
    tab[TRIPS : TRIPS + 1] = meta


def pair_loop(which, tab, source, matrix, acc):
    transposed = which >= ADJOINT_OWN

    def body(step, carry):
        done = []
        for u in range(UNROLL):
            place = (step * UNROLL + u) * 2
            one, two = tab[which, place], tab[which, place + 1]
            lhs = jnp.concatenate([source[(one >> 9) & 127], source[(two >> 9) & 127]], axis=1)
            first, second = matrix[one & 511], matrix[two & 511]
            rhs = jnp.concatenate([first, second], axis=0 if transposed else 1)
            dims = (((1,), (0 if transposed else 1,)), ((), ()))
            done.append((one >> 16, lax.dot_general(lhs, rhs, dims, preferred_element_type=jnp.float32)))
        for dest, value in done:
            acc[dest] += value
        return carry

    lax.fori_loop(0, tab[TRIPS, which], body, 0)


def clear(ref):
    def body(b, carry):
        ref[b] = jnp.zeros(ref.shape[1:], ref.dtype)
        return carry

    lax.fori_loop(0, ref.shape[0], body, 0)


def edge_kernel(start, density, head, tail, weights, held, raw, sems):
    size = head.shape[1]
    vectors = start.shape[0]
    edge = head.shape[0] // (vectors + 1)
    width = edge * size
    outs = (head, tail)
    origin = (0, start.shape[1] - width)
    copies = [
        pltpu.make_async_copy(start.at[:, pl.ds(origin[i], width)], held.at[i], sems.at[i]) for i in range(2)
    ]
    copies.append(pltpu.make_async_copy(density, raw, sems.at[2]))
    for copy in copies:
        copy.start()
    copies[2].wait()
    for b in range(weights.shape[0]):
        weights[b : b + 1] = raw[:, b * size : (b + 1) * size].astype(jnp.float32)
    for i in range(2):
        copies[i].wait()
        first = origin[i] // size
        for b in range(edge):
            value = held[i, :, b * size : (b + 1) * size].astype(jnp.float32) * weights[first + b : first + b + 1]
            outs[i][b * vectors : (b + 1) * vectors] = value.astype(jnp.bfloat16)
        outs[i][edge * vectors :] = weights[first : first + edge].astype(jnp.bfloat16)


def first_kernel(count, blocks, start, row, col, turned, weights, matrix, rows, tab, source, held, lists, smem, sems):
    slots = blocks.shape[0]
    part = slots // CHUNKS
    small = [pltpu.make_async_copy(ref, lists.at[i], sems.at[CHUNKS + 1 + i]) for i, ref in enumerate((row, col, turned))]
    copies = small + [pltpu.make_async_copy(start, held, sems.at[CHUNKS])]
    for c in range(CHUNKS):
        here = pl.ds(c * part, part)
        copies.append(pltpu.make_async_copy(blocks.at[here], matrix.at[here], sems.at[c]))
    for copy in copies:
        copy.start()
    num_blocks, vectors = rows.shape[0], start.shape[0]
    size = blocks.shape[-1]
    clear(rows)
    matrix[slots] = jnp.zeros((size, size), matrix.dtype)
    source[num_blocks] = jnp.zeros(source.shape[1:], source.dtype)
    for copy in small:
        copy.wait()
    fill_tables(count[0], count[1], count[2], lists[0], lists[1], lists[2], num_blocks, tab)
    table_copy = pltpu.make_async_copy(tab, smem, sems.at[CHUNKS + 4])
    table_copy.start()
    copies[3].wait()
    top = lax.broadcasted_iota(jnp.int32, (16, size), 0) == 0

    def fill(b, carry):
        cells = pl.ds(pl.multiple_of(b * size, size), size)
        weight = weights[pl.ds(b, 1)]
        source[b, :vectors] = (held[:, cells].astype(jnp.float32) * weight).astype(jnp.bfloat16)
        source[b, vectors:] = jnp.where(top, jnp.broadcast_to(weight, (16, size)), 0.0).astype(jnp.bfloat16)
        return carry

    lax.fori_loop(0, num_blocks, fill, 0, unroll=4)
    across = lax.broadcasted_iota(jnp.int32, (size, size), 0)
    along = lax.broadcasted_iota(jnp.int32, (size, size), 1)
    mirror = (across + along == size - 1).astype(jnp.float32).astype(jnp.bfloat16)
    table_copy.wait()
    for copy in copies[4:]:
        copy.wait()

    def turn(step, carry):
        done = []
        for u in range(TURN):
            slot = smem[FLIPS, step * TURN + u]
            value = jnp.dot(matrix[slot], mirror, preferred_element_type=jnp.float32)
            done.append((slot, value.astype(jnp.bfloat16)))
        for slot, value in done:
            matrix[slot] = value
        return carry

    lax.fori_loop(0, smem[TRIPS, FLIPS], turn, 0)
    pair_loop(FORWARD_OWN, smem, source, matrix, rows)


def own_kernel(tab, matrix, head, middle, tail, rows, source):
    clear(rows)
    num_blocks = rows.shape[0]
    edge = num_blocks // 4
    vectors = rows.shape[1]
    for b in range(edge):
        source[b] = head[b * vectors : (b + 1) * vectors]
        source[num_blocks - edge + b] = tail[b * vectors : (b + 1) * vectors]
    source[edge : num_blocks - edge] = middle[...]
    source[num_blocks] = jnp.zeros(source.shape[1:], source.dtype)
    pair_loop(FORWARD_OWN, tab, source, matrix, rows)


def load_rims(first, rims, source):
    edge = source.shape[0] // 2
    vectors = rims[0].shape[0] // edge - (1 if first else 0)
    size = source.shape[2]
    for side, rim in enumerate(rims):
        for b in range(edge):
            source[side * edge + b, :vectors] = rim[b * vectors : (b + 1) * vectors]
        if first:
            weights = rim[edge * vectors :].astype(jnp.float32)
            top = lax.broadcasted_iota(jnp.int32, (16, size), 0) == 0
            for b in range(edge):
                pad = jnp.where(top, jnp.broadcast_to(weights[b : b + 1], (16, size)), 0.0)
                source[side * edge + b, vectors:] = pad.astype(jnp.bfloat16)
    source[2 * edge] = jnp.zeros(source.shape[1:], source.dtype)


def heads_kernel(first, tab, matrix, rows_in, right, lower, rows, source):
    del rows_in
    load_rims(first, (right, lower), source)
    pair_loop(FORWARD_HEADS, tab, source, matrix, rows)


def send_back(total, backs):
    vectors = total.shape[1]
    edge = total.shape[0] // 2
    for side in range(2):
        for b in range(edge):
            backs[side][b * vectors : (b + 1) * vectors] = total[side * edge + b].astype(jnp.bfloat16)


def middle_kernel(first, tab, matrix, rows_in, left, upper, *rest):
    del rows_in
    if first:
        rows, image, inverse = rest[:3]
    else:
        inverse, rows, image = rest[:3]
    right_back, lower_back, source, total = rest[3:]
    num_blocks = rows.shape[0]
    vectors = image.shape[1]
    load_rims(first, (left, upper), source)
    clear(total)
    pair_loop(FORWARD_TAILS, tab, source, matrix, rows)

    def divide(b, carry):
        if first:
            factor = 1.0 / rows[b, vectors : vectors + 8]
            inverse[b] = factor
        else:
            factor = inverse[b]
        image[b] = (rows[b, :vectors] * factor[:1]).astype(jnp.bfloat16)
        return carry

    lax.fori_loop(0, num_blocks, divide, 0, unroll=4)
    image[num_blocks] = jnp.zeros(image.shape[1:], image.dtype)
    pair_loop(ADJOINT_HEADS, tab, image, matrix, total)
    send_back(total, (right_back, lower_back))


def tails_kernel(tab, matrix, image, left_back, upper_back, total):
    clear(total)
    pair_loop(ADJOINT_TAILS, tab, image, matrix, total)
    send_back(total, (left_back, upper_back))


def adjoint_kernel(tab, matrix, image, weights, total, norm, *rest):
    clear(total)
    pair_loop(ADJOINT_OWN, tab, image, matrix, total)
    num_blocks = total.shape[0]
    edge = num_blocks // 4

    def inside(b, sums):
        value = total[b]
        weighted = value * weights[pl.ds(b, 1)]
        if rest:
            rest[0][b - edge] = weighted.astype(jnp.bfloat16)
        return sums + weighted * value

    zero = jnp.zeros(norm.shape, jnp.float32)
    norm[...] = lax.fori_loop(edge, num_blocks - edge, inside, zero)


def add_edge(total, weights, from_block, one, two, sums, store):
    vectors = total.shape[1]

    def add(b, carry):
        rows = pl.ds(pl.multiple_of(b * vectors, vectors), vectors)
        value = total[from_block + b] + (one[rows].astype(jnp.float32) + two[rows].astype(jnp.float32))
        weighted = value * weights[pl.ds(from_block + b, 1)]
        store(b, rows, value, weighted)
        return carry + weighted * value

    return lax.fori_loop(0, total.shape[0] // 4, add, sums, unroll=2)


def join_kernel(tail, total, weights, one, two, norm_in, out, norm):
    def store(b, rows, value, weighted):
        out[rows] = weighted.astype(jnp.bfloat16)

    from_block = total.shape[0] // 4 * 3 if tail else 0
    norm[...] = add_edge(total, weights, from_block, one, two, norm_in[...], store)


def sum_kernel(total_in, weights, low0, low1, high0, high1, norm_in, norm_first, total, message):
    del total_in
    sums = norm_in[...]
    size = total.shape[2]
    for from_block, one, two in ((0, low0, low1), (total.shape[0] // 4 * 3, high0, high1)):

        def store(b, rows, value, weighted, from_block=from_block):
            total[from_block + b] = value

        sums = add_edge(total, weights, from_block, one, two, sums, store)
    ones = jnp.ones((8, size), jnp.float32)
    both = [
        lax.dot_general(
            ones, part, (((1,), (1,)), ((), ())), precision=lax.Precision.HIGHEST, preferred_element_type=jnp.float32
        )
        for part in (norm_first[...], sums)
    ]
    message[...] = jnp.broadcast_to(jnp.concatenate(both, axis=1)[:1], message.shape)


def final_kernel(total_cells, sums, total, out):
    num_blocks, vectors, size = total.shape
    both = jnp.sum(sums[...], axis=0, keepdims=True) * (1.0 / total_cells)
    diagonal = lax.broadcasted_iota(jnp.int32, (vectors, size), 0)
    lane = lax.broadcasted_iota(jnp.int32, (vectors, size), 1)
    both = jnp.broadcast_to(both, (vectors, size))
    first = jnp.sum(jnp.where(lane == diagonal, both, 0.0), axis=1, keepdims=True)
    second = jnp.sum(jnp.where(lane == diagonal + vectors, both, 0.0), axis=1, keepdims=True)
    factor = lax.rsqrt(first + 1e-06)
    scale = jnp.broadcast_to(factor * lax.rsqrt(factor * factor * second + 1e-06), (vectors, size))

    def body(b, carry):
        cells = pl.ds(pl.multiple_of(b * size, size), size)
        out[:, cells] = (total[b] * scale).astype(jnp.bfloat16)
        return carry

    lax.fori_loop(0, num_blocks, body, 0, unroll=4)


def shift(x, axis, step):
    count = lax.axis_size(axis)
    return lax.ppermute(x, axis, [(i, (i + step) % count) for i in range(count)])


def heads_out(head):
    return shift(head, "tile", -1), shift(head, "layer", -1)


def tails_out(tail):
    return shift(tail, "tile", 1), shift(tail, "layer", 1)


def call(kernel, name, outs, in_specs, scratch, flops, nbytes, aliases={}):
    return pl.pallas_call(
        kernel,
        name=name,
        out_shape=outs,
        in_specs=in_specs,
        out_specs=[VMEM_SPEC] * len(outs),
        scratch_shapes=scratch,
        input_output_aliases=aliases,
        compiler_params=pltpu.CompilerParams(vmem_limit_bytes=16 * 1024 * 1024),
        cost_estimate=pl.CostEstimate(flops=flops, bytes_accessed=nbytes, transcendentals=0),
    )


def local(blocks, slot_rows, slot_cols, rotation, live_block_count, density, start):
    bf16, f32 = jnp.bfloat16, jnp.float32
    blocks, start = blocks[0, 0], start[0, 0]
    slots, size = blocks.shape[0], blocks.shape[2]
    vectors, cells = start.shape
    num_blocks = cells // size
    edge = num_blocks // 4
    devices = lax.axis_size("layer") * lax.axis_size("tile")
    total_cells = cells * devices
    work = slots * size * size * vectors
    tall = vectors + 16
    rim_type = VM((edge * vectors, size), bf16)
    first_rim_type = VM((edge * (vectors + 1), size), bf16)
    block_f32 = VM((num_blocks, vectors, size), f32)
    tall_f32 = VM((num_blocks, tall, size), f32)
    image_type = VM((num_blocks + 1, vectors, size), bf16)
    middle_type = VM((num_blocks - 2 * edge, vectors, size), bf16)
    norm_type = VM((vectors, size), f32)

    def outside(x):
        return pltpu.with_memory_space_constraint(x, pltpu.HBM)

    start = outside(start)
    head, tail, weights = call(
        edge_kernel,
        "edges",
        [first_rim_type, first_rim_type, VM((num_blocks, size), f32)],
        [HBM_SPEC, HBM_SPEC],
        [
            VM((2, vectors, edge * size), bf16),
            VM((1, cells), bf16),
            pltpu.SemaphoreType.DMA((3,)),
        ],
        0,
        start.size,
    )(start, outside(density[0]))
    heads, tails = heads_out(head), tails_out(tail)

    layer = lax.axis_index("layer")
    above, beneath = layer > 0, layer < lax.axis_size("layer") - 1
    facts = jnp.stack([live_block_count[0, 0], above.astype(jnp.int32), beneath.astype(jnp.int32)])
    places = 2 * ((slots + num_blocks) // 2)
    matrix, rows, tab = call(
        first_kernel,
        "own_first",
        [VM((slots + 1, size, size), bf16), tall_f32, VM((8, places), jnp.int32)],
        [SMEM_SPEC] + [HBM_SPEC] * 5 + [VMEM_SPEC],
        [
            VM((num_blocks + 1, tall, size), bf16),
            VM((vectors, cells), bf16),
            VM((3, 1, slots), jnp.int32),
            pltpu.SMEM((8, places), jnp.int32),
            pltpu.SemaphoreType.DMA((CHUNKS + 5,)),
        ],
        2 * work,
        2 * blocks.size * 2,
    )(
        facts,
        outside(blocks),
        start,
        outside(slot_rows[0]),
        outside(slot_cols[0]),
        outside(rotation[0]),
        weights,
    )

    inverse = None
    for turn in range(2):
        first = turn == 0
        rows_type = tall_f32 if first else block_f32
        source_type = VM((2 * edge + 1, tall if first else vectors, size), bf16)
        half_f32 = VM((2 * edge, vectors, size), f32)
        suffix = "_first" if first else "_next"
        if not first:
            (rows,) = call(
                own_kernel,
                "own_next",
                [block_f32],
                [SMEM_SPEC] + [VMEM_SPEC] * 4,
                [VM((num_blocks + 1, vectors, size), bf16)],
                work,
                blocks.size,
            )(tab, matrix, head, middle, tail)
        (rows,) = call(
            functools.partial(heads_kernel, first),
            "heads" + suffix,
            [rows_type],
            [SMEM_SPEC] + [VMEM_SPEC] * 4,
            [source_type],
            work // 2,
            blocks.size // 2,
            {2: 0},
        )(tab, matrix, rows, *heads)
        extra = [] if first else [inverse]
        result = call(
            functools.partial(middle_kernel, first),
            "middle" + suffix,
            [rows_type, image_type] + ([VM((num_blocks, 8, size), f32)] if first else []) + [rim_type] * 2,
            [SMEM_SPEC] + [VMEM_SPEC] * (4 + len(extra)),
            [source_type, half_f32],
            work,
            blocks.size,
            {2: 0},
        )(tab, matrix, rows, *tails, *extra)
        image = result[1]
        if first:
            inverse = result[2]
        right, lower = result[-2:]
        lows = (shift(right, "tile", 1), shift(lower, "layer", 1))
        left, upper = call(
            tails_kernel,
            "tails" + suffix,
            [rim_type] * 2,
            [SMEM_SPEC] + [VMEM_SPEC] * 2,
            [half_f32],
            work // 2,
            blocks.size // 2,
        )(tab, matrix, image)
        highs = (shift(left, "tile", -1), shift(upper, "layer", -1))
        result = call(
            adjoint_kernel,
            "adjoint" + suffix,
            [block_f32, norm_type] + ([middle_type] if first else []),
            [SMEM_SPEC] + [VMEM_SPEC] * 3,
            [],
            work,
            blocks.size,
        )(tab, matrix, image, weights)
        total, norm = result[:2]
        if first:
            middle = result[2]
            head, norm = call(
                functools.partial(join_kernel, False),
                "join_head",
                [rim_type, norm_type],
                [VMEM_SPEC] * 5,
                [],
                0,
                edge * vectors * size * 8,
            )(total, weights, *lows, norm)
            heads = heads_out(head)
            tail, norm_first = call(
                functools.partial(join_kernel, True),
                "join_tail",
                [rim_type, norm_type],
                [VMEM_SPEC] * 5,
                [],
                0,
                edge * vectors * size * 8,
            )(total, weights, *highs, norm)
            tails = tails_out(tail)
    total, message = call(
        sum_kernel,
        "join_last",
        [block_f32, VM((devices, 2 * vectors), f32)],
        [VMEM_SPEC] * 8,
        [],
        0,
        2 * edge * vectors * size * 8,
        {0: 0},
    )(total, weights, *lows, *highs, norm, norm_first)
    sums = lax.all_to_all(message, ("layer", "tile"), 0, 0, tiled=True)
    out = call(
        functools.partial(final_kernel, total_cells),
        "write_out",
        [jax.ShapeDtypeStruct((vectors, cells), bf16)],
        [VMEM_SPEC] * 2,
        [],
        0,
        cells * vectors * 6,
    )(sums, total)[0]
    return out[None, None]


def solution(mesh):
    in_specs = (
        P("layer", "tile", None, None, None),
        P("layer", "tile", None),
        P("layer", "tile", None),
        P("layer", "tile", None),
        P("layer", "tile"),
        P("layer", "tile", None),
        P("layer", "tile", None, None),
    )
    out_specs = P("layer", "tile", None, None)
    return jax.shard_map(local, mesh=mesh, in_specs=in_specs, out_specs=out_specs, check_vma=False)
```

```python
import functools

import jax
import jax.numpy as jnp
from jax import lax
from jax.experimental import pallas as pl
from jax.experimental.pallas import tpu as pltpu
from jax.sharding import PartitionSpec as P

UNROLL = 16
HALF = UNROLL // 2
TURN = 16
CHUNKS = 8
VM = pltpu.VMEM
VMEM_SPEC = pl.BlockSpec(memory_space=pltpu.VMEM)
SMEM_SPEC = pl.BlockSpec(memory_space=pltpu.SMEM)
HBM_SPEC = pl.BlockSpec(memory_space=pltpu.HBM)
FORWARD_OWN, FORWARD_HEADS, FORWARD_TAILS, ADJOINT_OWN, ADJOINT_HEADS, ADJOINT_TAILS, FLIPS, TRIPS = range(8)


def fill_tables(live_count, above, beneath, row, col, turned, num_blocks, tab):
    f32, bf16 = jnp.float32, jnp.bfloat16
    slots = row.shape[1]
    places = tab.shape[1]
    index = lax.broadcasted_iota(jnp.int32, (1, slots), 1)
    live = index < live_count
    edge = num_blocks // 4
    outer = col - num_blocks
    side = outer // edge
    live = live & ((side != 2) | (above == 1)) & ((side != 3) | (beneath == 1))
    own = outer < 0
    heads = (outer >= 0) & ((side & 1) == 1)
    tails = (outer >= 0) & ((side & 1) == 0)
    source = jnp.where(own, col, (side >> 1) * edge + outer - side * edge)
    key = lax.broadcasted_iota(jnp.int32, (num_blocks, slots), 0)
    spot = lax.broadcasted_iota(jnp.int32, (128, slots), 0)
    earlier = (
        lax.broadcasted_iota(jnp.int32, (slots, slots), 0) < lax.broadcasted_iota(jnp.int32, (slots, slots), 1)
    ).astype(f32).astype(bf16)
    below = (
        lax.broadcasted_iota(jnp.int32, (num_blocks, num_blocks), 1)
        < lax.broadcasted_iota(jnp.int32, (num_blocks, num_blocks), 0)
    ).astype(f32).astype(bf16)
    lane = lax.broadcasted_iota(jnp.int32, (1, places), 1)
    meta = jnp.zeros((1, places), jnp.int32)

    def invert(position, parts):
        found = (spot == (position & 127)).astype(f32).astype(bf16)
        chunks = places // 128
        rows = [jnp.where((position >> 7) == c, p, 0) for p in parts for c in range(chunks)]
        rows = rows + [jnp.zeros((1, slots), jnp.int32)] * (-len(rows) % 16)
        values = jnp.concatenate([r.astype(f32) for r in rows], axis=0).astype(bf16)
        moved = lax.dot_general(values, found, (((1,), (1,)), ((), ())), preferred_element_type=f32)
        moved = moved.astype(jnp.int32)
        return [
            jnp.concatenate([moved[i * chunks + c : i * chunks + c + 1] for c in range(chunks)], axis=1)
            for i in range(len(parts))
        ]

    parts = ((own, num_blocks), (heads, 2 * edge), (tails, 2 * edge))
    cases = []
    for which in range(6):
        chosen, empty = parts[which % 3]
        dest, operand = row, source
        if which >= ADJOINT_OWN:
            dest, operand, empty = source, row, num_blocks
        used = live & chosen
        cases.append((dest, operand, empty, used, (key == jnp.where(used, dest, -1)).astype(f32)))
    flip = live & (turned == 1)
    ones = jnp.broadcast_to(flip.astype(f32), (16, slots))
    members = jnp.concatenate([case[4].astype(bf16) for case in cases] + [ones.astype(bf16)], axis=0)
    ranks = jnp.dot(members, earlier, preferred_element_type=f32)
    for which, (dest, operand, empty, used, member) in enumerate(cases):
        before = ranks[which * num_blocks : (which + 1) * num_blocks]
        pairs = (jnp.sum(member, axis=1, keepdims=True).astype(jnp.int32) + 1) >> 1
        wide = jnp.broadcast_to(pairs.astype(f32), (num_blocks, 128)).astype(bf16)
        offset = jnp.dot(below, wide, preferred_element_type=f32)[:, :1]
        position = jnp.sum(member * (before + 2.0 * offset), axis=0, keepdims=True).astype(jnp.int32)
        position = jnp.where(used, position, -1)
        low, high, move, to = invert(position, [index & 255, index >> 8, operand - empty, dest])
        tab[which : which + 1] = low + (high << 8) + ((move + empty) << 9) + (to << 16)
        count = jnp.sum(pairs.astype(f32), axis=0, keepdims=True).astype(jnp.int32)
        meta = meta + jnp.where(lane == which, (count + (HALF - 1)) // HALF, 0)
    rank = jnp.where(flip, ranks[6 * num_blocks : 6 * num_blocks + 1].astype(jnp.int32), -1)
    low, high, hit = invert(rank, [index & 255, index >> 8, flip.astype(jnp.int32)])
    tab[FLIPS : FLIPS + 1] = jnp.where(hit == 1, low + (high << 8), slots)
    count = jnp.sum(ones[:1], axis=1, keepdims=True).astype(jnp.int32)
    meta = meta + jnp.where(lane == FLIPS, (count + (TURN - 1)) // TURN, 0)
    tab[TRIPS : TRIPS + 1] = meta


def pair_loop(which, tab, source, matrix, acc):
    transposed = which >= ADJOINT_OWN

    def add(start, count):
        done = []
        for u in range(count):
            place = (start + u) * 2
            one, two = tab[which, place], tab[which, place + 1]
            lhs = jnp.concatenate([source[(one >> 9) & 127], source[(two >> 9) & 127]], axis=1)
            first, second = matrix[one & 511], matrix[two & 511]
            rhs = jnp.concatenate([first, second], axis=0 if transposed else 1)
            dims = (((1,), (0 if transposed else 1,)), ((), ()))
            done.append((one >> 16, lax.dot_general(lhs, rhs, dims, preferred_element_type=jnp.float32)))
        for dest, value in done:
            acc[dest] += value

    halves = tab[TRIPS, which]

    def body(step, carry):
        add(step * UNROLL, UNROLL)
        return carry

    lax.fori_loop(0, halves >> 1, body, 0)

    @pl.when((halves & 1) == 1)
    def _():
        add((halves - 1) * HALF, HALF)


def clear(ref):
    def body(b, carry):
        ref[b] = jnp.zeros(ref.shape[1:], ref.dtype)
        return carry

    lax.fori_loop(0, ref.shape[0], body, 0)


def edge_kernel(start, density, head, tail, weights, held, raw, sems):
    size = head.shape[1]
    vectors = start.shape[0]
    edge = head.shape[0] // (vectors + 1)
    width = edge * size
    outs = (head, tail)
    origin = (0, start.shape[1] - width)
    copies = [
        pltpu.make_async_copy(start.at[:, pl.ds(origin[i], width)], held.at[i], sems.at[i]) for i in range(2)
    ]
    copies.append(pltpu.make_async_copy(density, raw, sems.at[2]))
    for copy in copies:
        copy.start()
    copies[2].wait()
    for b in range(weights.shape[0]):
        weights[b : b + 1] = raw[:, b * size : (b + 1) * size].astype(jnp.float32)
    for i in range(2):
        copies[i].wait()
        first = origin[i] // size
        for b in range(edge):
            value = held[i, :, b * size : (b + 1) * size].astype(jnp.float32) * weights[first + b : first + b + 1]
            outs[i][b * vectors : (b + 1) * vectors] = value.astype(jnp.bfloat16)
        outs[i][edge * vectors :] = weights[first : first + edge].astype(jnp.bfloat16)


def first_kernel(count, blocks, start, row, col, turned, weights, matrix, rows, tab, source, held, lists, smem, sems):
    slots = blocks.shape[0]
    part = slots // CHUNKS
    small = [pltpu.make_async_copy(ref, lists.at[i], sems.at[CHUNKS + 1 + i]) for i, ref in enumerate((row, col, turned))]
    copies = small + [pltpu.make_async_copy(start, held, sems.at[CHUNKS])]
    for c in range(CHUNKS):
        here = pl.ds(c * part, part)
        copies.append(pltpu.make_async_copy(blocks.at[here], matrix.at[here], sems.at[c]))
    for copy in copies:
        copy.start()
    num_blocks, vectors = rows.shape[0], start.shape[0]
    size = blocks.shape[-1]
    clear(rows)
    matrix[slots] = jnp.zeros((size, size), matrix.dtype)
    source[num_blocks] = jnp.zeros(source.shape[1:], source.dtype)
    for copy in small:
        copy.wait()
    fill_tables(count[0], count[1], count[2], lists[0], lists[1], lists[2], num_blocks, tab)
    table_copy = pltpu.make_async_copy(tab, smem, sems.at[CHUNKS + 4])
    table_copy.start()
    copies[3].wait()
    top = lax.broadcasted_iota(jnp.int32, (16, size), 0) == 0

    def fill(b, carry):
        cells = pl.ds(pl.multiple_of(b * size, size), size)
        weight = weights[pl.ds(b, 1)]
        source[b, :vectors] = (held[:, cells].astype(jnp.float32) * weight).astype(jnp.bfloat16)
        source[b, vectors:] = jnp.where(top, jnp.broadcast_to(weight, (16, size)), 0.0).astype(jnp.bfloat16)
        return carry

    lax.fori_loop(0, num_blocks, fill, 0, unroll=4)
    across = lax.broadcasted_iota(jnp.int32, (size, size), 0)
    along = lax.broadcasted_iota(jnp.int32, (size, size), 1)
    mirror = (across + along == size - 1).astype(jnp.float32).astype(jnp.bfloat16)
    table_copy.wait()
    for copy in copies[4:]:
        copy.wait()

    def turn(step, carry):
        done = []
        for u in range(TURN):
            slot = smem[FLIPS, step * TURN + u]
            value = jnp.dot(matrix[slot], mirror, preferred_element_type=jnp.float32)
            done.append((slot, value.astype(jnp.bfloat16)))
        for slot, value in done:
            matrix[slot] = value
        return carry

    lax.fori_loop(0, smem[TRIPS, FLIPS], turn, 0)
    pair_loop(FORWARD_OWN, smem, source, matrix, rows)


def own_kernel(tab, matrix, head, middle, tail, rows, source):
    clear(rows)
    num_blocks = rows.shape[0]
    edge = num_blocks // 4
    vectors = rows.shape[1]
    for b in range(edge):
        source[b] = head[b * vectors : (b + 1) * vectors]
        source[num_blocks - edge + b] = tail[b * vectors : (b + 1) * vectors]
    source[edge : num_blocks - edge] = middle[...]
    source[num_blocks] = jnp.zeros(source.shape[1:], source.dtype)
    pair_loop(FORWARD_OWN, tab, source, matrix, rows)


def load_rims(first, rims, source):
    edge = source.shape[0] // 2
    vectors = rims[0].shape[0] // edge - (1 if first else 0)
    size = source.shape[2]
    for side, rim in enumerate(rims):
        for b in range(edge):
            source[side * edge + b, :vectors] = rim[b * vectors : (b + 1) * vectors]
        if first:
            weights = rim[edge * vectors :].astype(jnp.float32)
            top = lax.broadcasted_iota(jnp.int32, (16, size), 0) == 0
            for b in range(edge):
                pad = jnp.where(top, jnp.broadcast_to(weights[b : b + 1], (16, size)), 0.0)
                source[side * edge + b, vectors:] = pad.astype(jnp.bfloat16)
    source[2 * edge] = jnp.zeros(source.shape[1:], source.dtype)


def heads_kernel(first, tab, matrix, rows_in, right, lower, rows, source):
    del rows_in
    load_rims(first, (right, lower), source)
    pair_loop(FORWARD_HEADS, tab, source, matrix, rows)


def send_back(total, backs):
    vectors = total.shape[1]
    edge = total.shape[0] // 2
    for side in range(2):
        for b in range(edge):
            backs[side][b * vectors : (b + 1) * vectors] = total[side * edge + b].astype(jnp.bfloat16)


def middle_kernel(first, tab, matrix, rows_in, left, upper, *rest):
    del rows_in
    if first:
        rows, image, inverse = rest[:3]
    else:
        inverse, rows, image = rest[:3]
    right_back, lower_back, source, total = rest[3:]
    num_blocks = rows.shape[0]
    vectors = image.shape[1]
    load_rims(first, (left, upper), source)
    clear(total)
    pair_loop(FORWARD_TAILS, tab, source, matrix, rows)

    def divide(b, carry):
        if first:
            factor = 1.0 / rows[b, vectors : vectors + 8]
            inverse[b] = factor
        else:
            factor = inverse[b]
        image[b] = (rows[b, :vectors] * factor[:1]).astype(jnp.bfloat16)
        return carry

    lax.fori_loop(0, num_blocks, divide, 0, unroll=4)
    image[num_blocks] = jnp.zeros(image.shape[1:], image.dtype)
    pair_loop(ADJOINT_HEADS, tab, image, matrix, total)
    send_back(total, (right_back, lower_back))


def tails_kernel(tab, matrix, image, left_back, upper_back, total):
    clear(total)
    pair_loop(ADJOINT_TAILS, tab, image, matrix, total)
    send_back(total, (left_back, upper_back))


def adjoint_kernel(tab, matrix, image, weights, total, norm, *rest):
    clear(total)
    pair_loop(ADJOINT_OWN, tab, image, matrix, total)
    num_blocks = total.shape[0]
    edge = num_blocks // 4

    def inside(b, sums):
        value = total[b]
        weighted = value * weights[pl.ds(b, 1)]
        if rest:
            rest[0][b - edge] = weighted.astype(jnp.bfloat16)
        return sums + weighted * value

    zero = jnp.zeros(norm.shape, jnp.float32)
    norm[...] = lax.fori_loop(edge, num_blocks - edge, inside, zero)


def add_edge(total, weights, from_block, one, two, sums, store):
    vectors = total.shape[1]

    def add(b, carry):
        rows = pl.ds(pl.multiple_of(b * vectors, vectors), vectors)
        value = total[from_block + b] + (one[rows].astype(jnp.float32) + two[rows].astype(jnp.float32))
        weighted = value * weights[pl.ds(from_block + b, 1)]
        store(b, rows, value, weighted)
        return carry + weighted * value

    return lax.fori_loop(0, total.shape[0] // 4, add, sums, unroll=2)


def join_kernel(tail, total, weights, one, two, norm_in, out, norm):
    def store(b, rows, value, weighted):
        out[rows] = weighted.astype(jnp.bfloat16)

    from_block = total.shape[0] // 4 * 3 if tail else 0
    norm[...] = add_edge(total, weights, from_block, one, two, norm_in[...], store)


def sum_kernel(total_in, weights, low0, low1, high0, high1, norm_in, norm_first, total, message):
    del total_in
    sums = norm_in[...]
    size = total.shape[2]
    for from_block, one, two in ((0, low0, low1), (total.shape[0] // 4 * 3, high0, high1)):

        def store(b, rows, value, weighted, from_block=from_block):
            total[from_block + b] = value

        sums = add_edge(total, weights, from_block, one, two, sums, store)
    ones = jnp.ones((8, size), jnp.float32)
    both = [
        lax.dot_general(
            ones, part, (((1,), (1,)), ((), ())), precision=lax.Precision.HIGHEST, preferred_element_type=jnp.float32
        )
        for part in (norm_first[...], sums)
    ]
    message[...] = jnp.broadcast_to(jnp.concatenate(both, axis=1)[:1], message.shape)


def final_kernel(total_cells, sums, total, out):
    num_blocks, vectors, size = total.shape
    both = jnp.sum(sums[...], axis=0, keepdims=True) * (1.0 / total_cells)
    diagonal = lax.broadcasted_iota(jnp.int32, (vectors, size), 0)
    lane = lax.broadcasted_iota(jnp.int32, (vectors, size), 1)
    both = jnp.broadcast_to(both, (vectors, size))
    first = jnp.sum(jnp.where(lane == diagonal, both, 0.0), axis=1, keepdims=True)
    second = jnp.sum(jnp.where(lane == diagonal + vectors, both, 0.0), axis=1, keepdims=True)
    factor = lax.rsqrt(first + 1e-06)
    scale = jnp.broadcast_to(factor * lax.rsqrt(factor * factor * second + 1e-06), (vectors, size))

    def body(b, carry):
        cells = pl.ds(pl.multiple_of(b * size, size), size)
        out[:, cells] = (total[b] * scale).astype(jnp.bfloat16)
        return carry

    lax.fori_loop(0, num_blocks, body, 0, unroll=4)


def shift(x, axis, step):
    count = lax.axis_size(axis)
    return lax.ppermute(x, axis, [(i, (i + step) % count) for i in range(count)])


def heads_out(head):
    return shift(head, "tile", -1), shift(head, "layer", -1)


def tails_out(tail):
    return shift(tail, "tile", 1), shift(tail, "layer", 1)


def call(kernel, name, outs, in_specs, scratch, flops, nbytes, aliases={}):
    return pl.pallas_call(
        kernel,
        name=name,
        out_shape=outs,
        in_specs=in_specs,
        out_specs=[VMEM_SPEC] * len(outs),
        scratch_shapes=scratch,
        input_output_aliases=aliases,
        compiler_params=pltpu.CompilerParams(vmem_limit_bytes=16 * 1024 * 1024),
        cost_estimate=pl.CostEstimate(flops=flops, bytes_accessed=nbytes, transcendentals=0),
    )


def local(blocks, slot_rows, slot_cols, rotation, live_block_count, density, start):
    bf16, f32 = jnp.bfloat16, jnp.float32
    blocks, start = blocks[0, 0], start[0, 0]
    slots, size = blocks.shape[0], blocks.shape[2]
    vectors, cells = start.shape
    num_blocks = cells // size
    edge = num_blocks // 4
    devices = lax.axis_size("layer") * lax.axis_size("tile")
    total_cells = cells * devices
    work = slots * size * size * vectors
    tall = vectors + 16
    rim_type = VM((edge * vectors, size), bf16)
    first_rim_type = VM((edge * (vectors + 1), size), bf16)
    block_f32 = VM((num_blocks, vectors, size), f32)
    tall_f32 = VM((num_blocks, tall, size), f32)
    image_type = VM((num_blocks + 1, vectors, size), bf16)
    middle_type = VM((num_blocks - 2 * edge, vectors, size), bf16)
    norm_type = VM((vectors, size), f32)

    def outside(x):
        return pltpu.with_memory_space_constraint(x, pltpu.HBM)

    start = outside(start)
    head, tail, weights = call(
        edge_kernel,
        "edges",
        [first_rim_type, first_rim_type, VM((num_blocks, size), f32)],
        [HBM_SPEC, HBM_SPEC],
        [
            VM((2, vectors, edge * size), bf16),
            VM((1, cells), bf16),
            pltpu.SemaphoreType.DMA((3,)),
        ],
        0,
        start.size,
    )(start, outside(density[0]))
    heads, tails = heads_out(head), tails_out(tail)

    layer = lax.axis_index("layer")
    above, beneath = layer > 0, layer < lax.axis_size("layer") - 1
    facts = jnp.stack([live_block_count[0, 0], above.astype(jnp.int32), beneath.astype(jnp.int32)])
    places = 2 * ((slots + num_blocks) // 2)
    matrix, rows, tab = call(
        first_kernel,
        "own_first",
        [VM((slots + 1, size, size), bf16), tall_f32, VM((8, places), jnp.int32)],
        [SMEM_SPEC] + [HBM_SPEC] * 5 + [VMEM_SPEC],
        [
            VM((num_blocks + 1, tall, size), bf16),
            VM((vectors, cells), bf16),
            VM((3, 1, slots), jnp.int32),
            pltpu.SMEM((8, places), jnp.int32),
            pltpu.SemaphoreType.DMA((CHUNKS + 5,)),
        ],
        2 * work,
        2 * blocks.size * 2,
    )(
        facts,
        outside(blocks),
        start,
        outside(slot_rows[0]),
        outside(slot_cols[0]),
        outside(rotation[0]),
        weights,
    )

    inverse = None
    for turn in range(2):
        first = turn == 0
        rows_type = tall_f32 if first else block_f32
        source_type = VM((2 * edge + 1, tall if first else vectors, size), bf16)
        half_f32 = VM((2 * edge, vectors, size), f32)
        suffix = "_first" if first else "_next"
        if not first:
            (rows,) = call(
                own_kernel,
                "own_next",
                [block_f32],
                [SMEM_SPEC] + [VMEM_SPEC] * 4,
                [VM((num_blocks + 1, vectors, size), bf16)],
                work,
                blocks.size,
            )(tab, matrix, head, middle, tail)
        (rows,) = call(
            functools.partial(heads_kernel, first),
            "heads" + suffix,
            [rows_type],
            [SMEM_SPEC] + [VMEM_SPEC] * 4,
            [source_type],
            work // 2,
            blocks.size // 2,
            {2: 0},
        )(tab, matrix, rows, *heads)
        extra = [] if first else [inverse]
        result = call(
            functools.partial(middle_kernel, first),
            "middle" + suffix,
            [rows_type, image_type] + ([VM((num_blocks, 8, size), f32)] if first else []) + [rim_type] * 2,
            [SMEM_SPEC] + [VMEM_SPEC] * (4 + len(extra)),
            [source_type, half_f32],
            work,
            blocks.size,
            {2: 0},
        )(tab, matrix, rows, *tails, *extra)
        image = result[1]
        if first:
            inverse = result[2]
        right, lower = result[-2:]
        lows = (shift(right, "tile", 1), shift(lower, "layer", 1))
        left, upper = call(
            tails_kernel,
            "tails" + suffix,
            [rim_type] * 2,
            [SMEM_SPEC] + [VMEM_SPEC] * 2,
            [half_f32],
            work // 2,
            blocks.size // 2,
        )(tab, matrix, image)
        highs = (shift(left, "tile", -1), shift(upper, "layer", -1))
        result = call(
            adjoint_kernel,
            "adjoint" + suffix,
            [block_f32, norm_type] + ([middle_type] if first else []),
            [SMEM_SPEC] + [VMEM_SPEC] * 3,
            [],
            work,
            blocks.size,
        )(tab, matrix, image, weights)
        total, norm = result[:2]
        if first:
            middle = result[2]
            head, norm = call(
                functools.partial(join_kernel, False),
                "join_head",
                [rim_type, norm_type],
                [VMEM_SPEC] * 5,
                [],
                0,
                edge * vectors * size * 8,
            )(total, weights, *lows, norm)
            heads = heads_out(head)
            tail, norm_first = call(
                functools.partial(join_kernel, True),
                "join_tail",
                [rim_type, norm_type],
                [VMEM_SPEC] * 5,
                [],
                0,
                edge * vectors * size * 8,
            )(total, weights, *highs, norm)
            tails = tails_out(tail)
    total, message = call(
        sum_kernel,
        "join_last",
        [block_f32, VM((devices, 2 * vectors), f32)],
        [VMEM_SPEC] * 8,
        [],
        0,
        2 * edge * vectors * size * 8,
        {0: 0},
    )(total, weights, *lows, *highs, norm, norm_first)
    sums = lax.all_to_all(message, ("layer", "tile"), 0, 0, tiled=True)
    out = call(
        functools.partial(final_kernel, total_cells),
        "write_out",
        [jax.ShapeDtypeStruct((vectors, cells), bf16)],
        [VMEM_SPEC] * 2,
        [],
        0,
        cells * vectors * 6,
    )(sums, total)[0]
    return out[None, None]


def solution(mesh):
    in_specs = (
        P("layer", "tile", None, None, None),
        P("layer", "tile", None),
        P("layer", "tile", None),
        P("layer", "tile", None),
        P("layer", "tile"),
        P("layer", "tile", None),
        P("layer", "tile", None, None),
    )
    out_specs = P("layer", "tile", None, None)
    return jax.shard_map(local, mesh=mesh, in_specs=in_specs, out_specs=out_specs, check_vma=False)
```

```python
import functools

import jax
import jax.numpy as jnp
from jax import lax
from jax.experimental import pallas as pl
from jax.experimental.pallas import tpu as pltpu
from jax.sharding import PartitionSpec as P

UNROLL = 16
HALF = UNROLL // 2
TURN = 16
CHUNKS = 8
VM = pltpu.VMEM
VMEM_SPEC = pl.BlockSpec(memory_space=pltpu.VMEM)
SMEM_SPEC = pl.BlockSpec(memory_space=pltpu.SMEM)
HBM_SPEC = pl.BlockSpec(memory_space=pltpu.HBM)
INNER, OUTER, FORWARD_HEADS, FORWARD_TAILS, ADJOINT_OWN, ADJOINT_HEADS, ADJOINT_TAILS, FLIPS = range(8)


def fill_tables(live_count, above, beneath, row, col, turned, num_blocks, tab):
    f32, bf16 = jnp.float32, jnp.bfloat16
    slots = row.shape[1]
    places = tab.shape[1]
    index = lax.broadcasted_iota(jnp.int32, (1, slots), 1)
    live = index < live_count
    edge = num_blocks // 4
    outer = col - num_blocks
    side = outer // edge
    live = live & ((side != 2) | (above == 1)) & ((side != 3) | (beneath == 1))
    own = outer < 0
    heads = (outer >= 0) & ((side & 1) == 1)
    tails = (outer >= 0) & ((side & 1) == 0)
    source = jnp.where(own, col, (side >> 1) * edge + outer - side * edge)
    key = lax.broadcasted_iota(jnp.int32, (num_blocks, slots), 0)
    spot = lax.broadcasted_iota(jnp.int32, (128, slots), 0)
    earlier = (
        lax.broadcasted_iota(jnp.int32, (slots, slots), 0) < lax.broadcasted_iota(jnp.int32, (slots, slots), 1)
    ).astype(f32).astype(bf16)
    below = (
        lax.broadcasted_iota(jnp.int32, (num_blocks, num_blocks), 1)
        < lax.broadcasted_iota(jnp.int32, (num_blocks, num_blocks), 0)
    ).astype(f32).astype(bf16)
    lane = lax.broadcasted_iota(jnp.int32, (1, places), 1)
    meta = jnp.zeros((1, places), jnp.int32)

    def invert(position, parts):
        found = (spot == (position & 127)).astype(f32).astype(bf16)
        chunks = places // 128
        rows = [jnp.where((position >> 7) == c, p, 0) for p in parts for c in range(chunks)]
        rows = rows + [jnp.zeros((1, slots), jnp.int32)] * (-len(rows) % 16)
        values = jnp.concatenate([r.astype(f32) for r in rows], axis=0).astype(bf16)
        moved = lax.dot_general(values, found, (((1,), (1,)), ((), ())), preferred_element_type=f32)
        moved = moved.astype(jnp.int32)
        return [
            jnp.concatenate([moved[i * chunks + c : i * chunks + c + 1] for c in range(chunks)], axis=1)
            for i in range(len(parts))
        ]

    inner = own & (col >= edge) & (col < num_blocks - edge)
    parts = (inner, own & ~inner, heads, tails, own, heads, tails)
    cases = []
    for which in range(FLIPS):
        chosen = parts[which]
        dest, operand, empty = row, source, num_blocks if which < FORWARD_HEADS else 2 * edge
        if which >= ADJOINT_OWN:
            dest, operand, empty = source, row, num_blocks
        used = live & chosen
        cases.append((dest, operand, empty, used, (key == jnp.where(used, dest, -1)).astype(f32)))
    flip = live & (turned == 1)
    ones = jnp.broadcast_to(flip.astype(f32), (16, slots))
    members = jnp.concatenate([case[4].astype(bf16) for case in cases] + [ones.astype(bf16)], axis=0)
    ranks = jnp.dot(members, earlier, preferred_element_type=f32)
    for which, (dest, operand, empty, used, member) in enumerate(cases):
        before = ranks[which * num_blocks : (which + 1) * num_blocks]
        pairs = (jnp.sum(member, axis=1, keepdims=True).astype(jnp.int32) + 1) >> 1
        wide = jnp.broadcast_to(pairs.astype(f32), (num_blocks, 128)).astype(bf16)
        offset = jnp.dot(below, wide, preferred_element_type=f32)[:, :1]
        position = jnp.sum(member * (before + 2.0 * offset), axis=0, keepdims=True).astype(jnp.int32)
        position = jnp.where(used, position, -1)
        low, high, move, to = invert(position, [index & 255, index >> 8, operand - empty, dest])
        tab[which : which + 1] = low + (high << 8) + ((move + empty) << 9) + (to << 16)
        count = jnp.sum(pairs.astype(f32), axis=0, keepdims=True).astype(jnp.int32)
        meta = meta + jnp.where(lane == slots + which, (count + (HALF - 1)) // HALF, 0)
    rank = jnp.where(flip, ranks[FLIPS * num_blocks : FLIPS * num_blocks + 1].astype(jnp.int32), -1)
    low, high, hit = invert(rank, [index & 255, index >> 8, flip.astype(jnp.int32)])
    count = jnp.sum(ones[:1], axis=1, keepdims=True).astype(jnp.int32)
    meta = meta + jnp.where(lane == slots + FLIPS, (count + (TURN - 1)) // TURN, 0)
    flips = jnp.where(hit == 1, low + (high << 8), slots)
    tab[FLIPS : FLIPS + 1] = jnp.where(lane < slots, flips, meta)


def pair_loop(which, tab, source, matrix, acc):
    transposed = which >= ADJOINT_OWN

    def add(start, count):
        done = []
        for u in range(count):
            place = (start + u) * 2
            one, two = tab[which, place], tab[which, place + 1]
            lhs = jnp.concatenate([source[(one >> 9) & 127], source[(two >> 9) & 127]], axis=1)
            first, second = matrix[one & 511], matrix[two & 511]
            rhs = jnp.concatenate([first, second], axis=0 if transposed else 1)
            dims = (((1,), (0 if transposed else 1,)), ((), ()))
            done.append((one >> 16, lax.dot_general(lhs, rhs, dims, preferred_element_type=jnp.float32)))
        for dest, value in done:
            acc[dest] += value

    halves = tab[FLIPS, matrix.shape[0] - 1 + which]

    def body(step, carry):
        add(step * UNROLL, UNROLL)
        return carry

    lax.fori_loop(0, halves >> 1, body, 0)

    @pl.when((halves & 1) == 1)
    def _():
        add((halves - 1) * HALF, HALF)


def clear(ref):
    def body(b, carry):
        ref[b] = jnp.zeros(ref.shape[1:], ref.dtype)
        return carry

    lax.fori_loop(0, ref.shape[0], body, 0)


def edge_kernel(start, density, head, tail, weights, held, raw, sems):
    size = head.shape[1]
    vectors = start.shape[0]
    edge = head.shape[0] // (vectors + 1)
    width = edge * size
    outs = (head, tail)
    origin = (0, start.shape[1] - width)
    copies = [
        pltpu.make_async_copy(start.at[:, pl.ds(origin[i], width)], held.at[i], sems.at[i]) for i in range(2)
    ]
    copies.append(pltpu.make_async_copy(density, raw, sems.at[2]))
    for copy in copies:
        copy.start()
    copies[2].wait()
    for b in range(weights.shape[0]):
        weights[b : b + 1] = raw[:, b * size : (b + 1) * size].astype(jnp.float32)
    for i in range(2):
        copies[i].wait()
        first = origin[i] // size
        for b in range(edge):
            value = held[i, :, b * size : (b + 1) * size].astype(jnp.float32) * weights[first + b : first + b + 1]
            outs[i][b * vectors : (b + 1) * vectors] = value.astype(jnp.bfloat16)
        outs[i][edge * vectors :] = weights[first : first + edge].astype(jnp.bfloat16)


def first_kernel(count, blocks, start, row, col, turned, weights, matrix, rows, tab, source, held, lists, smem, sems):
    slots = blocks.shape[0]
    part = slots // CHUNKS
    small = [pltpu.make_async_copy(ref, lists.at[i], sems.at[CHUNKS + 1 + i]) for i, ref in enumerate((row, col, turned))]
    copies = small + [pltpu.make_async_copy(start, held, sems.at[CHUNKS])]
    for c in range(CHUNKS):
        here = pl.ds(c * part, part)
        copies.append(pltpu.make_async_copy(blocks.at[here], matrix.at[here], sems.at[c]))
    for copy in copies:
        copy.start()
    num_blocks, vectors = rows.shape[0], start.shape[0]
    size = blocks.shape[-1]
    clear(rows)
    matrix[slots] = jnp.zeros((size, size), matrix.dtype)
    source[num_blocks] = jnp.zeros(source.shape[1:], source.dtype)
    for copy in small:
        copy.wait()
    fill_tables(count[0], count[1], count[2], lists[0], lists[1], lists[2], num_blocks, tab)
    table_copy = pltpu.make_async_copy(tab, smem, sems.at[CHUNKS + 4])
    table_copy.start()
    copies[3].wait()
    top = lax.broadcasted_iota(jnp.int32, (16, size), 0) == 0

    def fill(b, carry):
        cells = pl.ds(pl.multiple_of(b * size, size), size)
        weight = weights[pl.ds(b, 1)]
        source[b, :vectors] = (held[:, cells].astype(jnp.float32) * weight).astype(jnp.bfloat16)
        source[b, vectors:] = jnp.where(top, jnp.broadcast_to(weight, (16, size)), 0.0).astype(jnp.bfloat16)
        return carry

    lax.fori_loop(0, num_blocks, fill, 0, unroll=4)
    across = lax.broadcasted_iota(jnp.int32, (size, size), 0)
    along = lax.broadcasted_iota(jnp.int32, (size, size), 1)
    mirror = (across + along == size - 1).astype(jnp.float32).astype(jnp.bfloat16)
    table_copy.wait()
    for copy in copies[4:]:
        copy.wait()

    def turn(step, carry):
        done = []
        for u in range(TURN):
            slot = smem[FLIPS, step * TURN + u]
            value = jnp.dot(matrix[slot], mirror, preferred_element_type=jnp.float32)
            done.append((slot, value.astype(jnp.bfloat16)))
        for slot, value in done:
            matrix[slot] = value
        return carry

    lax.fori_loop(0, smem[FLIPS, slots + FLIPS], turn, 0)
    pair_loop(INNER, smem, source, matrix, rows)
    pair_loop(OUTER, smem, source, matrix, rows)


def inner_kernel(tab, matrix, middle, rows, source):
    clear(rows)
    num_blocks = rows.shape[0]
    edge = num_blocks // 4
    source[edge : num_blocks - edge] = middle[...]
    source[num_blocks] = jnp.zeros(source.shape[1:], source.dtype)
    pair_loop(INNER, tab, source, matrix, rows)


def outer_kernel(tab, matrix, head, tail, rows_in, rows, source):
    del rows_in
    num_blocks, vectors = rows.shape[:2]
    edge = num_blocks // 4
    for b in range(edge):
        source[b] = head[b * vectors : (b + 1) * vectors]
        source[num_blocks - edge + b] = tail[b * vectors : (b + 1) * vectors]
    source[num_blocks] = jnp.zeros(source.shape[1:], source.dtype)
    pair_loop(OUTER, tab, source, matrix, rows)


def load_rims(first, rims, source):
    edge = source.shape[0] // 2
    vectors = rims[0].shape[0] // edge - (1 if first else 0)
    size = source.shape[2]
    for side, rim in enumerate(rims):
        for b in range(edge):
            source[side * edge + b, :vectors] = rim[b * vectors : (b + 1) * vectors]
        if first:
            weights = rim[edge * vectors :].astype(jnp.float32)
            top = lax.broadcasted_iota(jnp.int32, (16, size), 0) == 0
            for b in range(edge):
                pad = jnp.where(top, jnp.broadcast_to(weights[b : b + 1], (16, size)), 0.0)
                source[side * edge + b, vectors:] = pad.astype(jnp.bfloat16)
    source[2 * edge] = jnp.zeros(source.shape[1:], source.dtype)


def heads_kernel(first, tab, matrix, rows_in, right, lower, rows, source):
    del rows_in
    load_rims(first, (right, lower), source)
    pair_loop(FORWARD_HEADS, tab, source, matrix, rows)


def send_back(total, backs):
    vectors = total.shape[1]
    edge = total.shape[0] // 2
    for side in range(2):
        for b in range(edge):
            backs[side][b * vectors : (b + 1) * vectors] = total[side * edge + b].astype(jnp.bfloat16)


def middle_kernel(first, tab, matrix, rows_in, left, upper, *rest):
    del rows_in
    if first:
        rows, image, inverse = rest[:3]
    else:
        inverse, rows, image = rest[:3]
    right_back, lower_back, source, total = rest[3:]
    num_blocks = rows.shape[0]
    vectors = image.shape[1]
    load_rims(first, (left, upper), source)
    clear(total)
    pair_loop(FORWARD_TAILS, tab, source, matrix, rows)

    def divide(b, carry):
        if first:
            factor = 1.0 / rows[b, vectors : vectors + 8]
            inverse[b] = factor
        else:
            factor = inverse[b]
        image[b] = (rows[b, :vectors] * factor[:1]).astype(jnp.bfloat16)
        return carry

    lax.fori_loop(0, num_blocks, divide, 0, unroll=4)
    image[num_blocks] = jnp.zeros(image.shape[1:], image.dtype)
    pair_loop(ADJOINT_HEADS, tab, image, matrix, total)
    send_back(total, (right_back, lower_back))


def tails_kernel(tab, matrix, image, left_back, upper_back, total):
    clear(total)
    pair_loop(ADJOINT_TAILS, tab, image, matrix, total)
    send_back(total, (left_back, upper_back))


def adjoint_kernel(tab, matrix, image, weights, total, norm, *rest):
    clear(total)
    pair_loop(ADJOINT_OWN, tab, image, matrix, total)
    num_blocks = total.shape[0]
    edge = num_blocks // 4

    def inside(b, sums):
        value = total[b]
        weighted = value * weights[pl.ds(b, 1)]
        if rest:
            rest[0][b - edge] = weighted.astype(jnp.bfloat16)
        return sums + weighted * value

    zero = jnp.zeros(norm.shape, jnp.float32)
    norm[...] = lax.fori_loop(edge, num_blocks - edge, inside, zero)


def add_edge(total, weights, from_block, one, two, sums, store):
    vectors = total.shape[1]

    def add(b, carry):
        rows = pl.ds(pl.multiple_of(b * vectors, vectors), vectors)
        value = total[from_block + b] + (one[rows].astype(jnp.float32) + two[rows].astype(jnp.float32))
        weighted = value * weights[pl.ds(from_block + b, 1)]
        store(b, rows, value, weighted)
        return carry + weighted * value

    return lax.fori_loop(0, total.shape[0] // 4, add, sums, unroll=2)


def join_kernel(tail, total, weights, one, two, norm_in, out, norm):
    def store(b, rows, value, weighted):
        out[rows] = weighted.astype(jnp.bfloat16)

    from_block = total.shape[0] // 4 * 3 if tail else 0
    norm[...] = add_edge(total, weights, from_block, one, two, norm_in[...], store)


def sum_kernel(total_in, weights, low0, low1, high0, high1, norm_in, norm_first, total, message):
    del total_in
    sums = norm_in[...]
    size = total.shape[2]
    for from_block, one, two in ((0, low0, low1), (total.shape[0] // 4 * 3, high0, high1)):

        def store(b, rows, value, weighted, from_block=from_block):
            total[from_block + b] = value

        sums = add_edge(total, weights, from_block, one, two, sums, store)
    ones = jnp.ones((8, size), jnp.float32)
    both = [
        lax.dot_general(
            ones, part, (((1,), (1,)), ((), ())), precision=lax.Precision.HIGHEST, preferred_element_type=jnp.float32
        )
        for part in (norm_first[...], sums)
    ]
    message[...] = jnp.broadcast_to(jnp.concatenate(both, axis=1)[:1], message.shape)


def final_kernel(total_cells, sums, total, out):
    num_blocks, vectors, size = total.shape
    both = jnp.sum(sums[...], axis=0, keepdims=True) * (1.0 / total_cells)
    diagonal = lax.broadcasted_iota(jnp.int32, (vectors, size), 0)
    lane = lax.broadcasted_iota(jnp.int32, (vectors, size), 1)
    both = jnp.broadcast_to(both, (vectors, size))
    first = jnp.sum(jnp.where(lane == diagonal, both, 0.0), axis=1, keepdims=True)
    second = jnp.sum(jnp.where(lane == diagonal + vectors, both, 0.0), axis=1, keepdims=True)
    factor = lax.rsqrt(first + 1e-06)
    scale = jnp.broadcast_to(factor * lax.rsqrt(factor * factor * second + 1e-06), (vectors, size))

    def body(b, carry):
        cells = pl.ds(pl.multiple_of(b * size, size), size)
        out[:, cells] = (total[b] * scale).astype(jnp.bfloat16)
        return carry

    lax.fori_loop(0, num_blocks, body, 0, unroll=4)


def shift(x, axis, step):
    count = lax.axis_size(axis)
    return lax.ppermute(x, axis, [(i, (i + step) % count) for i in range(count)])


def heads_out(head):
    return shift(head, "tile", -1), shift(head, "layer", -1)


def tails_out(tail):
    return shift(tail, "tile", 1), shift(tail, "layer", 1)


def call(kernel, name, outs, in_specs, scratch, flops, nbytes, aliases={}):
    return pl.pallas_call(
        kernel,
        name=name,
        out_shape=outs,
        in_specs=in_specs,
        out_specs=[VMEM_SPEC] * len(outs),
        scratch_shapes=scratch,
        input_output_aliases=aliases,
        compiler_params=pltpu.CompilerParams(vmem_limit_bytes=16 * 1024 * 1024),
        cost_estimate=pl.CostEstimate(flops=flops, bytes_accessed=nbytes, transcendentals=0),
    )


def local(blocks, slot_rows, slot_cols, rotation, live_block_count, density, start):
    bf16, f32 = jnp.bfloat16, jnp.float32
    blocks, start = blocks[0, 0], start[0, 0]
    slots, size = blocks.shape[0], blocks.shape[2]
    vectors, cells = start.shape
    num_blocks = cells // size
    edge = num_blocks // 4
    devices = lax.axis_size("layer") * lax.axis_size("tile")
    total_cells = cells * devices
    work = slots * size * size * vectors
    tall = vectors + 16
    rim_type = VM((edge * vectors, size), bf16)
    first_rim_type = VM((edge * (vectors + 1), size), bf16)
    block_f32 = VM((num_blocks, vectors, size), f32)
    tall_f32 = VM((num_blocks, tall, size), f32)
    image_type = VM((num_blocks + 1, vectors, size), bf16)
    middle_type = VM((num_blocks - 2 * edge, vectors, size), bf16)
    norm_type = VM((vectors, size), f32)

    def outside(x):
        return pltpu.with_memory_space_constraint(x, pltpu.HBM)

    start = outside(start)
    head, tail, weights = call(
        edge_kernel,
        "edges",
        [first_rim_type, first_rim_type, VM((num_blocks, size), f32)],
        [HBM_SPEC, HBM_SPEC],
        [
            VM((2, vectors, edge * size), bf16),
            VM((1, cells), bf16),
            pltpu.SemaphoreType.DMA((3,)),
        ],
        0,
        start.size,
    )(start, outside(density[0]))
    heads, tails = heads_out(head), tails_out(tail)

    layer = lax.axis_index("layer")
    above, beneath = layer > 0, layer < lax.axis_size("layer") - 1
    facts = jnp.stack([live_block_count[0, 0], above.astype(jnp.int32), beneath.astype(jnp.int32)])
    places = 2 * ((slots + num_blocks) // 2)
    matrix, rows, tab = call(
        first_kernel,
        "own_first",
        [VM((slots + 1, size, size), bf16), tall_f32, VM((8, places), jnp.int32)],
        [SMEM_SPEC] + [HBM_SPEC] * 5 + [VMEM_SPEC],
        [
            VM((num_blocks + 1, tall, size), bf16),
            VM((vectors, cells), bf16),
            VM((3, 1, slots), jnp.int32),
            pltpu.SMEM((8, places), jnp.int32),
            pltpu.SemaphoreType.DMA((CHUNKS + 5,)),
        ],
        2 * work,
        2 * blocks.size * 2,
    )(
        facts,
        outside(blocks),
        start,
        outside(slot_rows[0]),
        outside(slot_cols[0]),
        outside(rotation[0]),
        weights,
    )

    inverse = None
    for turn in range(2):
        first = turn == 0
        rows_type = tall_f32 if first else block_f32
        source_type = VM((2 * edge + 1, tall if first else vectors, size), bf16)
        half_f32 = VM((2 * edge, vectors, size), f32)
        suffix = "_first" if first else "_next"
        if not first:
            (rows,) = call(
                outer_kernel,
                "outer",
                [block_f32],
                [SMEM_SPEC] + [VMEM_SPEC] * 4,
                [VM((num_blocks + 1, vectors, size), bf16)],
                work // 2,
                blocks.size // 2,
                {4: 0},
            )(tab, matrix, head, tail, rows)
        (rows,) = call(
            functools.partial(heads_kernel, first),
            "heads" + suffix,
            [rows_type],
            [SMEM_SPEC] + [VMEM_SPEC] * 4,
            [source_type],
            work // 2,
            blocks.size // 2,
            {2: 0},
        )(tab, matrix, rows, *heads)
        extra = [] if first else [inverse]
        result = call(
            functools.partial(middle_kernel, first),
            "middle" + suffix,
            [rows_type, image_type] + ([VM((num_blocks, 8, size), f32)] if first else []) + [rim_type] * 2,
            [SMEM_SPEC] + [VMEM_SPEC] * (4 + len(extra)),
            [source_type, half_f32],
            work,
            blocks.size,
            {2: 0},
        )(tab, matrix, rows, *tails, *extra)
        image = result[1]
        if first:
            inverse = result[2]
        right, lower = result[-2:]
        lows = (shift(right, "tile", 1), shift(lower, "layer", 1))
        left, upper = call(
            tails_kernel,
            "tails" + suffix,
            [rim_type] * 2,
            [SMEM_SPEC] + [VMEM_SPEC] * 2,
            [half_f32],
            work // 2,
            blocks.size // 2,
        )(tab, matrix, image)
        highs = (shift(left, "tile", -1), shift(upper, "layer", -1))
        result = call(
            adjoint_kernel,
            "adjoint" + suffix,
            [block_f32, norm_type] + ([middle_type] if first else []),
            [SMEM_SPEC] + [VMEM_SPEC] * 3,
            [],
            work,
            blocks.size,
        )(tab, matrix, image, weights)
        total, norm = result[:2]
        if first:
            (rows,) = call(
                inner_kernel,
                "inner",
                [block_f32],
                [SMEM_SPEC] + [VMEM_SPEC] * 2,
                [VM((num_blocks + 1, vectors, size), bf16)],
                work // 2,
                blocks.size // 2,
            )(tab, matrix, result[2])
            head, norm = call(
                functools.partial(join_kernel, False),
                "join_head",
                [rim_type, norm_type],
                [VMEM_SPEC] * 5,
                [],
                0,
                edge * vectors * size * 8,
            )(total, weights, *lows, norm)
            heads = heads_out(head)
            norm, rows = lax.optimization_barrier((norm, rows))
            tail, norm_first = call(
                functools.partial(join_kernel, True),
                "join_tail",
                [rim_type, norm_type],
                [VMEM_SPEC] * 5,
                [],
                0,
                edge * vectors * size * 8,
            )(total, weights, *highs, norm)
            tails = tails_out(tail)
    total, message = call(
        sum_kernel,
        "join_last",
        [block_f32, VM((devices, 2 * vectors), f32)],
        [VMEM_SPEC] * 8,
        [],
        0,
        2 * edge * vectors * size * 8,
        {0: 0},
    )(total, weights, *lows, *highs, norm, norm_first)
    sums = lax.all_to_all(message, ("layer", "tile"), 0, 0, tiled=True)
    out = call(
        functools.partial(final_kernel, total_cells),
        "write_out",
        [jax.ShapeDtypeStruct((vectors, cells), bf16)],
        [VMEM_SPEC] * 2,
        [],
        0,
        cells * vectors * 6,
    )(sums, total)[0]
    return out[None, None]


def solution(mesh):
    in_specs = (
        P("layer", "tile", None, None, None),
        P("layer", "tile", None),
        P("layer", "tile", None),
        P("layer", "tile", None),
        P("layer", "tile"),
        P("layer", "tile", None),
        P("layer", "tile", None, None),
    )
    out_specs = P("layer", "tile", None, None)
    return jax.shard_map(local, mesh=mesh, in_specs=in_specs, out_specs=out_specs, check_vma=False)
```

```python
import functools

import jax
import jax.numpy as jnp
from jax import lax
from jax.experimental import pallas as pl
from jax.experimental.pallas import tpu as pltpu
from jax.sharding import PartitionSpec as P

UNROLL = 16
HALF = UNROLL // 2
TURN = 16
CHUNKS = 8
VM = pltpu.VMEM
VMEM_SPEC = pl.BlockSpec(memory_space=pltpu.VMEM)
SMEM_SPEC = pl.BlockSpec(memory_space=pltpu.SMEM)
HBM_SPEC = pl.BlockSpec(memory_space=pltpu.HBM)
FORWARD_OWN, FORWARD_HEADS, FORWARD_TAILS, ADJOINT_OWN, ADJOINT_HEADS, ADJOINT_TAILS, FLIPS, TRIPS = range(8)


def fill_tables(live_count, above, beneath, row, col, turned, num_blocks, tab):
    f32, bf16 = jnp.float32, jnp.bfloat16
    slots = row.shape[1]
    places = tab.shape[1]
    index = lax.broadcasted_iota(jnp.int32, (1, slots), 1)
    live = index < live_count
    edge = num_blocks // 4
    outer = col - num_blocks
    side = outer // edge
    live = live & ((side != 2) | (above == 1)) & ((side != 3) | (beneath == 1))
    own = outer < 0
    heads = (outer >= 0) & ((side & 1) == 1)
    tails = (outer >= 0) & ((side & 1) == 0)
    source = jnp.where(own, col, (side >> 1) * edge + outer - side * edge)
    key = lax.broadcasted_iota(jnp.int32, (num_blocks, slots), 0)
    spot = lax.broadcasted_iota(jnp.int32, (128, slots), 0)
    earlier = (
        lax.broadcasted_iota(jnp.int32, (slots, slots), 0) < lax.broadcasted_iota(jnp.int32, (slots, slots), 1)
    ).astype(f32).astype(bf16)
    below = (
        lax.broadcasted_iota(jnp.int32, (num_blocks, num_blocks), 1)
        < lax.broadcasted_iota(jnp.int32, (num_blocks, num_blocks), 0)
    ).astype(f32).astype(bf16)
    lane = lax.broadcasted_iota(jnp.int32, (1, places), 1)
    meta = jnp.zeros((1, places), jnp.int32)

    def invert(position, parts):
        found = (spot == (position & 127)).astype(f32).astype(bf16)
        chunks = places // 128
        rows = [jnp.where((position >> 7) == c, p, 0) for p in parts for c in range(chunks)]
        rows = rows + [jnp.zeros((1, slots), jnp.int32)] * (-len(rows) % 16)
        values = jnp.concatenate([r.astype(f32) for r in rows], axis=0).astype(bf16)
        moved = lax.dot_general(values, found, (((1,), (1,)), ((), ())), preferred_element_type=f32)
        moved = moved.astype(jnp.int32)
        return [
            jnp.concatenate([moved[i * chunks + c : i * chunks + c + 1] for c in range(chunks)], axis=1)
            for i in range(len(parts))
        ]

    parts = ((own, num_blocks), (heads, 2 * edge), (tails, 2 * edge))
    cases = []
    for which in range(6):
        chosen, empty = parts[which % 3]
        dest, operand = row, source
        if which >= ADJOINT_OWN:
            dest, operand, empty = source, row, num_blocks
        used = live & chosen
        cases.append((dest, operand, empty, used, (key == jnp.where(used, dest, -1)).astype(f32)))
    flip = live & (turned == 1)
    ones = jnp.broadcast_to(flip.astype(f32), (16, slots))
    members = jnp.concatenate([case[4].astype(bf16) for case in cases] + [ones.astype(bf16)], axis=0)
    ranks = jnp.dot(members, earlier, preferred_element_type=f32)
    for which, (dest, operand, empty, used, member) in enumerate(cases):
        before = ranks[which * num_blocks : (which + 1) * num_blocks]
        pairs = (jnp.sum(member, axis=1, keepdims=True).astype(jnp.int32) + 1) >> 1
        wide = jnp.broadcast_to(pairs.astype(f32), (num_blocks, 128)).astype(bf16)
        offset = jnp.dot(below, wide, preferred_element_type=f32)[:, :1]
        position = jnp.sum(member * (before + 2.0 * offset), axis=0, keepdims=True).astype(jnp.int32)
        position = jnp.where(used, position, -1)
        low, high, move, to = invert(position, [index & 255, index >> 8, operand - empty, dest])
        tab[which : which + 1] = low + (high << 8) + ((move + empty) << 9) + (to << 16)
        count = jnp.sum(pairs.astype(f32), axis=0, keepdims=True).astype(jnp.int32)
        meta = meta + jnp.where(lane == which, (count + (HALF - 1)) // HALF, 0)
    rank = jnp.where(flip, ranks[6 * num_blocks : 6 * num_blocks + 1].astype(jnp.int32), -1)
    low, high, hit = invert(rank, [index & 255, index >> 8, flip.astype(jnp.int32)])
    tab[FLIPS : FLIPS + 1] = jnp.where(hit == 1, low + (high << 8), slots)
    count = jnp.sum(ones[:1], axis=1, keepdims=True).astype(jnp.int32)
    meta = meta + jnp.where(lane == FLIPS, (count + (TURN - 1)) // TURN, 0)
    tab[TRIPS : TRIPS + 1] = meta


def pair_loop(which, tab, source, matrix, acc):
    transposed = which >= ADJOINT_OWN

    def add(start, count):
        done = []
        for u in range(count):
            place = (start + u) * 2
            one, two = tab[which, place], tab[which, place + 1]
            lhs = jnp.concatenate([source[(one >> 9) & 127], source[(two >> 9) & 127]], axis=1)
            first, second = matrix[one & 511], matrix[two & 511]
            rhs = jnp.concatenate([first, second], axis=0 if transposed else 1)
            dims = (((1,), (0 if transposed else 1,)), ((), ()))
            done.append((one >> 16, lax.dot_general(lhs, rhs, dims, preferred_element_type=jnp.float32)))
        for dest, value in done:
            acc[dest] += value

    halves = tab[TRIPS, which]

    def body(step, carry):
        add(step * UNROLL, UNROLL)
        return carry

    lax.fori_loop(0, halves >> 1, body, 0)

    @pl.when((halves & 1) == 1)
    def _():
        add((halves - 1) * HALF, HALF)


def clear(ref):
    def body(b, carry):
        ref[b] = jnp.zeros(ref.shape[1:], ref.dtype)
        return carry

    lax.fori_loop(0, ref.shape[0], body, 0)


def edge_kernel(start, density, head, tail, weights, held, raw, sems):
    size = head.shape[1]
    vectors = start.shape[0]
    edge = head.shape[0] // (vectors + 1)
    width = edge * size
    outs = (head, tail)
    origin = (0, start.shape[1] - width)
    copies = [
        pltpu.make_async_copy(start.at[:, pl.ds(origin[i], width)], held.at[i], sems.at[i]) for i in range(2)
    ]
    copies.append(pltpu.make_async_copy(density, raw, sems.at[2]))
    for copy in copies:
        copy.start()
    copies[2].wait()
    for b in range(weights.shape[0]):
        weights[b : b + 1] = raw[:, b * size : (b + 1) * size].astype(jnp.float32)
    for i in range(2):
        copies[i].wait()
        first = origin[i] // size
        for b in range(edge):
            value = held[i, :, b * size : (b + 1) * size].astype(jnp.float32) * weights[first + b : first + b + 1]
            outs[i][b * vectors : (b + 1) * vectors] = value.astype(jnp.bfloat16)
        outs[i][edge * vectors :] = weights[first : first + edge].astype(jnp.bfloat16)


def first_kernel(count, blocks, start, row, col, turned, weights, matrix, rows, tab, source, held, lists, smem, sems):
    slots = blocks.shape[0]
    part = slots // CHUNKS
    small = [pltpu.make_async_copy(ref, lists.at[i], sems.at[CHUNKS + 1 + i]) for i, ref in enumerate((row, col, turned))]
    copies = small + [pltpu.make_async_copy(start, held, sems.at[CHUNKS])]
    for c in range(CHUNKS):
        here = pl.ds(c * part, part)
        copies.append(pltpu.make_async_copy(blocks.at[here], matrix.at[here], sems.at[c]))
    for copy in copies:
        copy.start()
    num_blocks, vectors = rows.shape[0], start.shape[0]
    size = blocks.shape[-1]
    clear(rows)
    matrix[slots] = jnp.zeros((size, size), matrix.dtype)
    source[num_blocks] = jnp.zeros(source.shape[1:], source.dtype)
    for copy in small:
        copy.wait()
    fill_tables(count[0], count[1], count[2], lists[0], lists[1], lists[2], num_blocks, tab)
    table_copy = pltpu.make_async_copy(tab, smem, sems.at[CHUNKS + 4])
    table_copy.start()
    copies[3].wait()
    top = lax.broadcasted_iota(jnp.int32, (16, size), 0) == 0

    def fill(b, carry):
        cells = pl.ds(pl.multiple_of(b * size, size), size)
        weight = weights[pl.ds(b, 1)]
        source[b, :vectors] = (held[:, cells].astype(jnp.float32) * weight).astype(jnp.bfloat16)
        source[b, vectors:] = jnp.where(top, jnp.broadcast_to(weight, (16, size)), 0.0).astype(jnp.bfloat16)
        return carry

    lax.fori_loop(0, num_blocks, fill, 0, unroll=4)
    across = lax.broadcasted_iota(jnp.int32, (size, size), 0)
    along = lax.broadcasted_iota(jnp.int32, (size, size), 1)
    mirror = (across + along == size - 1).astype(jnp.float32).astype(jnp.bfloat16)
    table_copy.wait()
    for copy in copies[4:]:
        copy.wait()

    def turn(step, carry):
        done = []
        for u in range(TURN):
            slot = smem[FLIPS, step * TURN + u]
            value = jnp.dot(matrix[slot], mirror, preferred_element_type=jnp.float32)
            done.append((slot, value.astype(jnp.bfloat16)))
        for slot, value in done:
            matrix[slot] = value
        return carry

    lax.fori_loop(0, smem[TRIPS, FLIPS], turn, 0)
    pair_loop(FORWARD_OWN, smem, source, matrix, rows)


def own_kernel(tab, matrix, head, middle, tail, rows, source):
    clear(rows)
    num_blocks = rows.shape[0]
    edge = num_blocks // 4
    vectors = rows.shape[1]
    for b in range(edge):
        source[b] = head[b * vectors : (b + 1) * vectors]
        source[num_blocks - edge + b] = tail[b * vectors : (b + 1) * vectors]
    source[edge : num_blocks - edge] = middle[...]
    source[num_blocks] = jnp.zeros(source.shape[1:], source.dtype)
    pair_loop(FORWARD_OWN, tab, source, matrix, rows)


def load_rims(first, rims, source):
    edge = source.shape[0] // 2
    vectors = rims[0].shape[0] // edge - (1 if first else 0)
    size = source.shape[2]
    for side, rim in enumerate(rims):
        for b in range(edge):
            source[side * edge + b, :vectors] = rim[b * vectors : (b + 1) * vectors]
        if first:
            weights = rim[edge * vectors :].astype(jnp.float32)
            top = lax.broadcasted_iota(jnp.int32, (16, size), 0) == 0
            for b in range(edge):
                pad = jnp.where(top, jnp.broadcast_to(weights[b : b + 1], (16, size)), 0.0)
                source[side * edge + b, vectors:] = pad.astype(jnp.bfloat16)
    source[2 * edge] = jnp.zeros(source.shape[1:], source.dtype)


def heads_kernel(first, tab, matrix, rows_in, right, lower, rows, source):
    del rows_in
    load_rims(first, (right, lower), source)
    pair_loop(FORWARD_HEADS, tab, source, matrix, rows)


def send_back(total, backs):
    vectors = total.shape[1]
    edge = total.shape[0] // 2
    for side in range(2):
        for b in range(edge):
            backs[side][b * vectors : (b + 1) * vectors] = total[side * edge + b].astype(jnp.bfloat16)


def middle_kernel(first, tab, matrix, rows_in, left, upper, *rest):
    del rows_in
    if first:
        rows, image, inverse = rest[:3]
    else:
        inverse, rows, image = rest[:3]
    lower_back, right_back, source, total = rest[3:]
    num_blocks = rows.shape[0]
    vectors = image.shape[1]
    load_rims(first, (left, upper), source)
    clear(total)
    pair_loop(FORWARD_TAILS, tab, source, matrix, rows)

    def divide(b, carry):
        if first:
            factor = 1.0 / rows[b, vectors : vectors + 8]
            inverse[b] = factor
        else:
            factor = inverse[b]
        image[b] = (rows[b, :vectors] * factor[:1]).astype(jnp.bfloat16)
        return carry

    lax.fori_loop(0, num_blocks, divide, 0, unroll=4)
    image[num_blocks] = jnp.zeros(image.shape[1:], image.dtype)
    pair_loop(ADJOINT_HEADS, tab, image, matrix, total)
    send_back(total, (right_back, lower_back))


def tails_kernel(tab, matrix, image, upper_back, left_back, total):
    clear(total)
    pair_loop(ADJOINT_TAILS, tab, image, matrix, total)
    send_back(total, (left_back, upper_back))


def adjoint_kernel(tab, matrix, image, weights, total, norm, *rest):
    clear(total)
    pair_loop(ADJOINT_OWN, tab, image, matrix, total)
    num_blocks = total.shape[0]
    edge = num_blocks // 4

    def inside(b, sums):
        value = total[b]
        weighted = value * weights[pl.ds(b, 1)]
        if rest:
            rest[0][b - edge] = weighted.astype(jnp.bfloat16)
        return sums + weighted * value

    zero = jnp.zeros(norm.shape, jnp.float32)
    norm[...] = lax.fori_loop(edge, num_blocks - edge, inside, zero)


def add_edge(total, weights, from_block, one, two, sums, store):
    vectors = total.shape[1]

    def add(b, carry):
        rows = pl.ds(pl.multiple_of(b * vectors, vectors), vectors)
        value = total[from_block + b] + (one[rows].astype(jnp.float32) + two[rows].astype(jnp.float32))
        weighted = value * weights[pl.ds(from_block + b, 1)]
        store(b, rows, value, weighted)
        return carry + weighted * value

    return lax.fori_loop(0, total.shape[0] // 4, add, sums, unroll=2)


def join_kernel(tail, total, weights, one, two, norm_in, out, norm):
    def store(b, rows, value, weighted):
        out[rows] = weighted.astype(jnp.bfloat16)

    from_block = total.shape[0] // 4 * 3 if tail else 0
    norm[...] = add_edge(total, weights, from_block, one, two, norm_in[...], store)


def sum_kernel(total_in, weights, low0, low1, high0, high1, norm_in, norm_first, total, message):
    del total_in
    sums = norm_in[...]
    size = total.shape[2]
    for from_block, one, two in ((0, low0, low1), (total.shape[0] // 4 * 3, high0, high1)):

        def store(b, rows, value, weighted, from_block=from_block):
            total[from_block + b] = value

        sums = add_edge(total, weights, from_block, one, two, sums, store)
    ones = jnp.ones((8, size), jnp.float32)
    both = [
        lax.dot_general(
            ones, part, (((1,), (1,)), ((), ())), precision=lax.Precision.HIGHEST, preferred_element_type=jnp.float32
        )
        for part in (norm_first[...], sums)
    ]
    message[...] = jnp.broadcast_to(jnp.concatenate(both, axis=1)[:1], message.shape)


def final_kernel(total_cells, sums, total, out):
    num_blocks, vectors, size = total.shape
    both = jnp.sum(sums[...], axis=0, keepdims=True) * (1.0 / total_cells)
    diagonal = lax.broadcasted_iota(jnp.int32, (vectors, size), 0)
    lane = lax.broadcasted_iota(jnp.int32, (vectors, size), 1)
    both = jnp.broadcast_to(both, (vectors, size))
    first = jnp.sum(jnp.where(lane == diagonal, both, 0.0), axis=1, keepdims=True)
    second = jnp.sum(jnp.where(lane == diagonal + vectors, both, 0.0), axis=1, keepdims=True)
    factor = lax.rsqrt(first + 1e-06)
    scale = jnp.broadcast_to(factor * lax.rsqrt(factor * factor * second + 1e-06), (vectors, size))

    def body(b, carry):
        cells = pl.ds(pl.multiple_of(b * size, size), size)
        out[:, cells] = (total[b] * scale).astype(jnp.bfloat16)
        return carry

    lax.fori_loop(0, num_blocks, body, 0, unroll=4)


def shift(x, axis, step):
    count = lax.axis_size(axis)
    return lax.ppermute(x, axis, [(i, (i + step) % count) for i in range(count)])


def heads_out(head):
    return shift(head, "tile", -1), shift(head, "layer", -1)


def tails_out(tail):
    return shift(tail, "tile", 1), shift(tail, "layer", 1)


def call(kernel, name, outs, in_specs, scratch, flops, nbytes, aliases={}):
    return pl.pallas_call(
        kernel,
        name=name,
        out_shape=outs,
        in_specs=in_specs,
        out_specs=[VMEM_SPEC] * len(outs),
        scratch_shapes=scratch,
        input_output_aliases=aliases,
        compiler_params=pltpu.CompilerParams(vmem_limit_bytes=16 * 1024 * 1024),
        cost_estimate=pl.CostEstimate(flops=flops, bytes_accessed=nbytes, transcendentals=0),
    )


def local(blocks, slot_rows, slot_cols, rotation, live_block_count, density, start):
    bf16, f32 = jnp.bfloat16, jnp.float32
    blocks, start = blocks[0, 0], start[0, 0]
    slots, size = blocks.shape[0], blocks.shape[2]
    vectors, cells = start.shape
    num_blocks = cells // size
    edge = num_blocks // 4
    devices = lax.axis_size("layer") * lax.axis_size("tile")
    total_cells = cells * devices
    work = slots * size * size * vectors
    tall = vectors + 16
    rim_type = VM((edge * vectors, size), bf16)
    first_rim_type = VM((edge * (vectors + 1), size), bf16)
    block_f32 = VM((num_blocks, vectors, size), f32)
    tall_f32 = VM((num_blocks, tall, size), f32)
    image_type = VM((num_blocks + 1, vectors, size), bf16)
    middle_type = VM((num_blocks - 2 * edge, vectors, size), bf16)
    norm_type = VM((vectors, size), f32)

    def outside(x):
        return pltpu.with_memory_space_constraint(x, pltpu.HBM)

    start = outside(start)
    head, tail, weights = call(
        edge_kernel,
        "edges",
        [first_rim_type, first_rim_type, VM((num_blocks, size), f32)],
        [HBM_SPEC, HBM_SPEC],
        [
            VM((2, vectors, edge * size), bf16),
            VM((1, cells), bf16),
            pltpu.SemaphoreType.DMA((3,)),
        ],
        0,
        start.size,
    )(start, outside(density[0]))
    heads, tails = heads_out(head), tails_out(tail)

    layer = lax.axis_index("layer")
    above, beneath = layer > 0, layer < lax.axis_size("layer") - 1
    facts = jnp.stack([live_block_count[0, 0], above.astype(jnp.int32), beneath.astype(jnp.int32)])
    places = 2 * ((slots + num_blocks) // 2)
    matrix, rows, tab = call(
        first_kernel,
        "own_first",
        [VM((slots + 1, size, size), bf16), tall_f32, VM((8, places), jnp.int32)],
        [SMEM_SPEC] + [HBM_SPEC] * 5 + [VMEM_SPEC],
        [
            VM((num_blocks + 1, tall, size), bf16),
            VM((vectors, cells), bf16),
            VM((3, 1, slots), jnp.int32),
            pltpu.SMEM((8, places), jnp.int32),
            pltpu.SemaphoreType.DMA((CHUNKS + 5,)),
        ],
        2 * work,
        2 * blocks.size * 2,
    )(
        facts,
        outside(blocks),
        start,
        outside(slot_rows[0]),
        outside(slot_cols[0]),
        outside(rotation[0]),
        weights,
    )

    inverse = None
    for turn in range(2):
        first = turn == 0
        rows_type = tall_f32 if first else block_f32
        source_type = VM((2 * edge + 1, tall if first else vectors, size), bf16)
        half_f32 = VM((2 * edge, vectors, size), f32)
        suffix = "_first" if first else "_next"
        if not first:
            (rows,) = call(
                own_kernel,
                "own_next",
                [block_f32],
                [SMEM_SPEC] + [VMEM_SPEC] * 4,
                [VM((num_blocks + 1, vectors, size), bf16)],
                work,
                blocks.size,
            )(tab, matrix, head, middle, tail)
        (rows,) = call(
            functools.partial(heads_kernel, first),
            "heads" + suffix,
            [rows_type],
            [SMEM_SPEC] + [VMEM_SPEC] * 4,
            [source_type],
            work // 2,
            blocks.size // 2,
            {2: 0},
        )(tab, matrix, rows, *heads)
        extra = [] if first else [inverse]
        result = call(
            functools.partial(middle_kernel, first),
            "middle" + suffix,
            [rows_type, image_type] + ([VM((num_blocks, 8, size), f32)] if first else []) + [rim_type] * 2,
            [SMEM_SPEC] + [VMEM_SPEC] * (4 + len(extra)),
            [source_type, half_f32],
            work,
            blocks.size,
            {2: 0},
        )(tab, matrix, rows, *tails, *extra)
        image = result[1]
        if first:
            inverse = result[2]
        lower, right = result[-2:]
        lows = (shift(lower, "layer", 1), shift(right, "tile", 1))
        upper, left = call(
            tails_kernel,
            "tails" + suffix,
            [rim_type] * 2,
            [SMEM_SPEC] + [VMEM_SPEC] * 2,
            [half_f32],
            work // 2,
            blocks.size // 2,
        )(tab, matrix, image)
        highs = (shift(upper, "layer", -1), shift(left, "tile", -1))
        result = call(
            adjoint_kernel,
            "adjoint" + suffix,
            [block_f32, norm_type] + ([middle_type] if first else []),
            [SMEM_SPEC] + [VMEM_SPEC] * 3,
            [],
            work,
            blocks.size,
        )(tab, matrix, image, weights)
        total, norm = result[:2]
        if first:
            middle = result[2]
            head, norm = call(
                functools.partial(join_kernel, False),
                "join_head",
                [rim_type, norm_type],
                [VMEM_SPEC] * 5,
                [],
                0,
                edge * vectors * size * 8,
            )(total, weights, *lows, norm)
            heads = heads_out(head)
            tail, norm_first = call(
                functools.partial(join_kernel, True),
                "join_tail",
                [rim_type, norm_type],
                [VMEM_SPEC] * 5,
                [],
                0,
                edge * vectors * size * 8,
            )(total, weights, *highs, norm)
            tails = tails_out(tail)
    total, message = call(
        sum_kernel,
        "join_last",
        [block_f32, VM((devices, 2 * vectors), f32)],
        [VMEM_SPEC] * 8,
        [],
        0,
        2 * edge * vectors * size * 8,
        {0: 0},
    )(total, weights, *lows, *highs, norm, norm_first)
    sums = lax.all_to_all(message, ("layer", "tile"), 0, 0, tiled=True)
    out = call(
        functools.partial(final_kernel, total_cells),
        "write_out",
        [jax.ShapeDtypeStruct((vectors, cells), bf16)],
        [VMEM_SPEC] * 2,
        [],
        0,
        cells * vectors * 6,
    )(sums, total)[0]
    return out[None, None]


def solution(mesh):
    in_specs = (
        P("layer", "tile", None, None, None),
        P("layer", "tile", None),
        P("layer", "tile", None),
        P("layer", "tile", None),
        P("layer", "tile"),
        P("layer", "tile", None),
        P("layer", "tile", None, None),
    )
    out_specs = P("layer", "tile", None, None)
    return jax.shard_map(local, mesh=mesh, in_specs=in_specs, out_specs=out_specs, check_vma=False)
```

```python
import functools

import jax
import jax.numpy as jnp
from jax import lax
from jax.experimental import pallas as pl
from jax.experimental.pallas import tpu as pltpu
from jax.sharding import PartitionSpec as P

UNROLL = 16
HALF = UNROLL // 2
TURN = 16
CHUNKS = 8
VM = pltpu.VMEM
VMEM_SPEC = pl.BlockSpec(memory_space=pltpu.VMEM)
SMEM_SPEC = pl.BlockSpec(memory_space=pltpu.SMEM)
HBM_SPEC = pl.BlockSpec(memory_space=pltpu.HBM)
FORWARD_OWN, FORWARD_HEADS, FORWARD_TAILS, ADJOINT_OWN, ADJOINT_HEADS, ADJOINT_TAILS, FLIPS, TRIPS = range(8)


def fill_tables(live_count, above, beneath, row, col, turned, num_blocks, tab):
    f32, bf16 = jnp.float32, jnp.bfloat16
    slots = row.shape[1]
    places = tab.shape[1]
    index = lax.broadcasted_iota(jnp.int32, (1, slots), 1)
    live = index < live_count
    edge = num_blocks // 4
    outer = col - num_blocks
    side = outer // edge
    live = live & ((side != 2) | (above == 1)) & ((side != 3) | (beneath == 1))
    own = outer < 0
    heads = (outer >= 0) & ((side & 1) == 1)
    tails = (outer >= 0) & ((side & 1) == 0)
    source = jnp.where(own, col, (side >> 1) * edge + outer - side * edge)
    key = lax.broadcasted_iota(jnp.int32, (num_blocks, slots), 0)
    spot = lax.broadcasted_iota(jnp.int32, (128, slots), 0)
    earlier = (
        lax.broadcasted_iota(jnp.int32, (slots, slots), 0) < lax.broadcasted_iota(jnp.int32, (slots, slots), 1)
    ).astype(f32).astype(bf16)
    below = (
        lax.broadcasted_iota(jnp.int32, (num_blocks, num_blocks), 1)
        < lax.broadcasted_iota(jnp.int32, (num_blocks, num_blocks), 0)
    ).astype(f32).astype(bf16)
    lane = lax.broadcasted_iota(jnp.int32, (1, places), 1)
    meta = jnp.zeros((1, places), jnp.int32)

    def invert(position, parts):
        found = (spot == (position & 127)).astype(f32).astype(bf16)
        chunks = places // 128
        rows = [jnp.where((position >> 7) == c, p, 0) for p in parts for c in range(chunks)]
        rows = rows + [jnp.zeros((1, slots), jnp.int32)] * (-len(rows) % 16)
        values = jnp.concatenate([r.astype(f32) for r in rows], axis=0).astype(bf16)
        moved = lax.dot_general(values, found, (((1,), (1,)), ((), ())), preferred_element_type=f32)
        moved = moved.astype(jnp.int32)
        return [
            jnp.concatenate([moved[i * chunks + c : i * chunks + c + 1] for c in range(chunks)], axis=1)
            for i in range(len(parts))
        ]

    parts = ((own, num_blocks), (heads, 2 * edge), (tails, 2 * edge))
    cases = []
    for which in range(6):
        chosen, empty = parts[which % 3]
        dest, operand = row, source
        if which >= ADJOINT_OWN:
            dest, operand, empty = source, row, num_blocks
        used = live & chosen
        cases.append((dest, operand, empty, used, (key == jnp.where(used, dest, -1)).astype(f32)))
    flip = live & (turned == 1)
    ones = jnp.broadcast_to(flip.astype(f32), (16, slots))
    members = jnp.concatenate([case[4].astype(bf16) for case in cases] + [ones.astype(bf16)], axis=0)
    ranks = jnp.dot(members, earlier, preferred_element_type=f32)
    for which, (dest, operand, empty, used, member) in enumerate(cases):
        before = ranks[which * num_blocks : (which + 1) * num_blocks]
        pairs = (jnp.sum(member, axis=1, keepdims=True).astype(jnp.int32) + 1) >> 1
        wide = jnp.broadcast_to(pairs.astype(f32), (num_blocks, 128)).astype(bf16)
        offset = jnp.dot(below, wide, preferred_element_type=f32)[:, :1]
        position = jnp.sum(member * (before + 2.0 * offset), axis=0, keepdims=True).astype(jnp.int32)
        position = jnp.where(used, position, -1)
        low, high, move, to = invert(position, [index & 255, index >> 8, operand - empty, dest])
        tab[which : which + 1] = low + (high << 8) + ((move + empty) << 9) + (to << 16)
        count = jnp.sum(pairs.astype(f32), axis=0, keepdims=True).astype(jnp.int32)
        meta = meta + jnp.where(lane == which, (count + (HALF - 1)) // HALF, 0)
    rank = jnp.where(flip, ranks[6 * num_blocks : 6 * num_blocks + 1].astype(jnp.int32), -1)
    low, high, hit = invert(rank, [index & 255, index >> 8, flip.astype(jnp.int32)])
    tab[FLIPS : FLIPS + 1] = jnp.where(hit == 1, low + (high << 8), slots)
    count = jnp.sum(ones[:1], axis=1, keepdims=True).astype(jnp.int32)
    meta = meta + jnp.where(lane == FLIPS, (count + (TURN - 1)) // TURN, 0)
    tab[TRIPS : TRIPS + 1] = meta


def pair_loop(which, tab, source, matrix, acc):
    transposed = which >= ADJOINT_OWN

    def add(start, count):
        done = []
        for u in range(count):
            place = (start + u) * 2
            one, two = tab[which, place], tab[which, place + 1]
            lhs = jnp.concatenate([source[(one >> 9) & 127], source[(two >> 9) & 127]], axis=1)
            first, second = matrix[one & 511], matrix[two & 511]
            rhs = jnp.concatenate([first, second], axis=0 if transposed else 1)
            dims = (((1,), (0 if transposed else 1,)), ((), ()))
            done.append((one >> 16, lax.dot_general(lhs, rhs, dims, preferred_element_type=jnp.float32)))
        for dest, value in done:
            acc[dest] += value

    halves = tab[TRIPS, which]

    def body(step, carry):
        add(step * UNROLL, UNROLL)
        return carry

    lax.fori_loop(0, halves >> 1, body, 0)

    @pl.when((halves & 1) == 1)
    def _():
        add((halves - 1) * HALF, HALF)


def clear(ref):
    def body(b, carry):
        ref[b] = jnp.zeros(ref.shape[1:], ref.dtype)
        return carry

    lax.fori_loop(0, ref.shape[0], body, 0)


def edge_kernel(start, density, head, tail, weights, held, raw, sems):
    size = head.shape[1]
    vectors = start.shape[0]
    edge = head.shape[0] // (vectors + 1)
    width = edge * size
    outs = (head, tail)
    origin = (0, start.shape[1] - width)
    copies = [
        pltpu.make_async_copy(start.at[:, pl.ds(origin[i], width)], held.at[i], sems.at[i]) for i in range(2)
    ]
    copies.append(pltpu.make_async_copy(density, raw, sems.at[2]))
    for copy in copies:
        copy.start()
    copies[2].wait()
    for b in range(weights.shape[0]):
        weights[b : b + 1] = raw[:, b * size : (b + 1) * size].astype(jnp.float32)
    for i in range(2):
        copies[i].wait()
        first = origin[i] // size
        for b in range(edge):
            value = held[i, :, b * size : (b + 1) * size].astype(jnp.float32) * weights[first + b : first + b + 1]
            outs[i][b * vectors : (b + 1) * vectors] = value.astype(jnp.bfloat16)
        outs[i][edge * vectors :] = weights[first : first + edge].astype(jnp.bfloat16)


def first_kernel(count, blocks, start, row, col, turned, weights, matrix, rows, tab, source, held, lists, smem, sems):
    slots = blocks.shape[0]
    part = slots // CHUNKS
    small = [pltpu.make_async_copy(ref, lists.at[i], sems.at[CHUNKS + 1 + i]) for i, ref in enumerate((row, col, turned))]
    copies = small + [pltpu.make_async_copy(start, held, sems.at[CHUNKS])]
    for c in range(CHUNKS):
        here = pl.ds(c * part, part)
        copies.append(pltpu.make_async_copy(blocks.at[here], matrix.at[here], sems.at[c]))
    for copy in copies:
        copy.start()
    num_blocks, vectors = rows.shape[0], start.shape[0]
    size = blocks.shape[-1]
    clear(rows)
    matrix[slots] = jnp.zeros((size, size), matrix.dtype)
    source[num_blocks] = jnp.zeros(source.shape[1:], source.dtype)
    for copy in small:
        copy.wait()
    fill_tables(count[0], count[1], count[2], lists[0], lists[1], lists[2], num_blocks, tab)
    table_copy = pltpu.make_async_copy(tab, smem, sems.at[CHUNKS + 4])
    table_copy.start()
    copies[3].wait()
    top = lax.broadcasted_iota(jnp.int32, (16, size), 0) == 0

    def fill(b, carry):
        cells = pl.ds(pl.multiple_of(b * size, size), size)
        weight = weights[pl.ds(b, 1)]
        source[b, :vectors] = (held[:, cells].astype(jnp.float32) * weight).astype(jnp.bfloat16)
        source[b, vectors:] = jnp.where(top, jnp.broadcast_to(weight, (16, size)), 0.0).astype(jnp.bfloat16)
        return carry

    lax.fori_loop(0, num_blocks, fill, 0, unroll=4)
    across = lax.broadcasted_iota(jnp.int32, (size, size), 0)
    along = lax.broadcasted_iota(jnp.int32, (size, size), 1)
    mirror = (across + along == size - 1).astype(jnp.float32).astype(jnp.bfloat16)
    table_copy.wait()
    for copy in copies[4:]:
        copy.wait()

    def turn(step, carry):
        done = []
        for u in range(TURN):
            slot = smem[FLIPS, step * TURN + u]
            value = jnp.dot(matrix[slot], mirror, preferred_element_type=jnp.float32)
            done.append((slot, value.astype(jnp.bfloat16)))
        for slot, value in done:
            matrix[slot] = value
        return carry

    lax.fori_loop(0, smem[TRIPS, FLIPS], turn, 0)
    pair_loop(FORWARD_OWN, smem, source, matrix, rows)


def own_kernel(tab, matrix, head, middle, tail, rows, source):
    clear(rows)
    num_blocks = rows.shape[0]
    edge = num_blocks // 4
    vectors = rows.shape[1]
    for b in range(edge):
        source[b] = head[b * vectors : (b + 1) * vectors]
        source[num_blocks - edge + b] = tail[b * vectors : (b + 1) * vectors]
    source[edge : num_blocks - edge] = middle[...]
    source[num_blocks] = jnp.zeros(source.shape[1:], source.dtype)
    pair_loop(FORWARD_OWN, tab, source, matrix, rows)


def load_rims(first, rims, source):
    edge = source.shape[0] // 2
    vectors = rims[0].shape[0] // edge - (1 if first else 0)
    size = source.shape[2]
    for side, rim in enumerate(rims):
        for b in range(edge):
            source[side * edge + b, :vectors] = rim[b * vectors : (b + 1) * vectors]
        if first:
            weights = rim[edge * vectors :].astype(jnp.float32)
            top = lax.broadcasted_iota(jnp.int32, (16, size), 0) == 0
            for b in range(edge):
                pad = jnp.where(top, jnp.broadcast_to(weights[b : b + 1], (16, size)), 0.0)
                source[side * edge + b, vectors:] = pad.astype(jnp.bfloat16)
    source[2 * edge] = jnp.zeros(source.shape[1:], source.dtype)


def heads_kernel(first, tab, matrix, rows_in, right, lower, rows, source):
    del rows_in
    load_rims(first, (right, lower), source)
    pair_loop(FORWARD_HEADS, tab, source, matrix, rows)


def send_back(total, backs):
    vectors = total.shape[1]
    edge = total.shape[0] // 2
    for side in range(2):
        for b in range(edge):
            backs[side][b * vectors : (b + 1) * vectors] = total[side * edge + b].astype(jnp.bfloat16)


def middle_kernel(first, tab, matrix, rows_in, left, upper, *rest):
    del rows_in
    if first:
        rows, image, inverse = rest[:3]
    else:
        inverse, rows, image = rest[:3]
    lower_back, right_back, source, total = rest[3:]
    num_blocks = rows.shape[0]
    vectors = image.shape[1]
    load_rims(first, (left, upper), source)
    clear(total)
    pair_loop(FORWARD_TAILS, tab, source, matrix, rows)

    def divide(b, carry):
        if first:
            factor = 1.0 / rows[b, vectors : vectors + 8]
            inverse[b] = factor
        else:
            factor = inverse[b]
        image[b] = (rows[b, :vectors] * factor[:1]).astype(jnp.bfloat16)
        return carry

    lax.fori_loop(0, num_blocks, divide, 0, unroll=4)
    image[num_blocks] = jnp.zeros(image.shape[1:], image.dtype)
    pair_loop(ADJOINT_HEADS, tab, image, matrix, total)
    send_back(total, (right_back, lower_back))


def tails_kernel(tab, matrix, image, upper_back, left_back, total):
    clear(total)
    pair_loop(ADJOINT_TAILS, tab, image, matrix, total)
    send_back(total, (left_back, upper_back))


def adjoint_kernel(tab, matrix, image, weights, total, norm, *rest):
    clear(total)
    pair_loop(ADJOINT_OWN, tab, image, matrix, total)
    num_blocks = total.shape[0]
    edge = num_blocks // 4

    def inside(b, sums):
        value = total[b]
        weighted = value * weights[pl.ds(b, 1)]
        if rest:
            rest[0][b - edge] = weighted.astype(jnp.bfloat16)
        return sums + weighted * value

    zero = jnp.zeros(norm.shape, jnp.float32)
    norm[...] = lax.fori_loop(edge, num_blocks - edge, inside, zero)


def add_edge(total, weights, from_block, one, two, sums, store):
    vectors = total.shape[1]

    def add(b, carry):
        rows = pl.ds(pl.multiple_of(b * vectors, vectors), vectors)
        value = total[from_block + b] + (one[rows].astype(jnp.float32) + two[rows].astype(jnp.float32))
        weighted = value * weights[pl.ds(from_block + b, 1)]
        store(b, rows, value, weighted)
        return carry + weighted * value

    return lax.fori_loop(0, total.shape[0] // 4, add, sums, unroll=2)


def join_kernel(tail, total, weights, one, two, norm_in, out, norm):
    def store(b, rows, value, weighted):
        out[rows] = weighted.astype(jnp.bfloat16)

    from_block = total.shape[0] // 4 * 3 if tail else 0
    norm[...] = add_edge(total, weights, from_block, one, two, norm_in[...], store)


def lane_row(norm):
    ones = jnp.ones((8, norm.shape[1]), jnp.float32)
    return lax.dot_general(
        ones, norm, (((1,), (1,)), ((), ())), precision=lax.Precision.HIGHEST, preferred_element_type=jnp.float32
    )


def keep_edge(total, weights, from_block, one, two, sums):
    def store(b, rows, value, weighted):
        total[from_block + b] = value

    return add_edge(total, weights, from_block, one, two, sums, store)


def low_kernel(total_in, weights, one, two, norm_in, norm_first, total, norm, row):
    del total_in
    norm[...] = keep_edge(total, weights, 0, one, two, norm_in[...])
    row[...] = lane_row(norm_first[...])


def sum_kernel(total_in, weights, one, two, norm_in, row, total, message):
    del total_in
    sums = keep_edge(total, weights, total.shape[0] // 4 * 3, one, two, norm_in[...])
    both = jnp.concatenate([row[...], lane_row(sums)], axis=1)[:1]
    message[...] = jnp.broadcast_to(both, message.shape)


def final_kernel(total_cells, sums, total, out, held, sems):
    num_blocks, vectors, size = total.shape
    both = jnp.sum(sums[...], axis=0, keepdims=True) * (1.0 / total_cells)
    diagonal = lax.broadcasted_iota(jnp.int32, (vectors, size), 0)
    lane = lax.broadcasted_iota(jnp.int32, (vectors, size), 1)
    both = jnp.broadcast_to(both, (vectors, size))
    first = jnp.sum(jnp.where(lane == diagonal, both, 0.0), axis=1, keepdims=True)
    second = jnp.sum(jnp.where(lane == diagonal + vectors, both, 0.0), axis=1, keepdims=True)
    factor = lax.rsqrt(first + 1e-06)
    scale = jnp.broadcast_to(factor * lax.rsqrt(factor * factor * second + 1e-06), (vectors, size))

    def body(b, carry):
        cells = pl.ds(pl.multiple_of(b * size, size), size)
        held[:, cells] = (total[b] * scale).astype(jnp.bfloat16)
        return carry

    quarter = num_blocks // 4
    copies = []
    for part in range(4):
        lax.fori_loop(part * quarter, (part + 1) * quarter, body, 0, unroll=4)
        cells = pl.ds(part * quarter * size, quarter * size)
        copies.append(pltpu.make_async_copy(held.at[:, cells], out.at[:, cells], sems.at[part]))
        copies[-1].start()
    for copy in copies:
        copy.wait()


def shift(x, axis, step):
    count = lax.axis_size(axis)
    return lax.ppermute(x, axis, [(i, (i + step) % count) for i in range(count)])


def heads_out(head):
    return shift(head, "tile", -1), shift(head, "layer", -1)


def tails_out(tail):
    return shift(tail, "tile", 1), shift(tail, "layer", 1)


def call(kernel, name, outs, in_specs, scratch, flops, nbytes, aliases={}, out_spec=VMEM_SPEC):
    return pl.pallas_call(
        kernel,
        name=name,
        out_shape=outs,
        in_specs=in_specs,
        out_specs=[out_spec] * len(outs),
        scratch_shapes=scratch,
        input_output_aliases=aliases,
        compiler_params=pltpu.CompilerParams(vmem_limit_bytes=16 * 1024 * 1024),
        cost_estimate=pl.CostEstimate(flops=flops, bytes_accessed=nbytes, transcendentals=0),
    )


def local(blocks, slot_rows, slot_cols, rotation, live_block_count, density, start):
    bf16, f32 = jnp.bfloat16, jnp.float32
    blocks, start = blocks[0, 0], start[0, 0]
    slots, size = blocks.shape[0], blocks.shape[2]
    vectors, cells = start.shape
    num_blocks = cells // size
    edge = num_blocks // 4
    devices = lax.axis_size("layer") * lax.axis_size("tile")
    total_cells = cells * devices
    work = slots * size * size * vectors
    tall = vectors + 16
    rim_type = VM((edge * vectors, size), bf16)
    first_rim_type = VM((edge * (vectors + 1), size), bf16)
    block_f32 = VM((num_blocks, vectors, size), f32)
    tall_f32 = VM((num_blocks, tall, size), f32)
    image_type = VM((num_blocks + 1, vectors, size), bf16)
    middle_type = VM((num_blocks - 2 * edge, vectors, size), bf16)
    norm_type = VM((vectors, size), f32)

    def outside(x):
        return pltpu.with_memory_space_constraint(x, pltpu.HBM)

    start = outside(start)
    head, tail, weights = call(
        edge_kernel,
        "edges",
        [first_rim_type, first_rim_type, VM((num_blocks, size), f32)],
        [HBM_SPEC, HBM_SPEC],
        [
            VM((2, vectors, edge * size), bf16),
            VM((1, cells), bf16),
            pltpu.SemaphoreType.DMA((3,)),
        ],
        0,
        start.size,
    )(start, outside(density[0]))
    heads, tails = heads_out(head), tails_out(tail)

    layer = lax.axis_index("layer")
    above, beneath = layer > 0, layer < lax.axis_size("layer") - 1
    facts = jnp.stack([live_block_count[0, 0], above.astype(jnp.int32), beneath.astype(jnp.int32)])
    places = 2 * ((slots + num_blocks) // 2)
    matrix, rows, tab = call(
        first_kernel,
        "own_first",
        [VM((slots + 1, size, size), bf16), tall_f32, VM((8, places), jnp.int32)],
        [SMEM_SPEC] + [HBM_SPEC] * 5 + [VMEM_SPEC],
        [
            VM((num_blocks + 1, tall, size), bf16),
            VM((vectors, cells), bf16),
            VM((3, 1, slots), jnp.int32),
            pltpu.SMEM((8, places), jnp.int32),
            pltpu.SemaphoreType.DMA((CHUNKS + 5,)),
        ],
        2 * work,
        2 * blocks.size * 2,
    )(
        facts,
        outside(blocks),
        start,
        outside(slot_rows[0]),
        outside(slot_cols[0]),
        outside(rotation[0]),
        weights,
    )

    inverse = None
    for turn in range(2):
        first = turn == 0
        rows_type = tall_f32 if first else block_f32
        source_type = VM((2 * edge + 1, tall if first else vectors, size), bf16)
        half_f32 = VM((2 * edge, vectors, size), f32)
        suffix = "_first" if first else "_next"
        if not first:
            (rows,) = call(
                own_kernel,
                "own_next",
                [block_f32],
                [SMEM_SPEC] + [VMEM_SPEC] * 4,
                [VM((num_blocks + 1, vectors, size), bf16)],
                work,
                blocks.size,
            )(tab, matrix, head, middle, tail)
        (rows,) = call(
            functools.partial(heads_kernel, first),
            "heads" + suffix,
            [rows_type],
            [SMEM_SPEC] + [VMEM_SPEC] * 4,
            [source_type],
            work // 2,
            blocks.size // 2,
            {2: 0},
        )(tab, matrix, rows, *heads)
        extra = [] if first else [inverse]
        result = call(
            functools.partial(middle_kernel, first),
            "middle" + suffix,
            [rows_type, image_type] + ([VM((num_blocks, 8, size), f32)] if first else []) + [rim_type] * 2,
            [SMEM_SPEC] + [VMEM_SPEC] * (4 + len(extra)),
            [source_type, half_f32],
            work,
            blocks.size,
            {2: 0},
        )(tab, matrix, rows, *tails, *extra)
        image = result[1]
        if first:
            inverse = result[2]
        lower, right = result[-2:]
        lows = (shift(lower, "layer", 1), shift(right, "tile", 1))
        upper, left = call(
            tails_kernel,
            "tails" + suffix,
            [rim_type] * 2,
            [SMEM_SPEC] + [VMEM_SPEC] * 2,
            [half_f32],
            work // 2,
            blocks.size // 2,
        )(tab, matrix, image)
        highs = (shift(upper, "layer", -1), shift(left, "tile", -1))
        result = call(
            adjoint_kernel,
            "adjoint" + suffix,
            [block_f32, norm_type] + ([middle_type] if first else []),
            [SMEM_SPEC] + [VMEM_SPEC] * 3,
            [],
            work,
            blocks.size,
        )(tab, matrix, image, weights)
        total, norm = result[:2]
        if first:
            middle = result[2]
            head, norm = call(
                functools.partial(join_kernel, False),
                "join_head",
                [rim_type, norm_type],
                [VMEM_SPEC] * 5,
                [],
                0,
                edge * vectors * size * 8,
            )(total, weights, *lows, norm)
            heads = heads_out(head)
            tail, norm_first = call(
                functools.partial(join_kernel, True),
                "join_tail",
                [rim_type, norm_type],
                [VMEM_SPEC] * 5,
                [],
                0,
                edge * vectors * size * 8,
            )(total, weights, *highs, norm)
            tails = tails_out(tail)
    total, norm, row = call(
        low_kernel,
        "join_low",
        [block_f32, norm_type, VM((8, vectors), f32)],
        [VMEM_SPEC] * 6,
        [],
        0,
        edge * vectors * size * 8,
        {0: 0},
    )(total, weights, *lows, norm, norm_first)
    total, message = call(
        sum_kernel,
        "join_last",
        [block_f32, VM((devices, 2 * vectors), f32)],
        [VMEM_SPEC] * 6,
        [],
        0,
        edge * vectors * size * 8,
        {0: 0},
    )(total, weights, *highs, norm, row)
    sums = lax.all_to_all(message, ("layer", "tile"), 0, 0, tiled=True)
    out = call(
        functools.partial(final_kernel, total_cells),
        "write_out",
        [jax.ShapeDtypeStruct((vectors, cells), bf16)],
        [VMEM_SPEC] * 2,
        [VM((vectors, cells), bf16), pltpu.SemaphoreType.DMA((4,))],
        0,
        cells * vectors * 6,
        out_spec=HBM_SPEC,
    )(sums, total)[0]
    return out[None, None]


def solution(mesh):
    in_specs = (
        P("layer", "tile", None, None, None),
        P("layer", "tile", None),
        P("layer", "tile", None),
        P("layer", "tile", None),
        P("layer", "tile"),
        P("layer", "tile", None),
        P("layer", "tile", None, None),
    )
    out_specs = P("layer", "tile", None, None)
    return jax.shard_map(local, mesh=mesh, in_specs=in_specs, out_specs=out_specs, check_vma=False)
```
